32 devices in a mesh: dp: 8 (over y, x, core), seq: 4 (over z).
Axes of the slice: x: 2, y: 2, z: 4, core: 2. Of those that a mesh axis runs over, the one named last changes fastest.
Arguments:
- query: bfloat16 [8, 512, 2048], P('dp', 'seq'), may hold values from -8 to 8
- key_value: bfloat16 [2, 8, 512, 2048], P(None, 'dp', 'seq'), may hold values from -8 to 8
- grad_y: bfloat16 [8, 512, 2048], P('dp', 'seq'), may hold values from -6 to 6
- tags: int32 [8, 512], P('dp', 'seq'), may hold values 0 or 1
- segments: int32 [8, 512], P('dp'), may hold values from 0 to 3, never falling along the last dimension, each value on 1 to 256 neighbouring positions
- out_weight: bfloat16 [2, 2048, 2048], P(None, None, 'dp'), may hold values from -0.125 to 0.125
Outputs:
- grad_query: bfloat16 [8, 512, 2048], P('dp', 'seq')
- grad_key_value: bfloat16 [2, 8, 512, 2048], P(None, 'dp', 'seq')
The draws below stay inside these ranges and needn't reach their ends.
Inputs may be any that keep to these rules, and one draw needn't show every extreme that they name: `segments`: sample numbers never fall along a sequence; a sample holds at most 256 positions and some sample holds exactly 256.
All inputs are finite; a program needn't handle non-finite values. No bound on the sum of `tags` on one device may be relied on, other than what follows from the above.
Results may differ from the reference program's by a relative error of at most 0.0075.
Values may be sent and summed in bfloat16 or wider, within the bound.
No kernel may reach another device: no remote copies, remote signals or barrier semaphores. Data moves between devices by JAX's collectives and lax.ppermute only.
A program may use at most 128 MiB of HBM per device.

```python
import math
import jax
import jax.numpy as jnp
import numpy as np
from jax import lax

HEADS = 16
HEAD_DIM = 128
DW = 2048
REACH = 2
T_DEV = 128
HC = 2048
LENGTH = 512
SEQS = 8
SAMPLES = 4


def draw_query(key, part):
    base = jnp.clip(jax.random.normal(jax.random.fold_in(key, 1), (SEQS, LENGTH, HC), jnp.float32), -6.0, 6.0)
    return base.astype(jnp.bfloat16)


def draw_key_value(key, part):
    base = jnp.clip(jax.random.normal(jax.random.fold_in(key, 2), (2, SEQS, LENGTH, HC), jnp.float32), -6.0, 6.0)
    return base.astype(jnp.bfloat16)


def set_ends(entries, own_key, smallest, largest):
    longest = entries.shape.index(max(entries.shape))
    spots = []
    for shift in (0, 1):
        where = [jax.random.randint(jax.random.fold_in(own_key, axis), (), 0, length) for axis, length in enumerate(entries.shape)]
        where[longest] = (where[longest] + shift) % entries.shape[longest]
        spots.append(tuple(where))
    return entries.at[spots[0]].set(smallest).at[spots[1]].set(largest)


def levels(stream_key, dims, cuts, least, largest):
    loudness = 1.0
    for dim, parts in cuts:
        steps = jax.random.uniform(jax.random.fold_in(jax.random.fold_in(stream_key, 6), dim), (parts,), jnp.float32, least / len(cuts), largest / len(cuts))
        loudness = loudness * jnp.repeat(jnp.exp(steps), dims[dim] // parts).reshape((-1,) + (1,) * (len(dims) - 1 - dim))
    return loudness


def profile(number_of, total, reach, lean):
    loads = [(1 << 20) // math.isqrt(standing ** lean) + 1 for standing in range(2, number_of + 1)]
    surplus, holding = total - reach - (number_of - 1), [1] * (number_of - 1)
    while surplus > 0:
        movable = [i for i in range(number_of - 1) if holding[i] < reach]
        pool, remaining = sum([loads[i] for i in movable]), surplus
        for i in movable:
            addition = min(reach - holding[i], max(1, remaining * loads[i] // pool), surplus)
            holding[i] = holding[i] + addition
            surplus = surplus - addition
    return np.array([reach] + holding)


def uneven(stream_key, amount, total, bound, skew):
    if amount == 2:
        one = jax.random.randint(stream_key, (), max(1, total - bound), min(bound, total - 1) + 1)
        return jnp.stack([one, total - one])
    tallies = jnp.asarray(profile(amount, total, bound, skew), jnp.int32)
    twos = (amount - 1) // 2
    donor, receiver = tallies[1:1 + 2 * twos:2], tallies[2:2 + 2 * twos:2]
    margin = jnp.minimum(donor - 1, bound - receiver)
    shifted = jax.random.randint(jax.random.fold_in(stream_key, 1), (twos,), 0, 1 << 20) % (margin + 1)
    tallies = tallies.at[1:1 + 2 * twos:2].set(donor - shifted).at[2:2 + 2 * twos:2].set(receiver + shifted)
    return tallies[jax.random.permutation(jax.random.fold_in(stream_key, 2), amount)]


def scatter_about(rng, shape, deviation, most, cuts=(), kind=jnp.bfloat16):
    values = jax.random.normal(rng, shape, jnp.float32) * deviation
    if len(cuts) > 0:
        values = levels(rng, shape, cuts, -0.22, 0.18) * values
    return jnp.clip(values, min=-most, max=most).astype(kind)


def setup_inputs(seed: int = 0) -> dict:
    seeds = jax.random.split(jax.random.key(seed), 7)
    return {
        "query": draw_query(jax.random.fold_in(seeds[6], 71), 0),
        "key_value": draw_key_value(jax.random.fold_in(seeds[6], 71), 0),
        "grad_y": scatter_about(seeds[2], (SEQS, LENGTH, DW), 1.0, 6.0, ((0, 8), (1, 4))),
        "tags": set_ends((jax.random.randint(seeds[3], (SEQS, LENGTH), 0, 2) < 1).astype(jnp.int32), jax.random.fold_in(seeds[3], 1), 0, 1),
        "segments": jax.vmap(lambda own: jnp.searchsorted(jnp.cumsum(uneven(own, SAMPLES, LENGTH, REACH * T_DEV, 0)), jnp.arange(LENGTH), side="right"))(jax.random.split(seeds[4], SEQS)).reshape((SEQS, LENGTH)).astype(jnp.int32),
        "out_weight": scatter_about(seeds[5], (2, HC, DW), DW ** -0.5, 0.125, ((2, 8),)),
    }


NEG = -1e30


def block_grads(query, keys, values, grad_out, mask):
    scale = HEAD_DIM ** -0.5
    qf = query.astype(jnp.float32)
    kf = keys.astype(jnp.float32)
    vf = values.astype(jnp.float32)
    gf = grad_out.astype(jnp.float32)
    scores = jnp.einsum("qhe,khe->hqk", qf, kf) * scale
    scores = jnp.where(mask[None], scores, NEG)
    top = jnp.max(scores, axis=2, keepdims=True)
    lse = top + jnp.log(jnp.sum(jnp.exp(scores - top), axis=2, keepdims=True))
    probs = jnp.exp(scores - lse)
    probs_low = lax.optimization_barrier(probs.astype(jnp.bfloat16)).astype(jnp.float32)
    dprob = jnp.einsum("qhe,khe->hqk", gf, vf)
    delta = jnp.sum(probs * dprob, axis=2, keepdims=True)
    dscore = lax.optimization_barrier((probs * (dprob - delta) * scale).astype(jnp.bfloat16)).astype(jnp.float32)
    grad_q = jnp.einsum("hqk,khe->qhe", dscore, kf)
    grad_k = jnp.einsum("hqk,qhe->khe", dscore, qf)
    grad_v = jnp.einsum("hqk,qhe->khe", probs_low, gf)
    return grad_q, grad_k, grad_v


def one_sequence(query, keys, values, grad, tags, segs, out_weight):
    text_part = jnp.dot(grad, out_weight[1].T, preferred_element_type=jnp.float32)
    image_part = jnp.dot(grad, out_weight[0].T, preferred_element_type=jnp.float32)
    grad_out = jnp.where(tags[:, None] == 1, text_part, image_part).astype(jnp.bfloat16)
    count = LENGTH // T_DEV

    def split(array):
        return array.reshape((count, T_DEV, HEADS, HEAD_DIM))

    def padded(array):
        return jnp.concatenate([jnp.zeros((REACH,) + array.shape[1:], array.dtype), array], axis=0)

    query_b = split(query)
    key_pad = padded(split(keys))
    value_pad = padded(split(values))
    grad_b = split(grad_out)
    seg_b = segs.reshape((count, T_DEV))
    seg_pad = jnp.concatenate([jnp.full((REACH, T_DEV), -1, seg_b.dtype), seg_b], axis=0)
    width = (REACH + 1) * T_DEV

    def one_block(number):
        k_win = lax.dynamic_slice_in_dim(key_pad, number, REACH + 1, 0).reshape((width, HEADS, HEAD_DIM))
        v_win = lax.dynamic_slice_in_dim(value_pad, number, REACH + 1, 0).reshape((width, HEADS, HEAD_DIM))
        s_win = lax.dynamic_slice_in_dim(seg_pad, number, REACH + 1, 0).reshape((width,))
        q_blk = query_b[number]
        g_blk = grad_b[number]
        s_blk = seg_b[number]
        q_pos = number * T_DEV + jnp.arange(T_DEV).astype(jnp.int32)
        k_pos = (number - REACH) * T_DEV + jnp.arange(width).astype(jnp.int32)
        mask = (s_blk[:, None] == s_win[None, :]) & (k_pos[None, :] <= q_pos[:, None])
        return block_grads(q_blk, k_win, v_win, g_blk, mask)

    grad_q, grad_k, grad_v = lax.map(one_block, jnp.arange(count).astype(jnp.int32))

    def fold(array):
        total = jnp.zeros((count + REACH, T_DEV, HEADS, HEAD_DIM), jnp.float32)
        for offset in range(REACH + 1):
            part = array[:, offset * T_DEV:(offset + 1) * T_DEV]
            total = total + jnp.pad(part, ((offset, REACH - offset), (0, 0), (0, 0), (0, 0)))
        return total[REACH:].reshape((LENGTH, HC)).astype(jnp.bfloat16)

    return grad_q.reshape((LENGTH, HC)).astype(jnp.bfloat16), fold(grad_k), fold(grad_v)


def reference(query, key_value, grad_y, tags, segments, out_weight):
    def per_sequence(number):
        return one_sequence(query[number], key_value[0, number], key_value[1, number], grad_y[number], tags[number], segments[number], out_weight)

    grad_q, grad_k, grad_v = lax.map(per_sequence, jnp.arange(SEQS).astype(jnp.int32))
    return grad_q, jnp.stack([grad_k, grad_v])
```

```python
import functools
import jax
import jax.numpy as jnp
from jax import lax
from jax.experimental import pallas as pl
from jax.experimental.pallas import tpu as pltpu
from jax.sharding import PartitionSpec as P

HEADS = 16
HEAD_DIM = 128
REACH = 2

NEG = -1e30
LANES = 128
BF16 = jnp.bfloat16
F32 = jnp.float32
NT = (((1,), (1,)), ((), ()))
TN = (((0,), (0,)), ((), ()))


def lane_slice(start, size):
    return pl.ds(pl.multiple_of(start, LANES), size)


def swap(value, axis, bits):
    return lax.ppermute(value, axis, [(i, i ^ bits) for i in range(lax.axis_size(axis))])


def column_of(row):
    n = row.shape[1]
    same = lax.broadcasted_iota(jnp.int32, (n, n), 0) == lax.broadcasted_iota(jnp.int32, (n, n), 1)
    return jnp.sum(jnp.where(same, row.astype(F32), 0.0), axis=1, keepdims=True)


def grad_slices_kernel(grad_ref, tags_ref, *outs):
    chip = lax.axis_index("dp") // 2
    width = outs[0].shape[1] - LANES
    tag = jnp.broadcast_to(column_of(tags_ref[...]), (grad_ref.shape[1], LANES)).astype(BF16)
    for k, out in enumerate(outs):
        out[:, :width] = grad_ref[0, :, lane_slice((chip ^ k) * width, width)]
        out[:, width:] = tag


def head_slices_kernel(q_ref, kv_ref, *outs):
    place = lax.axis_index("seq")
    chunks, _, _, width = outs[0].shape
    span = q_ref.shape[2] // chunks
    for k, out in enumerate(outs):
        for c in range(chunks):
            lanes = lane_slice(c * span + (place ^ k) * width, width)
            out[c, 0] = q_ref[0, :, lanes]
            out[c, 1] = kv_ref[0, 0, :, lanes]
            out[c, 2] = kv_ref[1, 0, :, lanes]


def project_kernel(chips, *refs):
    grads, (own_w, other_w), (mine, *parts, lhs) = refs[:chips], refs[chips : chips + 2], refs[chips + 2 :]
    rows = grads[0].shape[0]
    depth = own_w.shape[2]
    core = lax.axis_index("dp") % 2

    @pl.when(pl.program_id(0) == 0)
    def _():
        for k, grad in enumerate(grads):
            text = grad[:, 2 * depth : 2 * depth + 1] == 1
            for side in range(2):
                g = grad[:, lane_slice((core ^ side) * depth, depth)]
                lhs[side, 0, k * rows : (k + 1) * rows] = jnp.where(text, jnp.zeros_like(g), g)
                lhs[side, 1, k * rows : (k + 1) * rows] = jnp.where(text, g, jnp.zeros_like(g))

    total = None
    for side, w in enumerate((own_w, other_w)):
        for kind in range(2):
            term = lax.dot_general(lhs[side, kind], w[kind], NT, preferred_element_type=F32)
            total = term if total is None else total + term
    mine[...] = total[:rows]
    for k, part in enumerate(parts):
        part[...] = total[(k + 1) * rows : (k + 2) * rows].astype(BF16)


def collect_kernel(terms, mine, *refs):
    parts, outs = refs[:terms], refs[terms:]
    place = lax.axis_index("seq")
    width = outs[0].shape[1]
    for k, out in enumerate(outs):
        lanes = lane_slice((place ^ k) * width, width)
        total = mine[:, lanes]
        for part in parts:
            total = total + part[:, lanes].astype(F32)
        out[...] = total.astype(BF16)


def attention_kernel(count, scale, *refs):
    qkv, gouts, segs = refs[:count], refs[count : 2 * count], refs[2 * count]
    outs = refs[2 * count + 1 : 3 * count + 1]
    q_all, k_all, v_all, g_all, dq_all, dk_all, dv_all = refs[3 * count + 1 :]
    rows, width = gouts[0].shape
    place = lax.axis_index("seq")
    for k in range(count):
        at = pl.ds(pl.multiple_of((place ^ k) * rows, rows), rows)
        q_all[at] = qkv[k][0, 0]
        k_all[at] = qkv[k][0, 1]
        v_all[at] = qkv[k][0, 2]
        g_all[at] = gouts[k][...]
    dk_all[...] = jnp.zeros_like(dk_all)
    dv_all[...] = jnp.zeros_like(dv_all)
    for i in range(count):
        low = max(0, i - REACH) * rows
        high = (i + 1) * rows
        own = slice(i * rows, high)
        keys = slice(low, high)
        seg_q = column_of(segs[:, own])
        seg_k = segs[:, keys].astype(F32)
        q_at = i * rows + lax.broadcasted_iota(jnp.int32, (rows, high - low), 0)
        k_at = low + lax.broadcasted_iota(jnp.int32, (rows, high - low), 1)
        mask = (seg_q == seg_k) & (k_at <= q_at)
        for h in range(width // HEAD_DIM):
            lanes = slice(h * HEAD_DIM, (h + 1) * HEAD_DIM)
            q, g = q_all[own, lanes], g_all[own, lanes]
            ks, vs = k_all[keys, lanes], v_all[keys, lanes]
            s = lax.dot_general(q, ks, NT, preferred_element_type=F32) * scale
            s = jnp.where(mask, s, NEG)
            e = jnp.exp(s - jnp.max(s, axis=1, keepdims=True))
            p = e * (1.0 / jnp.sum(e, axis=1, keepdims=True))
            dp = lax.dot_general(g, vs, NT, preferred_element_type=F32)
            delta = jnp.sum(p * dp, axis=1, keepdims=True)
            ds = (p * (dp - delta) * scale).astype(BF16)
            dq_all[own, lanes] = jnp.dot(ds, ks, preferred_element_type=F32).astype(BF16)
            dk_all[keys, lanes] += lax.dot_general(ds, q, TN, preferred_element_type=F32)
            dv_all[keys, lanes] += lax.dot_general(p.astype(BF16), g, TN, preferred_element_type=F32)
    for k in range(count):
        at = pl.ds(pl.multiple_of((place ^ k) * rows, rows), rows)
        outs[k][0] = dq_all[at]
        outs[k][1] = dk_all[at].astype(BF16)
        outs[k][2] = dv_all[at].astype(BF16)


def place_kernel(count, *refs):
    pieces, (grad_q, grad_kv) = refs[:count], refs[-2:]
    place = lax.axis_index("seq")
    width = pieces[0].shape[2]
    for k, piece in enumerate(pieces):
        lanes = lane_slice((place ^ k) * width, width)
        grad_q[0, :, lanes] = piece[0]
        grad_kv[0, 0, :, lanes] = piece[1]
        grad_kv[1, 0, :, lanes] = piece[2]


def shape(dims, dtype=BF16):
    return jax.ShapeDtypeStruct(dims, dtype)


def cost(flops, moved):
    return pl.CostEstimate(flops=int(flops), bytes_accessed=int(moved), transcendentals=0)


def shards(query, key_value, grad_y, tags, segments, out_weight):
    _, rows, hc = query.shape
    dw = grad_y.shape[2]
    depth = out_weight.shape[2]
    chips = lax.axis_size("dp") // 2
    count = lax.axis_size("seq")
    heads_here = HEADS // count
    chunks = 2 if heads_here % 2 == 0 else 1
    span = hc // chunks
    width = span // count
    length = rows * count
    whole = pl.BlockSpec(memory_space=pltpu.VMEM)

    other_weight = swap(out_weight, "dp", 1)
    slices = pl.pallas_call(
        grad_slices_kernel,
        out_shape=[shape((rows, 2 * depth + LANES))] * chips,
        name="grad_slices",
        cost_estimate=cost(0, 4 * grad_y.size),
    )(grad_y, tags)
    grads = [slices[0]] + [swap(slices[k], "dp", 2 * k) for k in range(1, chips)]
    pieces = pl.pallas_call(
        head_slices_kernel,
        out_shape=[shape((chunks, 3, rows, width))] * count,
        name="head_slices",
        cost_estimate=cost(0, 12 * query.size),
    )(query, key_value)
    qkv = [pieces[0]] + [swap(pieces[k], "seq", k) for k in range(1, count)]

    tile = min(512, span)
    gouts = []
    for c in range(chunks):
        steps = span // tile
        w_spec = pl.BlockSpec((2, tile, depth), lambda t, c=c: (0, c * steps + t, 0))
        mine, *parts = pl.pallas_call(
            functools.partial(project_kernel, chips),
            grid=(steps,),
            in_specs=[pl.BlockSpec((rows, 2 * depth + LANES), lambda t: (0, 0))] * chips + [w_spec] * 2,
            out_specs=[pl.BlockSpec((rows, tile), lambda t: (0, t))] * chips,
            out_shape=[shape((rows, span), F32)] + [shape((rows, span))] * (chips - 1),
            scratch_shapes=[pltpu.VMEM((2, 2, chips * rows, depth), BF16)],
            name=f"project_{c}",
            cost_estimate=cost(8 * chips * rows * depth * span, 8 * span * depth),
        )(*grads, out_weight, other_weight)
        parts = [swap(part, "dp", 2 * k) for k, part in enumerate(parts, 1)]
        sent = pl.pallas_call(
            functools.partial(collect_kernel, chips - 1),
            out_shape=[shape((rows, width))] * count,
            name=f"collect_{c}",
            cost_estimate=cost(0, 12 * rows * span),
        )(mine, *parts)
        gouts.append([sent[0]] + [swap(sent[k], "seq", k) for k in range(1, count)])

    results = None
    for c in range(chunks):
        piece_spec = pl.BlockSpec((1, 3, rows, width), lambda t, c=c: (c, 0, 0, 0))
        block = pl.BlockSpec((rows, width), lambda t: (0, 0))
        out = pl.BlockSpec((3, rows, width), lambda t: (0, 0, 0))
        sent = pl.pallas_call(
            functools.partial(attention_kernel, count, HEAD_DIM ** (-0.5)),
            grid=(1,),
            in_specs=[piece_spec] * count + [block] * count + [pl.BlockSpec((1, length), lambda t: (0, 0))],
            out_specs=[out] * count,
            out_shape=[shape((3, rows, width))] * count,
            scratch_shapes=[pltpu.VMEM((length, width), BF16)] * 5 + [pltpu.VMEM((length, width), F32)] * 2,
            name=f"attention_{c}",
            cost_estimate=cost(10 * length * width * 3 * rows, 14 * length * width),
        )(*qkv, *gouts[c], segments)
        back = [sent[0]] + [swap(sent[k], "seq", k) for k in range(1, count)]
        old = () if results is None else tuple(results)
        results = pl.pallas_call(
            functools.partial(place_kernel, count),
            grid=(1,),
            in_specs=[out] * count + [pl.BlockSpec(memory_space=pl.ANY)] * len(old),
            out_specs=[
                pl.BlockSpec((1, rows, span), lambda t, c=c: (0, 0, c)),
                pl.BlockSpec((2, 1, rows, span), lambda t, c=c: (0, 0, 0, c)),
            ],
            out_shape=[shape(query.shape), shape(key_value.shape)],
            input_output_aliases={count + n: n for n in range(len(old))},
            name=f"place_{c}",
            cost_estimate=cost(0, 12 * rows * span),
        )(*back, *old)
    return tuple(results)


def solution(mesh):
    return jax.shard_map(
        shards,
        mesh=mesh,
        in_specs=(
            P("dp", "seq", None),
            P(None, "dp", "seq", None),
            P("dp", "seq", None),
            P("dp", "seq"),
            P("dp", None),
            P(None, None, "dp"),
        ),
        out_specs=(P("dp", "seq", None), P(None, "dp", "seq", None)),
        check_vma=False,
    )
```

```python
import functools
import jax
import jax.numpy as jnp
from jax import lax
from jax.experimental import pallas as pl
from jax.experimental.pallas import tpu as pltpu
from jax.sharding import PartitionSpec as P

HEADS = 16
HEAD_DIM = 128
REACH = 2

NEG = -1e30
LANES = 128
BF16 = jnp.bfloat16
F32 = jnp.float32
NT = (((1,), (1,)), ((), ()))
TN = (((0,), (0,)), ((), ()))

def params(mib):
    return pltpu.CompilerParams(vmem_limit_bytes=mib << 20)


def lane_slice(start, size):
    return pl.ds(pl.multiple_of(start, LANES), size)


def swap(value, axis, bits):
    return lax.ppermute(value, axis, [(i, i ^ bits) for i in range(lax.axis_size(axis))])


def column_of(row):
    n = row.shape[1]
    same = lax.broadcasted_iota(jnp.int32, (n, n), 0) == lax.broadcasted_iota(jnp.int32, (n, n), 1)
    return jnp.sum(jnp.where(same, row.astype(F32), 0.0), axis=1, keepdims=True)


def grad_slices_kernel(grad_ref, tags_ref, *outs):
    chip = lax.axis_index("dp") // 2
    width = outs[0].shape[1] - LANES
    tag = jnp.broadcast_to(column_of(tags_ref[...]), (grad_ref.shape[1], LANES)).astype(BF16)
    for k, out in enumerate(outs):
        out[:, :width] = grad_ref[0, :, lane_slice((chip ^ k) * width, width)]
        out[:, width:] = tag


def head_slices_kernel(q_ref, kv_ref, *outs):
    place = lax.axis_index("seq")
    chunks, _, _, width = outs[0].shape
    span = q_ref.shape[2] // chunks
    for k, out in enumerate(outs):
        for c in range(chunks):
            lanes = lane_slice(c * span + (place ^ k) * width, width)
            out[c, 0] = q_ref[0, :, lanes]
            out[c, 1] = kv_ref[0, 0, :, lanes]
            out[c, 2] = kv_ref[1, 0, :, lanes]


def project_kernel(chips, *refs):
    grads, (own_w, other_w), (mine, *parts, lhs) = refs[:chips], refs[chips : chips + 2], refs[chips + 2 :]
    rows = grads[0].shape[0]
    depth = own_w.shape[2]
    core = lax.axis_index("dp") % 2

    @pl.when(pl.program_id(0) == 0)
    def _():
        for k, grad in enumerate(grads):
            text = grad[:, 2 * depth : 2 * depth + 1] == 1
            for side in range(2):
                g = grad[:, lane_slice((core ^ side) * depth, depth)]
                lhs[side, 0, k * rows : (k + 1) * rows] = jnp.where(text, jnp.zeros_like(g), g)
                lhs[side, 1, k * rows : (k + 1) * rows] = jnp.where(text, g, jnp.zeros_like(g))

    total = None
    for side, w in enumerate((own_w, other_w)):
        for kind in range(2):
            term = lax.dot_general(lhs[side, kind], w[kind], NT, preferred_element_type=F32)
            total = term if total is None else total + term
    mine[...] = total[:rows]
    for k, part in enumerate(parts):
        part[...] = total[(k + 1) * rows : (k + 2) * rows].astype(BF16)


def collect_kernel(terms, mine, *refs):
    parts, outs = refs[:terms], refs[terms:]
    place = lax.axis_index("seq")
    width = outs[0].shape[1]
    for k, out in enumerate(outs):
        lanes = lane_slice((place ^ k) * width, width)
        total = mine[:, lanes]
        for part in parts:
            total = total + part[:, lanes].astype(F32)
        out[...] = total.astype(BF16)


def attention_kernel(count, scale, *refs):
    qkv, gouts, segs = refs[:count], refs[count : 2 * count], refs[2 * count]
    outs = refs[2 * count + 1 : 3 * count + 1]
    q_all, k_all, v_all, g_all, dq_all, dk_all, dv_all = refs[3 * count + 1 :]
    rows, width = gouts[0].shape
    place = lax.axis_index("seq")
    for k in range(count):
        at = pl.ds(pl.multiple_of((place ^ k) * rows, rows), rows)
        q_all[at] = qkv[k][0, 0]
        k_all[at] = qkv[k][0, 1]
        v_all[at] = qkv[k][0, 2]
        g_all[at] = gouts[k][...]
    dk_all[...] = jnp.zeros_like(dk_all)
    dv_all[...] = jnp.zeros_like(dv_all)
    for i in range(count):
        low = max(0, i - REACH) * rows
        high = (i + 1) * rows
        own = slice(i * rows, high)
        keys = slice(low, high)
        seg_q = column_of(segs[:, own])
        seg_k = segs[:, keys].astype(F32)
        q_at = i * rows + lax.broadcasted_iota(jnp.int32, (rows, high - low), 0)
        k_at = low + lax.broadcasted_iota(jnp.int32, (rows, high - low), 1)
        mask = (seg_q == seg_k) & (k_at <= q_at)
        for h in range(width // HEAD_DIM):
            lanes = slice(h * HEAD_DIM, (h + 1) * HEAD_DIM)
            q, g = q_all[own, lanes], g_all[own, lanes]
            ks, vs = k_all[keys, lanes], v_all[keys, lanes]
            s = lax.dot_general(q, ks, NT, preferred_element_type=F32) * scale
            s = jnp.where(mask, s, NEG)
            e = jnp.exp(s - jnp.max(s, axis=1, keepdims=True))
            p = e * (1.0 / jnp.sum(e, axis=1, keepdims=True))
            dp = lax.dot_general(g, vs, NT, preferred_element_type=F32)
            delta = jnp.sum(p * dp, axis=1, keepdims=True)
            ds = (p * (dp - delta) * scale).astype(BF16)
            dq_all[own, lanes] = jnp.dot(ds, ks, preferred_element_type=F32).astype(BF16)
            dk_all[keys, lanes] += lax.dot_general(ds, q, TN, preferred_element_type=F32)
            dv_all[keys, lanes] += lax.dot_general(p.astype(BF16), g, TN, preferred_element_type=F32)
    for k in range(count):
        at = pl.ds(pl.multiple_of((place ^ k) * rows, rows), rows)
        outs[k][0] = dq_all[at]
        outs[k][1] = dk_all[at].astype(BF16)
        outs[k][2] = dv_all[at].astype(BF16)


def place_kernel(count, *refs):
    pieces, (grad_q, grad_kv) = refs[:count], refs[-2:]
    place = lax.axis_index("seq")
    width = pieces[0].shape[2]
    for k, piece in enumerate(pieces):
        lanes = lane_slice((place ^ k) * width, width)
        grad_q[0, :, lanes] = piece[0]
        grad_kv[0, 0, :, lanes] = piece[1]
        grad_kv[1, 0, :, lanes] = piece[2]


def shape(dims, dtype=BF16):
    return jax.ShapeDtypeStruct(dims, dtype)


def cost(flops, moved):
    return pl.CostEstimate(flops=int(flops), bytes_accessed=int(moved), transcendentals=0)


def shards(query, key_value, grad_y, tags, segments, out_weight):
    _, rows, hc = query.shape
    dw = grad_y.shape[2]
    depth = out_weight.shape[2]
    chips = lax.axis_size("dp") // 2
    count = lax.axis_size("seq")
    heads_here = HEADS // count
    chunks = 2 if heads_here % 2 == 0 else 1
    span = hc // chunks
    width = span // count
    length = rows * count
    whole = pl.BlockSpec(memory_space=pltpu.VMEM)

    other_weight = swap(out_weight, "dp", 1)
    slices = pl.pallas_call(
        grad_slices_kernel,
        out_shape=[shape((rows, 2 * depth + LANES))] * chips,
        compiler_params=params(12),
        name="grad_slices",
        cost_estimate=cost(0, 4 * grad_y.size),
    )(grad_y, tags)
    grads = [slices[0]] + [swap(slices[k], "dp", 2 * k) for k in range(1, chips)]
    pieces = pl.pallas_call(
        head_slices_kernel,
        out_shape=[shape((chunks, 3, rows, width))] * count,
        compiler_params=params(12),
        name="head_slices",
        cost_estimate=cost(0, 12 * query.size),
    )(query, key_value)
    qkv = [pieces[0]] + [swap(pieces[k], "seq", k) for k in range(1, count)]

    tile = min(512, span)
    gouts = []
    for c in range(chunks):
        steps = span // tile
        w_spec = pl.BlockSpec((2, tile, depth), lambda t, c=c: (0, c * steps + t, 0))
        mine, *parts = pl.pallas_call(
            functools.partial(project_kernel, chips),
            grid=(steps,),
            in_specs=[pl.BlockSpec((rows, 2 * depth + LANES), lambda t: (0, 0))] * chips + [w_spec] * 2,
            out_specs=[pl.BlockSpec((rows, tile), lambda t: (0, t))] * chips,
            out_shape=[shape((rows, span), F32)] + [shape((rows, span))] * (chips - 1),
            scratch_shapes=[pltpu.VMEM((2, 2, chips * rows, depth), BF16)],
            compiler_params=params(12),
            name=f"project_{c}",
            cost_estimate=cost(8 * chips * rows * depth * span, 8 * span * depth),
        )(*grads, out_weight, other_weight)
        parts = [swap(part, "dp", 2 * k) for k, part in enumerate(parts, 1)]
        sent = pl.pallas_call(
            functools.partial(collect_kernel, chips - 1),
            out_shape=[shape((rows, width))] * count,
            compiler_params=params(12),
            name=f"collect_{c}",
            cost_estimate=cost(0, 12 * rows * span),
        )(mine, *parts)
        gouts.append([sent[0]] + [swap(sent[k], "seq", k) for k in range(1, count)])

    results = None
    for c in range(chunks):
        piece_spec = pl.BlockSpec((1, 3, rows, width), lambda t, c=c: (c, 0, 0, 0))
        block = pl.BlockSpec((rows, width), lambda t: (0, 0))
        out = pl.BlockSpec((3, rows, width), lambda t: (0, 0, 0))
        sent = pl.pallas_call(
            functools.partial(attention_kernel, count, HEAD_DIM ** (-0.5)),
            grid=(1,),
            in_specs=[piece_spec] * count + [block] * count + [pl.BlockSpec((1, length), lambda t: (0, 0))],
            out_specs=[out] * count,
            out_shape=[shape((3, rows, width))] * count,
            scratch_shapes=[pltpu.VMEM((length, width), BF16)] * 5 + [pltpu.VMEM((length, width), F32)] * 2,
            compiler_params=params(12),
            name=f"attention_{c}",
            cost_estimate=cost(10 * length * width * 3 * rows, 14 * length * width),
        )(*qkv, *gouts[c], segments)
        back = [sent[0]] + [swap(sent[k], "seq", k) for k in range(1, count)]
        old = () if results is None else tuple(results)
        results = pl.pallas_call(
            functools.partial(place_kernel, count),
            grid=(1,),
            in_specs=[out] * count + [pl.BlockSpec(memory_space=pl.ANY)] * len(old),
            out_specs=[
                pl.BlockSpec((1, rows, span), lambda t, c=c: (0, 0, c)),
                pl.BlockSpec((2, 1, rows, span), lambda t, c=c: (0, 0, 0, c)),
            ],
            out_shape=[shape(query.shape), shape(key_value.shape)],
            input_output_aliases={count + n: n for n in range(len(old))},
            compiler_params=params(12),
            name=f"place_{c}",
            cost_estimate=cost(0, 12 * rows * span),
        )(*back, *old)
    return tuple(results)


def solution(mesh):
    return jax.shard_map(
        shards,
        mesh=mesh,
        in_specs=(
            P("dp", "seq", None),
            P(None, "dp", "seq", None),
            P("dp", "seq", None),
            P("dp", "seq"),
            P("dp", None),
            P(None, None, "dp"),
        ),
        out_specs=(P("dp", "seq", None), P(None, "dp", "seq", None)),
        check_vma=False,
    )
```

```python
import functools
import jax
import jax.numpy as jnp
from jax import lax
from jax.experimental import pallas as pl
from jax.experimental.pallas import tpu as pltpu
from jax.sharding import PartitionSpec as P

HEADS = 16
HEAD_DIM = 128
REACH = 2

NEG = -1e30
LANES = 128
BF16 = jnp.bfloat16
F32 = jnp.float32
NT = (((1,), (1,)), ((), ()))
TN = (((0,), (0,)), ((), ()))

def params(mib):
    return pltpu.CompilerParams(vmem_limit_bytes=mib << 20)


def lane_slice(start, size):
    return pl.ds(pl.multiple_of(start, LANES), size)


def swap(value, axis, bits):
    return lax.ppermute(value, axis, [(i, i ^ bits) for i in range(lax.axis_size(axis))])


def column_of(row):
    n = row.shape[1]
    same = lax.broadcasted_iota(jnp.int32, (n, n), 0) == lax.broadcasted_iota(jnp.int32, (n, n), 1)
    return jnp.sum(jnp.where(same, row.astype(F32), 0.0), axis=1, keepdims=True)


def grad_slices_kernel(grad_ref, tags_ref, *outs):
    chip = lax.axis_index("dp") // 2
    width = outs[0].shape[1] - LANES
    tag = jnp.broadcast_to(column_of(tags_ref[...]), (grad_ref.shape[1], LANES)).astype(BF16)
    for k, out in enumerate(outs):
        out[:, :width] = grad_ref[0, :, lane_slice((chip ^ k) * width, width)]
        out[:, width:] = tag


def project_kernel(chips, *refs):
    grads, (own_w, other_w), (mine, *parts, lhs) = refs[:chips], refs[chips : chips + 2], refs[chips + 2 :]
    rows = grads[0].shape[0]
    depth = own_w.shape[2]
    core = lax.axis_index("dp") % 2

    @pl.when(pl.program_id(0) == 0)
    def _():
        for k, grad in enumerate(grads):
            text = grad[:, 2 * depth : 2 * depth + 1] == 1
            for side in range(2):
                g = grad[:, lane_slice((core ^ side) * depth, depth)]
                lhs[side, 0, k * rows : (k + 1) * rows] = jnp.where(text, jnp.zeros_like(g), g)
                lhs[side, 1, k * rows : (k + 1) * rows] = jnp.where(text, g, jnp.zeros_like(g))

    total = None
    for side, w in enumerate((own_w, other_w)):
        for kind in range(2):
            term = lax.dot_general(lhs[side, kind], w[kind], NT, preferred_element_type=F32)
            total = term if total is None else total + term
    mine[...] = total[:rows]
    for k, part in enumerate(parts):
        part[...] = total[(k + 1) * rows : (k + 2) * rows].astype(BF16)


def neighbour_slices_kernel(q_ref, kv_ref, *outs):
    even = lax.axis_index("seq") % 2 == 0

    def up(out):
        out[...] = kv_ref[:, 0]

    def down(out):
        out[0] = q_ref[0]
        out[1] = q_ref[0]

    send(even, outs, down, up)


def send(even, outs, down, up):
    @pl.when(even)
    def _():
        up(outs[0])
        down(outs[1])

    @pl.when(jnp.logical_not(even))
    def _():
        down(outs[0])
        up(outs[1])


def collect_kernel(terms, mine, *refs):
    parts, out = refs[:terms], refs[terms]
    total = mine[...]
    for part in parts:
        total = total + part[...].astype(F32)
    out[...] = total.astype(BF16)


def masks(count, segs, index, rows):
    def segment(back):
        at = jnp.clip(index + back, 0, count - 1)
        return segs[:, lane_slice(at * rows, rows)].astype(F32)

    left, own, right = segment(-1), segment(0), segment(1)
    left_at, own_at = column_of(left), column_of(own)
    first, last = index == 0, index == count - 1
    key = lax.broadcasted_iota(jnp.int32, (rows, rows), 0)
    query = lax.broadcasted_iota(jnp.int32, (rows, rows), 1)
    return (
        (left_at == own) & jnp.logical_not(first),
        (left_at == right) & jnp.logical_not(first | last),
        (own_at == own) & (key <= query),
    )


def gather_sides(even, first, second, left_kv, right_q, lanes):
    def fill(from_left, from_right):
        left_kv[...] = from_left[:, :, lanes]
        right_q[...] = from_right[0, :, lanes]

    @pl.when(even)
    def _():
        fill(second, first)

    @pl.when(jnp.logical_not(even))
    def _():
        fill(first, second)


def pick_right(even, first, second, out):
    @pl.when(even)
    def _():
        out[...] = first[...]

    @pl.when(jnp.logical_not(even))
    def _():
        out[...] = second[...]


def block_terms(h, lanes, scale, q_ref, kv_ref, g_ref, left_kv, both_q, both_g, mask):
    at = slice(h * HEAD_DIM, (h + 1) * HEAD_DIM)
    wide = slice(lanes.start + at.start, lanes.start + at.stop)
    kl, vl = left_kv[0, :, at], left_kv[1, :, at]
    k, v = kv_ref[0, 0, :, wide], kv_ref[1, 0, :, wide]
    q2, g2 = both_q[:, at], both_g[:, at]
    rows = k.shape[0]
    s_left = lax.dot_general(kl, q2, NT, preferred_element_type=F32) * scale
    s_own = lax.dot_general(k, q2[:rows], NT, preferred_element_type=F32) * scale
    d_left = lax.dot_general(vl, g2, NT, preferred_element_type=F32)
    d_own = lax.dot_general(v, g2[:rows], NT, preferred_element_type=F32)
    s_pre = jnp.where(mask[0], s_left[:, :rows], NEG)
    s_far = jnp.where(mask[1], s_left[:, rows:], NEG)
    s_own = jnp.where(mask[2], s_own, NEG)
    return (kl, k, q2, g2), (s_pre, s_far, s_own), (d_left[:, :rows], d_left[:, rows:], d_own)


def fill_both(even, lanes, q_ref, g_ref, side1, side2, gsum1, gsum2, left_kv, both_q, both_g):
    rows = q_ref.shape[1]
    gather_sides(even, side1, side2, left_kv, both_q.at[rows:], lanes)
    pick_right(even, gsum1, gsum2, both_g.at[rows:])
    both_q[:rows] = q_ref[0, :, lanes]
    both_g[:rows] = g_ref[...]


def stats_kernel(count, chunk, scale, q_ref, kv_ref, g_ref, side1, side2, gsum1, gsum2, segs,
                 own_out, far_out, to1, to2, left_kv, both_q, both_g):
    index = lax.axis_index("seq")
    even = index % 2 == 0
    rows, span = g_ref.shape
    lanes = slice(chunk * span, (chunk + 1) * span)
    fill_both(even, lanes, q_ref, g_ref, side1, side2, gsum1, gsum2, left_kv, both_q, both_g)
    mask = masks(count, segs, index, rows)
    for h in range(span // HEAD_DIM):
        _, (s_pre, s_far, s_own), (d_pre, d_far, d_own) = block_terms(
            h, lanes, scale, q_ref, kv_ref, g_ref, left_kv, both_q, both_g, mask)
        top = jnp.maximum(jnp.max(s_pre, axis=0, keepdims=True), jnp.max(s_own, axis=0, keepdims=True))
        e_pre, e_own = jnp.exp(s_pre - top), jnp.exp(s_own - top)
        own_out[0, h : h + 1] = top
        own_out[1, h : h + 1] = jnp.sum(e_pre + e_own, axis=0, keepdims=True)
        own_out[2, h : h + 1] = jnp.sum(e_pre * d_pre + e_own * d_own, axis=0, keepdims=True)
        top = jnp.max(s_far, axis=0, keepdims=True)
        e_far = jnp.exp(s_far - top)
        far_out[0, h : h + 1] = top
        far_out[1, h : h + 1] = jnp.sum(e_far, axis=0, keepdims=True)
        far_out[2, h : h + 1] = jnp.sum(e_far * d_far, axis=0, keepdims=True)

    def down(out):
        out[...] = own_out[...]

    def up(out):
        out[...] = far_out[...]

    send(even, (to1, to2), down, up)


def merged(one, two):
    top = jnp.maximum(one[0], two[0])
    first, second = jnp.exp(one[0] - top), jnp.exp(two[0] - top)
    total = 1.0 / (one[1] * first + two[1] * second)
    return top, total, (one[2] * first + two[2] * second) * total


def grads_kernel(count, chunk, scale, q_ref, kv_ref, g_ref, side1, side2, gsum1, gsum2, segs,
                 own_stats, far_stats, got1, got2, dq_out, dkv_out, to1, to2,
                 left_kv, both_q, both_g, from_left, from_right):
    index = lax.axis_index("seq")
    even = index % 2 == 0
    rows, span = g_ref.shape
    lanes = slice(chunk * span, (chunk + 1) * span)
    fill_both(even, lanes, q_ref, g_ref, side1, side2, gsum1, gsum2, left_kv, both_q, both_g)
    mask = masks(count, segs, index, rows)
    pick_right(even, got1, got2, from_right)
    pick_right(even, got2, got1, from_left)
    first, last = index == 0, index == count - 1
    own_l = (jnp.where(first, NEG, from_left[0]), jnp.where(first, 0.0, from_left[1]), jnp.where(first, 0.0, from_left[2]))
    top, inv, delta = merged(own_stats, own_l)
    right = (jnp.where(last, 0.0, from_right[0]), jnp.where(last, 1.0, from_right[1]), jnp.where(last, 0.0, from_right[2]))
    far_top, far_inv, far_delta = merged(right, far_stats)

    def near(up_out, down_out):
        for h in range(span // HEAD_DIM):
            (kl, k, q2, g2), (s_pre, s_far, s_own), (d_pre, d_far, d_own) = block_terms(
                h, lanes, scale, q_ref, kv_ref, g_ref, left_kv, both_q, both_g, mask)
            row = slice(h, h + 1)
            at = slice(h * HEAD_DIM, (h + 1) * HEAD_DIM)
            p_pre = jnp.exp(s_pre - top[row]) * inv[row]
            p_own = jnp.exp(s_own - top[row]) * inv[row]
            p_far = jnp.exp(s_far - far_top[row]) * far_inv[row]
            ds_pre = (p_pre * (d_pre - delta[row]) * scale).astype(BF16)
            ds_own = (p_own * (d_own - delta[row]) * scale).astype(BF16)
            ds_far = (p_far * (d_far - far_delta[row]) * scale).astype(BF16)
            ds_left = jnp.concatenate([ds_pre, ds_far], axis=1)
            p_left = jnp.concatenate([p_pre.astype(BF16), p_far.astype(BF16)], axis=1)
            dkv_out[0, :, at] = jnp.dot(ds_own, q2[:rows], preferred_element_type=F32)
            dkv_out[1, :, at] = jnp.dot(p_own.astype(BF16), g2[:rows], preferred_element_type=F32)
            down_out[0, :, at] = jnp.dot(ds_left, q2, preferred_element_type=F32).astype(BF16)
            down_out[1, :, at] = jnp.dot(p_left, g2, preferred_element_type=F32).astype(BF16)
            dq_out[:, at] = lax.dot_general(ds_pre, kl, TN, preferred_element_type=F32) + lax.dot_general(
                ds_own, k, TN, preferred_element_type=F32)
            up_out[0, :, at] = lax.dot_general(ds_far, kl, TN, preferred_element_type=F32).astype(BF16)

    @pl.when(even)
    def _():
        near(to1, to2)

    @pl.when(jnp.logical_not(even))
    def _():
        near(to2, to1)


def finish_kernel(count, dq_ref, dkv_ref, got1, got2, *refs):
    grad_q, grad_kv = refs[-2:]
    index = lax.axis_index("seq")
    even = index % 2 == 0

    def add(from_left, from_right):
        grad_q[0] = (dq_ref[...] + jnp.where(index == 0, 0.0, from_left[0].astype(F32))).astype(BF16)
        for n in range(2):
            more = jnp.where(index == count - 1, 0.0, from_right[n].astype(F32))
            grad_kv[n, 0] = (dkv_ref[n] + more).astype(BF16)

    @pl.when(even)
    def _():
        add(got2, got1)

    @pl.when(jnp.logical_not(even))
    def _():
        add(got1, got2)


def neighbour_swaps(first, second):
    count = lax.axis_size("seq")
    one = [(i, min(i ^ 1, count - 1)) for i in range(count)]
    two = [(i, ((i + 1) ^ 1) - 1) for i in range(count)]
    two = [(i, j if 0 <= j < count else i) for i, j in two]
    return lax.ppermute(first, "seq", one), lax.ppermute(second, "seq", two)


def shape(dims, dtype=BF16):
    return jax.ShapeDtypeStruct(dims, dtype)


def cost(flops, moved):
    return pl.CostEstimate(flops=int(flops), bytes_accessed=int(moved), transcendentals=0)


def shards(query, key_value, grad_y, tags, segments, out_weight):
    _, rows, hc = query.shape
    depth = out_weight.shape[2]
    chips = lax.axis_size("dp") // 2
    count = lax.axis_size("seq")
    chunks = 2
    span = hc // chunks
    heads = span // HEAD_DIM
    scale = HEAD_DIM ** (-0.5)

    other_weight = swap(out_weight, "dp", 1)
    slices = pl.pallas_call(
        grad_slices_kernel,
        out_shape=[shape((rows, 2 * depth + LANES))] * chips,
        compiler_params=params(4),
        name="grad_slices",
        cost_estimate=cost(0, 4 * grad_y.size),
    )(grad_y, tags)
    grads = [slices[0]] + [swap(slices[k], "dp", 2 * k) for k in range(1, chips)]
    pair = shape((2, rows, hc))
    sides = neighbour_swaps(*pl.pallas_call(
        neighbour_slices_kernel,
        out_shape=[pair, pair],
        compiler_params=params(8),
        name="neighbour_slices",
        cost_estimate=cost(0, 16 * query.size),
    )(query, key_value))

    tile = min(512, span)
    gouts, gsums = [], []
    for c in range(chunks):
        steps = span // tile
        w_spec = pl.BlockSpec((2, tile, depth), lambda t, c=c: (0, c * steps + t, 0))
        mine, *parts = pl.pallas_call(
            functools.partial(project_kernel, chips),
            grid=(steps,),
            in_specs=[pl.BlockSpec((rows, 2 * depth + LANES), lambda t: (0, 0))] * chips + [w_spec] * 2,
            out_specs=[pl.BlockSpec((rows, tile), lambda t: (0, t))] * chips,
            out_shape=[shape((rows, span), F32)] + [shape((rows, span))] * (chips - 1),
            scratch_shapes=[pltpu.VMEM((2, 2, chips * rows, depth), BF16)],
            compiler_params=params(12),
            name=f"project_{c}",
            cost_estimate=cost(8 * chips * rows * depth * span, 8 * span * depth),
        )(*grads, out_weight, other_weight)
        parts = [swap(part, "dp", 2 * k) for k, part in enumerate(parts, 1)]
        gout = pl.pallas_call(
            functools.partial(collect_kernel, chips - 1),
            out_shape=shape((rows, span)),
            compiler_params=params(4),
            name=f"collect_{c}",
            cost_estimate=cost(0, 12 * rows * span),
        )(mine, *parts)
        gouts.append(gout)
        gsums.append(neighbour_swaps(gout, gout))

    small = shape((3, heads, rows), F32)
    sides_scratch = [
        pltpu.VMEM((2, rows, span), BF16), pltpu.VMEM((2 * rows, span), BF16), pltpu.VMEM((2 * rows, span), BF16)]
    stats, swapped = [], []
    for c in range(chunks):
        own, far, to1, to2 = pl.pallas_call(
            functools.partial(stats_kernel, count, c, scale),
            out_shape=[small] * 4,
            scratch_shapes=sides_scratch,
            compiler_params=params(8),
            name=f"stats_{c}",
            cost_estimate=cost(4 * 3 * rows * rows * span, 20 * rows * span),
        )(query, key_value, gouts[c], *sides, *gsums[c], segments)
        stats.append((own, far))
        swapped.append(neighbour_swaps(to1, to2))

    parts = []
    for c in range(chunks):
        half = shape((2, rows, span))
        dq, dkv, to1, to2 = pl.pallas_call(
            functools.partial(grads_kernel, count, c, scale),
            out_shape=[shape((rows, span), F32), shape((2, rows, span), F32), half, half],
            scratch_shapes=sides_scratch + [pltpu.VMEM((3, heads, rows), F32)] * 2,
            compiler_params=params(12),
            name=f"grads_{c}",
            cost_estimate=cost(10 * 3 * rows * rows * span, 40 * rows * span),
        )(query, key_value, gouts[c], *sides, *gsums[c], segments, *stats[c], *swapped[c])
        parts.append((dq, dkv, *neighbour_swaps(to1, to2)))

    results = ()
    for c in range(chunks):
        block = pl.BlockSpec((rows, span), lambda t: (0, 0))
        blocks = pl.BlockSpec((2, rows, span), lambda t: (0, 0, 0))
        results = pl.pallas_call(
            functools.partial(finish_kernel, count),
            grid=(1,),
            in_specs=[block, blocks, blocks, blocks] + [pl.BlockSpec(memory_space=pl.ANY)] * len(results),
            out_specs=[
                pl.BlockSpec((1, rows, span), lambda t, c=c: (0, 0, c)),
                pl.BlockSpec((2, 1, rows, span), lambda t, c=c: (0, 0, 0, c)),
            ],
            out_shape=[shape(query.shape), shape(key_value.shape)],
            input_output_aliases={4 + n: n for n in range(len(results))},
            compiler_params=params(12),
            name=f"finish_{c}",
            cost_estimate=cost(0, 20 * rows * span),
        )(*parts[c], *results)
    return tuple(results)


def solution(mesh):
    return jax.shard_map(
        shards,
        mesh=mesh,
        in_specs=(
            P("dp", "seq", None),
            P(None, "dp", "seq", None),
            P("dp", "seq", None),
            P("dp", "seq"),
            P("dp", None),
            P(None, None, "dp"),
        ),
        out_specs=(P("dp", "seq", None), P(None, "dp", "seq", None)),
        check_vma=False,
    )
```

```python
import functools
import jax
import jax.numpy as jnp
from jax import lax
from jax.experimental import pallas as pl
from jax.experimental.pallas import tpu as pltpu
from jax.sharding import PartitionSpec as P


HEAD_DIM = 128
CHUNKS = 2

NEG = -1e30
LANES = 128
BF16 = jnp.bfloat16
F32 = jnp.float32
NT = (((1,), (1,)), ((), ()))
TN = (((0,), (0,)), ((), ()))


def params(mib):
    return pltpu.CompilerParams(vmem_limit_bytes=mib << 20)


def lane_slice(start, size):
    return pl.ds(pl.multiple_of(start, LANES), size)


def swap(value, axis, bits):
    return lax.ppermute(value, axis, [(i, i ^ bits) for i in range(lax.axis_size(axis))])


def column_of(row):
    n = row.shape[1]
    same = lax.broadcasted_iota(jnp.int32, (n, n), 0) == lax.broadcasted_iota(jnp.int32, (n, n), 1)
    return jnp.sum(jnp.where(same, row.astype(F32), 0.0), axis=1, keepdims=True)


def grad_slices_kernel(grad_ref, tags_ref, *outs):
    chip = lax.axis_index("dp") // 2
    width = outs[0].shape[1] - LANES
    tag = jnp.broadcast_to(column_of(tags_ref[...]), (grad_ref.shape[1], LANES)).astype(BF16)
    for k, out in enumerate(outs):
        out[:, :width] = grad_ref[0, :, lane_slice((chip ^ k) * width, width)]
        out[:, width:] = tag


def project_kernel(chips, *refs):
    grads, (own_w, other_w), (mine, *parts, lhs) = refs[:chips], refs[chips : chips + 2], refs[chips + 2 :]
    rows = grads[0].shape[0]
    depth = own_w.shape[2]
    core = lax.axis_index("dp") % 2

    @pl.when(pl.program_id(0) == 0)
    def _():
        for k, grad in enumerate(grads):
            text = grad[:, 2 * depth : 2 * depth + 1] == 1
            for side in range(2):
                g = grad[:, lane_slice((core ^ side) * depth, depth)]
                lhs[side, 0, k * rows : (k + 1) * rows] = jnp.where(text, jnp.zeros_like(g), g)
                lhs[side, 1, k * rows : (k + 1) * rows] = jnp.where(text, g, jnp.zeros_like(g))

    total = None
    for side, w in enumerate((own_w, other_w)):
        for kind in range(2):
            term = lax.dot_general(lhs[side, kind], w[kind], NT, preferred_element_type=F32)
            total = term if total is None else total + term
    mine[...] = total[:rows]
    for k, part in enumerate(parts):
        part[...] = total[(k + 1) * rows : (k + 2) * rows].astype(BF16)


def neighbour_slices_kernel(q_ref, kv_ref, *outs):
    even = lax.axis_index("seq") % 2 == 0

    def up(out):
        out[...] = kv_ref[:, 0]

    def down(out):
        out[0] = q_ref[0]
        out[1] = q_ref[0]

    send(even, outs, down, up)


def send(even, outs, down, up):
    @pl.when(even)
    def _():
        up(outs[0])
        down(outs[1])

    @pl.when(jnp.logical_not(even))
    def _():
        down(outs[0])
        up(outs[1])


def collect_kernel(terms, mine, *refs):
    parts, out = refs[:terms], refs[terms]
    total = mine[...]
    for part in parts:
        total = total + part[...].astype(F32)
    out[...] = total.astype(BF16)


def masks(count, segs, index, rows):
    def segment(back):
        at = jnp.clip(index + back, 0, count - 1)
        return segs[:, lane_slice(at * rows, rows)].astype(F32)

    left, own, right = segment(-1), segment(0), segment(1)
    left_at, own_at = column_of(left), column_of(own)
    first, last = index == 0, index == count - 1
    key = lax.broadcasted_iota(jnp.int32, (rows, rows), 0)
    query = lax.broadcasted_iota(jnp.int32, (rows, rows), 1)
    return (
        (left_at == own) & jnp.logical_not(first),
        (left_at == right) & jnp.logical_not(first | last),
        (own_at == own) & (key <= query),
    )


def gather_sides(even, first, second, left_kv, right_q, lanes):
    def fill(from_left, from_right):
        left_kv[...] = from_left[:, :, lanes]
        right_q[...] = from_right[0, :, lanes]

    @pl.when(even)
    def _():
        fill(second, first)

    @pl.when(jnp.logical_not(even))
    def _():
        fill(first, second)


def block_terms(h, lanes, scale, kv_ref, left_kv, both_q, both_g, mask):
    at = slice(h * HEAD_DIM, (h + 1) * HEAD_DIM)
    wide = slice(lanes.start + at.start, lanes.start + at.stop)
    kl, vl = left_kv[0, :, at], left_kv[1, :, at]
    k, v = kv_ref[0, 0, :, wide], kv_ref[1, 0, :, wide]
    q2, g2 = both_q[:, at], both_g[:, at]
    rows = k.shape[0]
    s_left = lax.dot_general(kl, q2, NT, preferred_element_type=F32) * scale
    s_own = lax.dot_general(k, q2[:rows], NT, preferred_element_type=F32) * scale
    d_left = lax.dot_general(vl, g2, NT, preferred_element_type=F32)
    d_own = lax.dot_general(v, g2[:rows], NT, preferred_element_type=F32)
    s_pre = jnp.where(mask[0], s_left[:, :rows], NEG)
    s_far = jnp.where(mask[1], s_left[:, rows:], NEG)
    s_own = jnp.where(mask[2], s_own, NEG)
    return (kl, k, q2, g2), (s_pre, s_far, s_own), (d_left[:, :rows], d_left[:, rows:], d_own)


def fill_both(even, lanes, q_ref, g_ref, side1, side2, right_g, left_kv, both_q, both_g):
    rows = q_ref.shape[1]
    gather_sides(even, side1, side2, left_kv, both_q.at[rows:], lanes)
    both_g[rows:] = right_g[...]
    both_q[:rows] = q_ref[0, :, lanes]
    both_g[:rows] = g_ref[...]


def stats_kernel(count, chunk, scale, q_ref, kv_ref, g_ref, side1, side2, right_g, segs,
                 own_out, far_out, left_kv, both_q, both_g):
    index = lax.axis_index("seq")
    even = index % 2 == 0
    rows, span = g_ref.shape
    lanes = slice(chunk * span, (chunk + 1) * span)
    fill_both(even, lanes, q_ref, g_ref, side1, side2, right_g, left_kv, both_q, both_g)
    mask = masks(count, segs, index, rows)
    for h in range(span // HEAD_DIM):
        _, (s_pre, s_far, s_own), (d_pre, d_far, d_own) = block_terms(
            h, lanes, scale, kv_ref, left_kv, both_q, both_g, mask)
        top = jnp.maximum(jnp.max(s_pre, axis=0, keepdims=True), jnp.max(s_own, axis=0, keepdims=True))
        e_pre, e_own = jnp.exp(s_pre - top), jnp.exp(s_own - top)
        own_out[0, h : h + 1] = top
        own_out[1, h : h + 1] = jnp.sum(e_pre + e_own, axis=0, keepdims=True)
        own_out[2, h : h + 1] = jnp.sum(e_pre * d_pre + e_own * d_own, axis=0, keepdims=True)
        top = jnp.max(s_far, axis=0, keepdims=True)
        e_far = jnp.exp(s_far - top)
        far_out[0, h : h + 1] = top
        far_out[1, h : h + 1] = jnp.sum(e_far, axis=0, keepdims=True)
        far_out[2, h : h + 1] = jnp.sum(e_far * d_far, axis=0, keepdims=True)


def merged(one, two):
    top = jnp.maximum(one[0], two[0])
    first, second = jnp.exp(one[0] - top), jnp.exp(two[0] - top)
    total = 1.0 / (one[1] * first + two[1] * second)
    return top, total, (one[2] * first + two[2] * second) * total


def grads_kernel(count, chunk, scale, q_ref, kv_ref, g_ref, side1, side2, right_g, segs,
                 own_stats, far_stats, from_left, from_right, dq_out, dkv_out, to1, to2,
                 left_kv, both_q, both_g):
    index = lax.axis_index("seq")
    even = index % 2 == 0
    rows, span = g_ref.shape
    lanes = slice(chunk * span, (chunk + 1) * span)
    fill_both(even, lanes, q_ref, g_ref, side1, side2, right_g, left_kv, both_q, both_g)
    mask = masks(count, segs, index, rows)
    first, last = index == 0, index == count - 1
    own_l = (jnp.where(first, NEG, from_left[0]), jnp.where(first, 0.0, from_left[1]), jnp.where(first, 0.0, from_left[2]))
    top, inv, delta = merged(own_stats, own_l)
    right = (jnp.where(last, 0.0, from_right[0]), jnp.where(last, 1.0, from_right[1]), jnp.where(last, 0.0, from_right[2]))
    far_top, far_inv, far_delta = merged(right, far_stats)

    def near(up_out, down_out):
        for h in range(span // HEAD_DIM):
            (kl, k, q2, g2), (s_pre, s_far, s_own), (d_pre, d_far, d_own) = block_terms(
                h, lanes, scale, kv_ref, left_kv, both_q, both_g, mask)
            row = slice(h, h + 1)
            at = slice(h * HEAD_DIM, (h + 1) * HEAD_DIM)
            p_pre = jnp.exp(s_pre - top[row]) * inv[row]
            p_own = jnp.exp(s_own - top[row]) * inv[row]
            p_far = jnp.exp(s_far - far_top[row]) * far_inv[row]
            ds_pre = (p_pre * (d_pre - delta[row]) * scale).astype(BF16)
            ds_own = (p_own * (d_own - delta[row]) * scale).astype(BF16)
            ds_far = (p_far * (d_far - far_delta[row]) * scale).astype(BF16)
            ds_left = jnp.concatenate([ds_pre, ds_far], axis=1)
            p_left = jnp.concatenate([p_pre.astype(BF16), p_far.astype(BF16)], axis=1)
            dkv_out[0, :, at] = jnp.dot(ds_own, q2[:rows], preferred_element_type=F32)
            dkv_out[1, :, at] = jnp.dot(p_own.astype(BF16), g2[:rows], preferred_element_type=F32)
            down_out[0, :, at] = jnp.dot(ds_left, q2, preferred_element_type=F32).astype(BF16)
            down_out[1, :, at] = jnp.dot(p_left, g2, preferred_element_type=F32).astype(BF16)
            dq_out[:, at] = lax.dot_general(ds_pre, kl, TN, preferred_element_type=F32) + lax.dot_general(
                ds_own, k, TN, preferred_element_type=F32)
            up_out[0, :, at] = lax.dot_general(ds_far, kl, TN, preferred_element_type=F32).astype(BF16)

    @pl.when(even)
    def _():
        near(to1, to2)

    @pl.when(jnp.logical_not(even))
    def _():
        near(to2, to1)


def finish_kernel(count, dq_ref, dkv_ref, got1, got2, *refs):
    grad_q, grad_kv = refs[-2:]
    index = lax.axis_index("seq")
    even = index % 2 == 0

    def add(from_left, from_right):
        grad_q[0] = (dq_ref[...] + jnp.where(index == 0, 0.0, from_left[0].astype(F32))).astype(BF16)
        for n in range(2):
            more = jnp.where(index == count - 1, 0.0, from_right[n].astype(F32))
            grad_kv[n, 0] = (dkv_ref[n] + more).astype(BF16)

    @pl.when(even)
    def _():
        add(got2, got1)

    @pl.when(jnp.logical_not(even))
    def _():
        add(got1, got2)


def shifted(value, steps):
    count = lax.axis_size("seq")
    return lax.ppermute(value, "seq", [(i, (i + steps) % count) for i in range(count)])


def neighbour_swaps(first, second):
    count = lax.axis_size("seq")
    one = [(i, min(i ^ 1, count - 1)) for i in range(count)]
    two = [(i, ((i + 1) ^ 1) - 1) for i in range(count)]
    two = [(i, j if 0 <= j < count else i) for i, j in two]
    return lax.ppermute(first, "seq", one), lax.ppermute(second, "seq", two)


def shape(dims, dtype=BF16):
    return jax.ShapeDtypeStruct(dims, dtype)


def cost(flops, moved):
    return pl.CostEstimate(flops=int(flops), bytes_accessed=int(moved), transcendentals=0)


def step(query, key_value, grad_y, tags, segments, out_weight):
    _, rows, hc = query.shape
    depth = out_weight.shape[2]
    chips = lax.axis_size("dp") // 2
    count = lax.axis_size("seq")
    span = hc // CHUNKS
    heads = span // HEAD_DIM
    scale = HEAD_DIM ** (-0.5)

    other_weight = swap(out_weight, "dp", 1)
    slices = pl.pallas_call(
        grad_slices_kernel,
        out_shape=[shape((rows, 2 * depth + LANES))] * chips,
        compiler_params=params(4),
        name="grad_slices",
        cost_estimate=cost(0, 4 * grad_y.size),
    )(grad_y, tags)
    grads = [slices[0]] + [swap(slices[k], "dp", 2 * k) for k in range(1, chips)]
    pair = shape((2, rows, hc))
    sides = pl.pallas_call(
        neighbour_slices_kernel,
        out_shape=[pair, pair],
        compiler_params=params(8),
        name="neighbour_slices",
        cost_estimate=cost(0, 16 * query.size),
    )(query, key_value)
    sides = neighbour_swaps(*sides)

    tile = min(512, span)
    steps = span // tile
    gouts, right_gs = [], []
    for c in range(CHUNKS):
        w_spec = pl.BlockSpec((2, tile, depth), lambda t, c=c: (0, c * steps + t, 0))
        mine, *parts = pl.pallas_call(
            functools.partial(project_kernel, chips),
            grid=(steps,),
            in_specs=[pl.BlockSpec((rows, 2 * depth + LANES), lambda t: (0, 0))] * chips + [w_spec] * 2,
            out_specs=[pl.BlockSpec((rows, tile), lambda t: (0, t))] * chips,
            out_shape=[shape((rows, span), F32)] + [shape((rows, span))] * (chips - 1),
            scratch_shapes=[pltpu.VMEM((2, 2, chips * rows, depth), BF16)],
            compiler_params=params(12),
            cost_estimate=cost(8 * chips * rows * depth * span, 8 * span * depth),
        )(*grads, out_weight, other_weight)
        parts = [swap(part, "dp", 2 * k) for k, part in enumerate(parts, 1)]
        gout = pl.pallas_call(
            functools.partial(collect_kernel, chips - 1),
            out_shape=shape((rows, span)),
            compiler_params=params(4),
            cost_estimate=cost(0, 12 * rows * span),
        )(mine, *parts)
        gouts.append(gout)
        right_gs.append(shifted(gout, -1))

    small = shape((3, heads, rows), F32)
    sides_scratch = [
        pltpu.VMEM((2, rows, span), BF16), pltpu.VMEM((2 * rows, span), BF16), pltpu.VMEM((2 * rows, span), BF16)]
    half = shape((2, rows, span))
    parts = []
    for c in range(CHUNKS):
        common = (query, key_value, gouts[c], *sides, right_gs[c], segments)
        own, far = pl.pallas_call(
            functools.partial(stats_kernel, count, c, scale),
            out_shape=[small] * 2,
            scratch_shapes=sides_scratch,
            compiler_params=params(8),
            cost_estimate=cost(4 * 3 * rows * rows * span, 20 * rows * span),
        )(*common)
        from_right, from_left = shifted(own, -1), shifted(far, 1)
        dq, dkv, to1, to2 = pl.pallas_call(
            functools.partial(grads_kernel, count, c, scale),
            out_shape=[shape((rows, span), F32), shape((2, rows, span), F32), half, half],
            scratch_shapes=sides_scratch,
            compiler_params=params(12),
            cost_estimate=cost(10 * 3 * rows * rows * span, 40 * rows * span),
        )(*common, own, far, from_left, from_right)
        parts.append((dq, dkv, *neighbour_swaps(to1, to2)))

    results = ()
    for c in range(CHUNKS):
        block = pl.BlockSpec((rows, span), lambda t: (0, 0))
        blocks = pl.BlockSpec((2, rows, span), lambda t: (0, 0, 0))
        results = pl.pallas_call(
            functools.partial(finish_kernel, count),
            grid=(1,),
            in_specs=[block, blocks, blocks, blocks] + [pl.BlockSpec(memory_space=pl.ANY)] * len(results),
            out_specs=[
                pl.BlockSpec((1, rows, span), lambda t, c=c: (0, 0, c)),
                pl.BlockSpec((2, 1, rows, span), lambda t, c=c: (0, 0, 0, c)),
            ],
            out_shape=[shape(query.shape), shape(key_value.shape)],
            input_output_aliases={4 + n: n for n in range(len(results))},
            compiler_params=params(12),
            cost_estimate=cost(0, 20 * rows * span),
        )(*parts[c], *results)
    return tuple(results)


def solution(mesh):
    return jax.shard_map(
        step,
        mesh=mesh,
        in_specs=(
            P("dp", "seq", None),
            P(None, "dp", "seq", None),
            P("dp", "seq", None),
            P("dp", "seq"),
            P("dp", None),
            P(None, None, "dp"),
        ),
        out_specs=(P("dp", "seq", None), P(None, "dp", "seq", None)),
        check_vma=False,
    )
```

```python
import functools
import jax
import jax.numpy as jnp
from jax import lax
from jax.experimental import pallas as pl
from jax.experimental.pallas import tpu as pltpu
from jax.sharding import PartitionSpec as P


HEAD_DIM = 128
CHUNKS = 2

NEG = -1e30
LANES = 128
BF16 = jnp.bfloat16
F32 = jnp.float32
NT = (((1,), (1,)), ((), ()))
TN = (((0,), (0,)), ((), ()))


def params(mib):
    return pltpu.CompilerParams(vmem_limit_bytes=mib << 20)


def lane_slice(start, size):
    return pl.ds(pl.multiple_of(start, LANES), size)


def swap(value, axis, bits):
    return lax.ppermute(value, axis, [(i, i ^ bits) for i in range(lax.axis_size(axis))])


def column_of(row):
    n = row.shape[1]
    same = lax.broadcasted_iota(jnp.int32, (n, n), 0) == lax.broadcasted_iota(jnp.int32, (n, n), 1)
    return jnp.sum(jnp.where(same, row.astype(F32), 0.0), axis=1, keepdims=True)


def grad_slices_kernel(grad_ref, tags_ref, *refs):
    outs, (tags, tag_sem, sem) = refs[:-3], refs[-3:]
    chip = lax.axis_index("dp") // 2
    width = outs[0].shape[1] - LANES
    tag_copy = pltpu.make_async_copy(tags_ref, tags, tag_sem)
    copies = [
        pltpu.make_async_copy(grad_ref.at[0, :, lane_slice((chip ^ k) * width, width)], out.at[:, :width], sem.at[k])
        for k, out in enumerate(outs)
    ]
    for copy in [tag_copy] + copies:
        copy.start()
    tag_copy.wait()
    tag = jnp.broadcast_to(column_of(tags[...]), (grad_ref.shape[1], LANES)).astype(BF16)
    for out in outs:
        out[:, width:] = tag
    for copy in copies:
        copy.wait()


def project_kernel(chips, *refs):
    grads, (own_w, other_w), (mine, *parts, lhs) = refs[:chips], refs[chips : chips + 2], refs[chips + 2 :]
    rows = grads[0].shape[0]
    depth = own_w.shape[2]
    core = lax.axis_index("dp") % 2

    @pl.when(pl.program_id(0) == 0)
    def _():
        for k, grad in enumerate(grads):
            text = grad[:, 2 * depth : 2 * depth + 1] == 1
            for side in range(2):
                g = grad[:, lane_slice((core ^ side) * depth, depth)]
                lhs[side, 0, k * rows : (k + 1) * rows] = jnp.where(text, jnp.zeros_like(g), g)
                lhs[side, 1, k * rows : (k + 1) * rows] = jnp.where(text, g, jnp.zeros_like(g))

    total = None
    for side, w in enumerate((own_w, other_w)):
        for kind in range(2):
            term = lax.dot_general(lhs[side, kind], w[kind], NT, preferred_element_type=F32)
            total = term if total is None else total + term
    mine[...] = total[:rows]
    for k, part in enumerate(parts):
        part[...] = total[(k + 1) * rows : (k + 2) * rows].astype(BF16)


def neighbour_slices_kernel(q_ref, kv_ref, out1, out2, sem):
    def fill(up, down):
        copies = [
            pltpu.make_async_copy(kv_ref.at[:, 0], up, sem.at[0]),
            pltpu.make_async_copy(q_ref.at[0], down.at[0], sem.at[1]),
            pltpu.make_async_copy(q_ref.at[0], down.at[1], sem.at[2]),
        ]
        for copy in copies:
            copy.start()
        for copy in copies:
            copy.wait()

    even = lax.axis_index("seq") % 2 == 0

    @pl.when(even)
    def _():
        fill(out1, out2)

    @pl.when(jnp.logical_not(even))
    def _():
        fill(out2, out1)


def collect_kernel(terms, mine, *refs):
    parts, out = refs[:terms], refs[terms]
    total = mine[...]
    for part in parts:
        total = total + part[...].astype(F32)
    out[...] = total.astype(BF16)


def masks(count, segs, index, rows):
    def segment(back):
        at = jnp.clip(index + back, 0, count - 1)
        return segs[:, lane_slice(at * rows, rows)].astype(F32)

    left, own, right = segment(-1), segment(0), segment(1)
    left_at, own_at = column_of(left), column_of(own)
    first, last = index == 0, index == count - 1
    key = lax.broadcasted_iota(jnp.int32, (rows, rows), 0)
    query = lax.broadcasted_iota(jnp.int32, (rows, rows), 1)
    return (
        (left_at == own) & jnp.logical_not(first),
        (left_at == right) & jnp.logical_not(first | last),
        (own_at == own) & (key <= query),
    )


def gather_sides(even, first, second, left_kv, right_q, lanes):
    def fill(from_left, from_right):
        left_kv[...] = from_left[:, :, lanes]
        right_q[...] = from_right[0, :, lanes]

    @pl.when(even)
    def _():
        fill(second, first)

    @pl.when(jnp.logical_not(even))
    def _():
        fill(first, second)


def block_terms(h, lanes, scale, kv_ref, left_kv, both_q, both_g, mask):
    at = slice(h * HEAD_DIM, (h + 1) * HEAD_DIM)
    wide = slice(lanes.start + at.start, lanes.start + at.stop)
    kl, vl = left_kv[0, :, at], left_kv[1, :, at]
    k, v = kv_ref[0, 0, :, wide], kv_ref[1, 0, :, wide]
    q2, g2 = both_q[:, at], both_g[:, at]
    rows = k.shape[0]
    s_left = lax.dot_general(kl, q2, NT, preferred_element_type=F32) * scale
    s_own = lax.dot_general(k, q2[:rows], NT, preferred_element_type=F32) * scale
    d_left = lax.dot_general(vl, g2, NT, preferred_element_type=F32)
    d_own = lax.dot_general(v, g2[:rows], NT, preferred_element_type=F32)
    s_pre = jnp.where(mask[0], s_left[:, :rows], NEG)
    s_far = jnp.where(mask[1], s_left[:, rows:], NEG)
    s_own = jnp.where(mask[2], s_own, NEG)
    return (kl, k, q2, g2), (s_pre, s_far, s_own), (d_left[:, :rows], d_left[:, rows:], d_own)


def fill_both(even, lanes, q_ref, g_ref, side1, side2, right_g, left_kv, both_q, both_g):
    rows = q_ref.shape[1]
    gather_sides(even, side1, side2, left_kv, both_q.at[rows:], lanes)
    both_g[rows:] = right_g[...]
    both_q[:rows] = q_ref[0, :, lanes]
    both_g[:rows] = g_ref[...]


def stats_kernel(count, chunk, scale, q_ref, kv_ref, g_ref, side1, side2, right_g, segs,
                 own_out, far_out, left_kv, both_q, both_g):
    index = lax.axis_index("seq")
    even = index % 2 == 0
    rows, span = g_ref.shape
    lanes = slice(chunk * span, (chunk + 1) * span)
    fill_both(even, lanes, q_ref, g_ref, side1, side2, right_g, left_kv, both_q, both_g)
    mask = masks(count, segs, index, rows)
    for h in range(span // HEAD_DIM):
        _, (s_pre, s_far, s_own), (d_pre, d_far, d_own) = block_terms(
            h, lanes, scale, kv_ref, left_kv, both_q, both_g, mask)
        top = jnp.maximum(jnp.max(s_pre, axis=0, keepdims=True), jnp.max(s_own, axis=0, keepdims=True))
        e_pre, e_own = jnp.exp(s_pre - top), jnp.exp(s_own - top)
        own_out[0, h : h + 1] = top
        own_out[1, h : h + 1] = jnp.sum(e_pre + e_own, axis=0, keepdims=True)
        own_out[2, h : h + 1] = jnp.sum(e_pre * d_pre + e_own * d_own, axis=0, keepdims=True)
        top = jnp.max(s_far, axis=0, keepdims=True)
        e_far = jnp.exp(s_far - top)
        far_out[0, h : h + 1] = top
        far_out[1, h : h + 1] = jnp.sum(e_far, axis=0, keepdims=True)
        far_out[2, h : h + 1] = jnp.sum(e_far * d_far, axis=0, keepdims=True)


def merged(one, two):
    top = jnp.maximum(one[0], two[0])
    first, second = jnp.exp(one[0] - top), jnp.exp(two[0] - top)
    total = 1.0 / (one[1] * first + two[1] * second)
    return top, total, (one[2] * first + two[2] * second) * total


def grads_kernel(count, chunk, scale, q_ref, kv_ref, g_ref, side1, side2, right_g, segs,
                 own_stats, far_stats, from_left, from_right, dq_out, dkv_out, to1, to2,
                 left_kv, both_q, both_g):
    index = lax.axis_index("seq")
    even = index % 2 == 0
    rows, span = g_ref.shape
    lanes = slice(chunk * span, (chunk + 1) * span)
    fill_both(even, lanes, q_ref, g_ref, side1, side2, right_g, left_kv, both_q, both_g)
    mask = masks(count, segs, index, rows)
    first, last = index == 0, index == count - 1
    own_l = (jnp.where(first, NEG, from_left[0]), jnp.where(first, 0.0, from_left[1]), jnp.where(first, 0.0, from_left[2]))
    top, inv, delta = merged(own_stats, own_l)
    right = (jnp.where(last, 0.0, from_right[0]), jnp.where(last, 1.0, from_right[1]), jnp.where(last, 0.0, from_right[2]))
    far_top, far_inv, far_delta = merged(right, far_stats)

    def near(up_out, down_out):
        for h in range(span // HEAD_DIM):
            (kl, k, q2, g2), (s_pre, s_far, s_own), (d_pre, d_far, d_own) = block_terms(
                h, lanes, scale, kv_ref, left_kv, both_q, both_g, mask)
            row = slice(h, h + 1)
            at = slice(h * HEAD_DIM, (h + 1) * HEAD_DIM)
            p_pre = jnp.exp(s_pre - top[row]) * inv[row]
            p_own = jnp.exp(s_own - top[row]) * inv[row]
            p_far = jnp.exp(s_far - far_top[row]) * far_inv[row]
            ds_pre = (p_pre * (d_pre - delta[row]) * scale).astype(BF16)
            ds_own = (p_own * (d_own - delta[row]) * scale).astype(BF16)
            ds_far = (p_far * (d_far - far_delta[row]) * scale).astype(BF16)
            ds_left = jnp.concatenate([ds_pre, ds_far], axis=1)
            p_left = jnp.concatenate([p_pre.astype(BF16), p_far.astype(BF16)], axis=1)
            dkv_out[0, :, at] = jnp.dot(ds_own, q2[:rows], preferred_element_type=F32)
            dkv_out[1, :, at] = jnp.dot(p_own.astype(BF16), g2[:rows], preferred_element_type=F32)
            down_out[0, :, at] = jnp.dot(ds_left, q2, preferred_element_type=F32).astype(BF16)
            down_out[1, :, at] = jnp.dot(p_left, g2, preferred_element_type=F32).astype(BF16)
            dq_out[:, at] = lax.dot_general(ds_pre, kl, TN, preferred_element_type=F32) + lax.dot_general(
                ds_own, k, TN, preferred_element_type=F32)
            up_out[0, :, at] = lax.dot_general(ds_far, kl, TN, preferred_element_type=F32).astype(BF16)

    @pl.when(even)
    def _():
        near(to1, to2)

    @pl.when(jnp.logical_not(even))
    def _():
        near(to2, to1)


def finish_kernel(count, dq_ref, dkv_ref, got1, got2, *refs):
    grad_q, grad_kv = refs[-2:]
    index = lax.axis_index("seq")
    even = index % 2 == 0

    def add(from_left, from_right):
        grad_q[0] = (dq_ref[...] + jnp.where(index == 0, 0.0, from_left[0].astype(F32))).astype(BF16)
        for n in range(2):
            more = jnp.where(index == count - 1, 0.0, from_right[n].astype(F32))
            grad_kv[n, 0] = (dkv_ref[n] + more).astype(BF16)

    @pl.when(even)
    def _():
        add(got2, got1)

    @pl.when(jnp.logical_not(even))
    def _():
        add(got1, got2)


def shifted(value, steps):
    count = lax.axis_size("seq")
    return lax.ppermute(value, "seq", [(i, (i + steps) % count) for i in range(count)])


def neighbour_swaps(first, second):
    count = lax.axis_size("seq")
    one = [(i, min(i ^ 1, count - 1)) for i in range(count)]
    two = [(i, ((i + 1) ^ 1) - 1) for i in range(count)]
    two = [(i, j if 0 <= j < count else i) for i, j in two]
    return lax.ppermute(first, "seq", one), lax.ppermute(second, "seq", two)


def in_hbm(value):
    return pltpu.with_memory_space_constraint(value, pltpu.HBM)


def shape(dims, dtype=BF16):
    return jax.ShapeDtypeStruct(dims, dtype)


def cost(flops, moved):
    return pl.CostEstimate(flops=int(flops), bytes_accessed=int(moved), transcendentals=0)


def step(query, key_value, grad_y, tags, segments, out_weight):
    _, rows, hc = query.shape
    depth = out_weight.shape[2]
    chips = lax.axis_size("dp") // 2
    count = lax.axis_size("seq")
    span = hc // CHUNKS
    heads = span // HEAD_DIM
    scale = HEAD_DIM ** (-0.5)

    other_weight = swap(out_weight, "dp", 1)
    slices = pl.pallas_call(
        grad_slices_kernel,
        in_specs=[pl.BlockSpec(memory_space=pltpu.HBM)] * 2,
        out_shape=[shape((rows, 2 * depth + LANES))] * chips,
        scratch_shapes=[
            pltpu.VMEM(tags.shape, tags.dtype), pltpu.SemaphoreType.DMA, pltpu.SemaphoreType.DMA((chips,))],
        compiler_params=params(4),
        name="grad_slices",
        cost_estimate=cost(0, 4 * grad_y.size),
    )(in_hbm(grad_y), in_hbm(tags))
    grads = [slices[0]] + [swap(slices[k], "dp", 2 * k) for k in range(1, chips)]
    pair = shape((2, rows, hc))
    sides = pl.pallas_call(
        neighbour_slices_kernel,
        in_specs=[pl.BlockSpec(memory_space=pltpu.HBM)] * 2,
        out_shape=[pair, pair],
        scratch_shapes=[pltpu.SemaphoreType.DMA((3,))],
        compiler_params=params(8),
        name="neighbour_slices",
        cost_estimate=cost(0, 16 * query.size),
    )(in_hbm(query), in_hbm(key_value))
    sides = neighbour_swaps(*sides)

    tile = min(512, span)
    steps = span // tile
    gouts, right_gs = [], []
    for c in range(CHUNKS):
        w_spec = pl.BlockSpec((2, tile, depth), lambda t, c=c: (0, c * steps + t, 0))
        mine, *parts = pl.pallas_call(
            functools.partial(project_kernel, chips),
            grid=(steps,),
            in_specs=[pl.BlockSpec((rows, 2 * depth + LANES), lambda t: (0, 0))] * chips + [w_spec] * 2,
            out_specs=[pl.BlockSpec((rows, tile), lambda t: (0, t))] * chips,
            out_shape=[shape((rows, span), F32)] + [shape((rows, span))] * (chips - 1),
            scratch_shapes=[pltpu.VMEM((2, 2, chips * rows, depth), BF16)],
            compiler_params=params(12),
            cost_estimate=cost(8 * chips * rows * depth * span, 8 * span * depth),
        )(*grads, out_weight, other_weight)
        parts = [swap(part, "dp", 2 * k) for k, part in enumerate(parts, 1)]
        gout = pl.pallas_call(
            functools.partial(collect_kernel, chips - 1),
            out_shape=shape((rows, span)),
            compiler_params=params(4),
            cost_estimate=cost(0, 12 * rows * span),
        )(mine, *parts)
        gouts.append(gout)
        right_gs.append(shifted(gout, -1))

    small = shape((3, heads, rows), F32)
    sides_scratch = [
        pltpu.VMEM((2, rows, span), BF16), pltpu.VMEM((2 * rows, span), BF16), pltpu.VMEM((2 * rows, span), BF16)]
    half = shape((2, rows, span))
    parts = []
    for c in range(CHUNKS):
        common = (query, key_value, gouts[c], *sides, right_gs[c], segments)
        own, far = pl.pallas_call(
            functools.partial(stats_kernel, count, c, scale),
            out_shape=[small] * 2,
            scratch_shapes=sides_scratch,
            compiler_params=params(8),
            cost_estimate=cost(4 * 3 * rows * rows * span, 20 * rows * span),
        )(*common)
        from_right, from_left = shifted(own, -1), shifted(far, 1)
        dq, dkv, to1, to2 = pl.pallas_call(
            functools.partial(grads_kernel, count, c, scale),
            out_shape=[shape((rows, span), F32), shape((2, rows, span), F32), half, half],
            scratch_shapes=sides_scratch,
            compiler_params=params(12),
            cost_estimate=cost(10 * 3 * rows * rows * span, 40 * rows * span),
        )(*common, own, far, from_left, from_right)
        parts.append((dq, dkv, *neighbour_swaps(to1, to2)))

    results = ()
    for c in range(CHUNKS):
        block = pl.BlockSpec((rows, span), lambda t: (0, 0))
        blocks = pl.BlockSpec((2, rows, span), lambda t: (0, 0, 0))
        results = pl.pallas_call(
            functools.partial(finish_kernel, count),
            grid=(1,),
            in_specs=[block, blocks, blocks, blocks] + [pl.BlockSpec(memory_space=pl.ANY)] * len(results),
            out_specs=[
                pl.BlockSpec((1, rows, span), lambda t, c=c: (0, 0, c)),
                pl.BlockSpec((2, 1, rows, span), lambda t, c=c: (0, 0, 0, c)),
            ],
            out_shape=[shape(query.shape), shape(key_value.shape)],
            input_output_aliases={4 + n: n for n in range(len(results))},
            compiler_params=params(12),
            cost_estimate=cost(0, 20 * rows * span),
        )(*parts[c], *results)
    return tuple(results)


def solution(mesh):
    return jax.shard_map(
        step,
        mesh=mesh,
        in_specs=(
            P("dp", "seq", None),
            P(None, "dp", "seq", None),
            P("dp", "seq", None),
            P("dp", "seq"),
            P("dp", None),
            P(None, None, "dp"),
        ),
        out_specs=(P("dp", "seq", None), P(None, "dp", "seq", None)),
        check_vma=False,
    )
```

```python
import functools
import jax
import jax.numpy as jnp
from jax import lax
from jax.experimental import pallas as pl
from jax.experimental.pallas import tpu as pltpu
from jax.sharding import PartitionSpec as P


HEADS = 16
HEAD_DIM = 128
CHUNKS = 2

NEG = -1e30
LANES = 128
BF16 = jnp.bfloat16
F32 = jnp.float32
NT = (((1,), (1,)), ((), ()))
TN = (((0,), (0,)), ((), ()))


def params(mib):
    return pltpu.CompilerParams(vmem_limit_bytes=mib << 20)


def lane_slice(start, size):
    return pl.ds(pl.multiple_of(start, LANES), size)


def swap(value, axis, bits):
    return lax.ppermute(value, axis, [(i, i ^ bits) for i in range(lax.axis_size(axis))])


def column_of(row):
    n = row.shape[1]
    same = lax.broadcasted_iota(jnp.int32, (n, n), 0) == lax.broadcasted_iota(jnp.int32, (n, n), 1)
    return jnp.sum(jnp.where(same, row.astype(F32), 0.0), axis=1, keepdims=True)


def slices_kernel(grad_ref, tags_ref, q_ref, kv_ref, *refs):
    outs, (first, second, v_out), (tags, tag_sem, sem) = refs[:-6], refs[-6:-3], refs[-3:]
    chip = lax.axis_index("dp") // 2
    even = lax.axis_index("seq") % 2 == 0
    width = outs[0].shape[1] - LANES
    tag_copy = pltpu.make_async_copy(tags_ref, tags, tag_sem)
    copies = [
        pltpu.make_async_copy(grad_ref.at[0, :, lane_slice((chip ^ k) * width, width)], out.at[:, :width], sem.at[k])
        for k, out in enumerate(outs)
    ]
    count = len(outs)
    v_copy = pltpu.make_async_copy(kv_ref.at[1, 0], v_out, sem.at[count])
    for copy in [tag_copy] + copies:
        copy.start()

    def sides(up, down):
        both = [
            pltpu.make_async_copy(kv_ref.at[0, 0], up, sem.at[count + 1]),
            pltpu.make_async_copy(q_ref.at[0], down, sem.at[count + 2]),
        ]
        for copy in both:
            copy.start()
        for copy in both:
            copy.wait()

    @pl.when(even)
    def _():
        sides(first, second)

    @pl.when(jnp.logical_not(even))
    def _():
        sides(second, first)

    v_copy.start()
    tag_copy.wait()
    tag = jnp.broadcast_to(column_of(tags[...]), (grad_ref.shape[1], LANES)).astype(BF16)
    for out in outs:
        out[:, width:] = tag
    for copy in copies + [v_copy]:
        copy.wait()


def project_kernel(chips, *refs):
    grads, (own_w, other_w), (mine, *parts, lhs) = refs[:chips], refs[chips : chips + 2], refs[chips + 2 :]
    rows = grads[0].shape[0]
    depth = own_w.shape[2]
    core = lax.axis_index("dp") % 2

    @pl.when(pl.program_id(0) == 0)
    def _():
        for k, grad in enumerate(grads):
            text = grad[:, 2 * depth : 2 * depth + 1] == 1
            for side in range(2):
                g = grad[:, lane_slice((core ^ side) * depth, depth)]
                lhs[side, 0, k * rows : (k + 1) * rows] = jnp.where(text, jnp.zeros_like(g), g)
                lhs[side, 1, k * rows : (k + 1) * rows] = jnp.where(text, g, jnp.zeros_like(g))

    total = None
    for side, w in enumerate((own_w, other_w)):
        for kind in range(2):
            term = lax.dot_general(lhs[side, kind], w[kind], NT, preferred_element_type=F32)
            total = term if total is None else total + term
    mine[...] = total[:rows]
    for k, part in enumerate(parts):
        part[...] = total[(k + 1) * rows : (k + 2) * rows].astype(BF16)


def split(values):
    high = values.astype(BF16)
    return jnp.concatenate([high, (values - high.astype(F32)).astype(BF16)], axis=0)


def joined(pieces):
    half = pieces.shape[0] // 2
    return pieces[:half].astype(F32) + pieces[half:].astype(F32)


def masks(count, segs, index, rows):
    def segment(back):
        at = jnp.clip(index + back, 0, count - 1)
        return segs[:, lane_slice(at * rows, rows)].astype(F32)

    left, own, right = segment(-1), segment(0), segment(1)
    left_at, own_at = column_of(left), column_of(own)
    no_left, no_right = index == 0, index == count - 1
    key = lax.broadcasted_iota(jnp.int32, (rows, rows), 0)
    query = lax.broadcasted_iota(jnp.int32, (rows, rows), 1)
    return (
        (left_at == own) & jnp.logical_not(no_left),
        (left_at == right) & jnp.logical_not(no_left | no_right),
        (own_at == own) & (key <= query),
        (own_at == right) & jnp.logical_not(no_right),
    )


def score(keys, queries, scale, mask):
    s = lax.dot_general(keys, queries, NT, preferred_element_type=F32) * scale
    return jnp.where(mask, s, NEG)


def pair_of(even, to_even, to_odd):
    def copy(items):
        for source, target in items:
            target[...] = source[...]

    @pl.when(even)
    def _():
        copy(to_even)

    @pl.when(jnp.logical_not(even))
    def _():
        copy(to_odd)


def stats_kernel(count, scale, q_ref, kv_ref, got1, got2, segs, own_out, far_out, left_k, right_q):
    index = lax.axis_index("seq")
    rows, hc = left_k.shape
    pair_of(index % 2 == 0, [(got2, left_k), (got1, right_q)], [(got1, left_k), (got2, right_q)])
    pre, far, own, _ = masks(count, segs, index, rows)
    for h in range(hc // HEAD_DIM):
        at = slice(h * HEAD_DIM, (h + 1) * HEAD_DIM)
        kl, q = left_k[:, at], q_ref[0, :, at]
        s_pre = score(kl, q, scale, pre)
        s_own = score(kv_ref[0, 0, :, at], q, scale, own)
        s_far = score(kl, right_q[:, at], scale, far)
        top = jnp.max(jnp.maximum(s_pre, s_own), axis=0, keepdims=True)
        own_out[0, h : h + 1] = top
        own_out[1, h : h + 1] = jnp.sum(jnp.exp(s_pre - top) + jnp.exp(s_own - top), axis=0, keepdims=True)
        top = jnp.max(s_far, axis=0, keepdims=True)
        far_out[0, h : h + 1] = top
        far_out[1, h : h + 1] = jnp.sum(jnp.exp(s_far - top), axis=0, keepdims=True)


def merged(one, two):
    top = jnp.maximum(one[0], two[0])
    return top, 1.0 / (one[1] * jnp.exp(one[0] - top) + two[1] * jnp.exp(two[0] - top))


def own_rows(index, own_stats, from_left, heads):
    no_left = index == 0
    far = (jnp.where(no_left, NEG, from_left[0, heads]), jnp.where(no_left, 0.0, from_left[1, heads]))
    return merged((own_stats[0, heads], own_stats[1, heads]), far)


def right_rows(index, count, far_stats, from_right, heads):
    no_right = index == count - 1
    own = (jnp.where(no_right, 0.0, from_right[0, heads]), jnp.where(no_right, 1.0, from_right[1, heads]))
    return merged(own, (far_stats[0, heads], far_stats[1, heads]))


def delta_kernel(count, chunk, terms, scale, mine, *refs):
    parts = refs[:terms]
    q_ref, kv_ref, left_k, got1, got2, segs, own_stats, from_left, g_out, d_out, left_v = refs[terms:]
    rows, span = mine.shape
    index = lax.axis_index("seq")
    first = chunk * span
    lanes = slice(first, first + span)
    pair_of(index % 2 == 0, [(got2.at[:, lanes], left_v)], [(got1.at[:, lanes], left_v)])
    total = mine[...]
    for part in parts:
        total = total + part[...].astype(F32)
    g_out[:rows] = total.astype(BF16)
    pre, _, own, _ = masks(count, segs, index, rows)
    heads = span // HEAD_DIM
    top, inv = own_rows(index, own_stats, from_left, slice(chunk * heads, (chunk + 1) * heads))
    for h in range(heads):
        at = slice(h * HEAD_DIM, (h + 1) * HEAD_DIM)
        wide = slice(first + at.start, first + at.stop)
        row = slice(h, h + 1)
        q, g = q_ref[0, :, wide], g_out[:rows, at]
        s_pre = score(left_k[:, wide], q, scale, pre)
        s_own = score(kv_ref[0, 0, :, wide], q, scale, own)
        d_pre = lax.dot_general(left_v[:, at], g, NT, preferred_element_type=F32)
        d_own = lax.dot_general(kv_ref[1, 0, :, wide], g, NT, preferred_element_type=F32)
        terms_ = jnp.exp(s_pre - top[row]) * d_pre + jnp.exp(s_own - top[row]) * d_own
        d_out[row] = jnp.sum(terms_, axis=0, keepdims=True) * inv[row]
    g_out[rows:] = jnp.zeros((2 * heads, span), BF16)
    g_out[rows:, :LANES] = split(d_out[...])


def grads_kernel(count, chunk, scale, q_ref, kv_ref, left_k, left_v, right_q, g_ref, right_g, segs,
                 own_stats, far_stats, from_left, from_right, delta_own,
                 dq_out, dkv_out, p_out, to1, to2, far_delta):
    index = lax.axis_index("seq")
    rows, span = left_v.shape
    first = chunk * span
    heads = span // HEAD_DIM
    chosen = slice(chunk * heads, (chunk + 1) * heads)
    pre, far, own, nxt = masks(count, segs, index, rows)
    top, inv = own_rows(index, own_stats, from_left, chosen)
    r_top, r_inv = right_rows(index, count, far_stats, from_right, chosen)
    right_delta = joined(right_g[rows:, :LANES])

    def run(up_out, down_out):
        for h in range(heads):
            at = slice(h * HEAD_DIM, (h + 1) * HEAD_DIM)
            wide = slice(first + at.start, first + at.stop)
            row = slice(h, h + 1)
            q2 = jnp.concatenate([q_ref[0, :, wide], right_q[:, wide]], axis=0)
            g2 = jnp.concatenate([g_ref[:rows, at], right_g[:rows, at]], axis=0)
            k, kl = kv_ref[0, 0, :, wide], left_k[:, wide]
            s_left = lax.dot_general(kl, q2, NT, preferred_element_type=F32) * scale
            s_here = lax.dot_general(k, q2, NT, preferred_element_type=F32) * scale
            d_left = lax.dot_general(left_v[:, at], g2, NT, preferred_element_type=F32)
            d_own = lax.dot_general(kv_ref[1, 0, :, wide], g2[:rows], NT, preferred_element_type=F32)
            p_pre = jnp.exp(jnp.where(pre, s_left[:, :rows], NEG) - top[row]) * inv[row]
            p_own = jnp.exp(jnp.where(own, s_here[:, :rows], NEG) - top[row]) * inv[row]
            p_far = jnp.exp(jnp.where(far, s_left[:, rows:], NEG) - r_top[row]) * r_inv[row]
            p_nxt = jnp.exp(jnp.where(nxt, s_here[:, rows:], NEG) - r_top[row]) * r_inv[row]
            d_pre, d_far = d_left[:, :rows], d_left[:, rows:]
            extra = jnp.sum(p_far * d_far, axis=0, keepdims=True)
            far_delta[row] = extra
            ds_pre = (p_pre * (d_pre - delta_own[row]) * scale).astype(BF16)
            ds_own = (p_own * (d_own - delta_own[row]) * scale).astype(BF16)
            ds_far = (p_far * (d_far - (right_delta[row] + extra)) * scale).astype(BF16)
            ds_nxt = (p_nxt * (extra * -scale)).astype(BF16)
            p_low = p_pre.astype(BF16)
            p_here = p_own.astype(BF16)
            p_out[h, :rows] = p_low
            p_out[h, rows:] = p_here
            dkv_out[0, :, at] = jnp.dot(
                jnp.concatenate([ds_own, ds_nxt], axis=1), q2, preferred_element_type=F32)
            dkv_out[1, :, at] = jnp.dot(p_here, g2[:rows], preferred_element_type=F32)
            down_out[0, :, at] = jnp.dot(
                jnp.concatenate([ds_pre, ds_far], axis=1), q2, preferred_element_type=F32).astype(BF16)
            down_out[1, :, at] = jnp.dot(
                jnp.concatenate([p_low, p_far.astype(BF16)], axis=1), g2, preferred_element_type=F32).astype(BF16)
            dq_out[:, at] = lax.dot_general(ds_pre, kl, TN, preferred_element_type=F32) + lax.dot_general(
                ds_own, k, TN, preferred_element_type=F32)
            up_out[0, :, at] = lax.dot_general(ds_far, kl, TN, preferred_element_type=F32).astype(BF16)
        up_out[1, : 2 * heads, :LANES] = split(far_delta[...])

    @pl.when(index % 2 == 0)
    def _():
        run(to1, to2)

    @pl.when(index % 2 == 1)
    def _():
        run(to2, to1)


def finish_kernel(count, chunk, scale, dq_ref, dkv_ref, p_ref, q_ref, kv_ref, left_k, got1, got2, *refs):
    grad_q, grad_kv = refs[-2:]
    index = lax.axis_index("seq")
    rows, span = dq_ref.shape
    heads = span // HEAD_DIM
    first = chunk * span

    def add(from_left, from_right):
        no_left, no_right = index == 0, index == count - 1
        delta = jnp.where(no_left, 0.0, joined(from_left[1, : 2 * heads, :LANES]))
        for h in range(heads):
            at = slice(h * HEAD_DIM, (h + 1) * HEAD_DIM)
            wide = slice(first + at.start, first + at.stop)
            factor = delta[h : h + 1] * -scale
            ds_pre = (p_ref[h, :rows].astype(F32) * factor).astype(BF16)
            ds_own = (p_ref[h, rows:].astype(F32) * factor).astype(BF16)
            dq = dq_ref[:, at] + jnp.where(no_left, 0.0, from_left[0, :, at].astype(F32))
            dq = dq + lax.dot_general(ds_pre, left_k[:, wide], TN, preferred_element_type=F32)
            dq = dq + lax.dot_general(ds_own, kv_ref[0, 0, :, wide], TN, preferred_element_type=F32)
            grad_q[0, :, at] = dq.astype(BF16)
            dk = dkv_ref[0, :, at] + jnp.where(no_right, 0.0, from_right[0, :, at].astype(F32))
            dk = dk + jnp.dot(ds_own, q_ref[0, :, wide], preferred_element_type=F32)
            grad_kv[0, 0, :, at] = dk.astype(BF16)
            dv = dkv_ref[1, :, at] + jnp.where(no_right, 0.0, from_right[1, :, at].astype(F32))
            grad_kv[1, 0, :, at] = dv.astype(BF16)

    @pl.when(index % 2 == 0)
    def _():
        add(got2, got1)

    @pl.when(index % 2 == 1)
    def _():
        add(got1, got2)


def shifted(value, steps):
    count = lax.axis_size("seq")
    return lax.ppermute(value, "seq", [(i, (i + steps) % count) for i in range(count)])


def neighbour_swaps(first, second):
    count = lax.axis_size("seq")
    one = [(i, min(i ^ 1, count - 1)) for i in range(count)]
    two = [(i, ((i + 1) ^ 1) - 1) for i in range(count)]
    two = [(i, j if 0 <= j < count else i) for i, j in two]
    return lax.ppermute(first, "seq", one), lax.ppermute(second, "seq", two)


def in_hbm(value):
    return pltpu.with_memory_space_constraint(value, pltpu.HBM)


def shape(dims, dtype=BF16):
    return jax.ShapeDtypeStruct(dims, dtype)


def cost(flops, moved):
    return pl.CostEstimate(flops=int(flops), bytes_accessed=int(moved), transcendentals=0)


def step(query, key_value, grad_y, tags, segments, out_weight):
    _, rows, hc = query.shape
    depth = out_weight.shape[2]
    chips = lax.axis_size("dp") // 2
    count = lax.axis_size("seq")
    span = hc // CHUNKS
    heads = span // HEAD_DIM
    scale = HEAD_DIM ** (-0.5)

    other_weight = swap(out_weight, "dp", 1)
    *slices, first, second, own_v = pl.pallas_call(
        slices_kernel,
        in_specs=[pl.BlockSpec(memory_space=pltpu.HBM)] * 4,
        out_shape=[shape((rows, 2 * depth + LANES))] * chips + [shape((rows, hc))] * 3,
        scratch_shapes=[
            pltpu.VMEM(tags.shape, tags.dtype), pltpu.SemaphoreType.DMA, pltpu.SemaphoreType.DMA((chips + 3,))],
        compiler_params=params(8),
        name="slices",
        cost_estimate=cost(0, 4 * grad_y.size),
    )(in_hbm(grad_y), in_hbm(tags), in_hbm(query), in_hbm(key_value))
    grads = [slices[0]] + [swap(slices[k], "dp", 2 * k) for k in range(1, chips)]
    sides = neighbour_swaps(first, second)
    values = neighbour_swaps(own_v, own_v)

    tile = min(512, span)
    steps = span // tile
    sums = []
    for c in range(CHUNKS):
        w_spec = pl.BlockSpec((2, tile, depth), lambda t, c=c: (0, c * steps + t, 0))
        mine, *parts = pl.pallas_call(
            functools.partial(project_kernel, chips),
            grid=(steps,),
            in_specs=[pl.BlockSpec((rows, 2 * depth + LANES), lambda t: (0, 0))] * chips + [w_spec] * 2,
            out_specs=[pl.BlockSpec((rows, tile), lambda t: (0, t))] * chips,
            out_shape=[shape((rows, span), F32)] + [shape((rows, span))] * (chips - 1),
            scratch_shapes=[pltpu.VMEM((2, 2, chips * rows, depth), BF16)],
            compiler_params=params(12),
            cost_estimate=cost(8 * chips * rows * depth * span, 8 * span * depth),
        )(*grads, out_weight, other_weight)
        sums.append([mine] + [swap(part, "dp", 2 * k) for k, part in enumerate(parts, 1)])

    small = shape((2, HEADS, rows), F32)
    own, far, left_k, right_q = pl.pallas_call(
        functools.partial(stats_kernel, count, scale),
        out_shape=[small] * 2 + [shape((rows, hc))] * 2,
        compiler_params=params(8),
        name="stats",
        cost_estimate=cost(2 * 3 * rows * rows * hc, 20 * rows * hc),
    )(query, key_value, *sides, segments)
    from_right, from_left = shifted(own, -1), shifted(far, 1)

    pieces = []
    for c in range(CHUNKS):
        gout, delta, left_v = pl.pallas_call(
            functools.partial(delta_kernel, count, c, chips - 1, scale),
            out_shape=[shape((rows + 2 * heads, span)), shape((heads, rows), F32), shape((rows, span))],
            compiler_params=params(8),
            cost_estimate=cost(4 * 2 * rows * rows * span, 20 * rows * span),
        )(*sums[c], query, key_value, left_k, *values, segments, own, from_left)
        pieces.append((gout, delta, left_v, shifted(gout, -1)))

    half = shape((2, rows, span))
    parts = []
    for c in range(CHUNKS):
        gout, delta, left_v, right_g = pieces[c]
        *kept, to1, to2 = pl.pallas_call(
            functools.partial(grads_kernel, count, c, scale),
            out_shape=[
                shape((rows, span), F32), shape((2, rows, span), F32), shape((heads, 2 * rows, rows)), half, half],
            scratch_shapes=[pltpu.VMEM((heads, rows), F32)],
            compiler_params=params(12),
            cost_estimate=cost(10 * 3 * rows * rows * span, 40 * rows * span),
        )(query, key_value, left_k, left_v, right_q, gout, right_g, segments, own, far, from_left, from_right, delta)
        parts.append((*kept, query, key_value, left_k, *neighbour_swaps(to1, to2)))

    results = ()
    for c in range(CHUNKS):
        results = pl.pallas_call(
            functools.partial(finish_kernel, count, c, scale),
            grid=(1,),
            in_specs=[pl.BlockSpec(memory_space=pltpu.VMEM)] * len(parts[c])
            + [pl.BlockSpec(memory_space=pl.ANY)] * len(results),
            out_specs=[
                pl.BlockSpec((1, rows, span), lambda t, c=c: (0, 0, c)),
                pl.BlockSpec((2, 1, rows, span), lambda t, c=c: (0, 0, 0, c)),
            ],
            out_shape=[shape(query.shape), shape(key_value.shape)],
            input_output_aliases={len(parts[c]) + n: n for n in range(len(results))},
            compiler_params=params(12),
            cost_estimate=cost(0, 20 * rows * span),
        )(*parts[c], *results)
    return tuple(results)


def solution(mesh):
    return jax.shard_map(
        step,
        mesh=mesh,
        in_specs=(
            P("dp", "seq", None),
            P(None, "dp", "seq", None),
            P("dp", "seq", None),
            P("dp", "seq"),
            P("dp", None),
            P(None, None, "dp"),
        ),
        out_specs=(P("dp", "seq", None), P(None, "dp", "seq", None)),
        check_vma=False,
    )
```

```python
import functools
import jax
import jax.numpy as jnp
from jax import lax
from jax.experimental import pallas as pl
from jax.experimental.pallas import tpu as pltpu
from jax.sharding import PartitionSpec as P


HEADS = 16
HEAD_DIM = 128
PARTS = 2

NEG = -1e30
LANES = 128
BF16 = jnp.bfloat16
F32 = jnp.float32
NT = (((1,), (1,)), ((), ()))
TN = (((0,), (0,)), ((), ()))


def params(mib):
    return pltpu.CompilerParams(vmem_limit_bytes=mib << 20)


def lane_slice(start, size):
    return pl.ds(pl.multiple_of(start, LANES), size)


def swap(value, axis, bits):
    return lax.ppermute(value, axis, [(i, i ^ bits) for i in range(lax.axis_size(axis))])


def column_of(row):
    n = row.shape[1]
    same = lax.broadcasted_iota(jnp.int32, (n, n), 0) == lax.broadcasted_iota(jnp.int32, (n, n), 1)
    return jnp.sum(jnp.where(same, row.astype(F32), 0.0), axis=1, keepdims=True)


def grad_slices_kernel(grad_ref, tags_ref, *refs):
    outs, (tags, tag_sem, sem) = refs[:-3], refs[-3:]
    chip = lax.axis_index("dp") // 2
    width = outs[0].shape[1] - LANES
    tag_copy = pltpu.make_async_copy(tags_ref, tags, tag_sem)
    copies = [
        pltpu.make_async_copy(grad_ref.at[0, :, lane_slice((chip ^ k) * width, width)], out.at[:, :width], sem.at[k])
        for k, out in enumerate(outs)
    ]
    for copy in [tag_copy] + copies:
        copy.start()
    tag_copy.wait()
    tag = jnp.broadcast_to(column_of(tags[...]), (grad_ref.shape[1], LANES)).astype(BF16)
    for out in outs:
        out[:, width:] = tag
    for copy in copies:
        copy.wait()


def side_slices_kernel(q_ref, kv_ref, first, second, v_out, sem):
    v_copy = pltpu.make_async_copy(kv_ref.at[1, 0], v_out, sem.at[0])

    def sides(up, down):
        copies = [
            pltpu.make_async_copy(kv_ref.at[0, 0], up, sem.at[1]),
            pltpu.make_async_copy(q_ref.at[0], down, sem.at[2]),
            v_copy,
        ]
        for copy in copies:
            copy.start()
        for copy in copies:
            copy.wait()

    even = lax.axis_index("seq") % 2 == 0

    @pl.when(even)
    def _():
        sides(first, second)

    @pl.when(jnp.logical_not(even))
    def _():
        sides(second, first)


def project_kernel(chips, first, *refs):
    grads, (own_w, other_w), (mine, *parts, lhs) = refs[:chips], refs[chips : chips + 2], refs[chips + 2 :]
    rows = grads[0].shape[0]
    depth = own_w.shape[2]
    core = lax.axis_index("dp") % 2

    for k, grad in enumerate(grads):
        text = grad[:, 2 * depth : 2 * depth + 1] == 1
        for side in range(2):
            g = grad[:, lane_slice((core ^ side) * depth, depth)]
            lhs[side, 0, k * rows : (k + 1) * rows] = jnp.where(text, jnp.zeros_like(g), g)
            lhs[side, 1, k * rows : (k + 1) * rows] = jnp.where(text, g, jnp.zeros_like(g))

    total = None
    for side, w in enumerate((own_w, other_w)):
        for kind in range(2):
            rhs = w[kind, first : first + mine.shape[1]]
            term = lax.dot_general(lhs[side, kind], rhs, NT, preferred_element_type=F32)
            total = term if total is None else total + term
    mine[...] = total[:rows]
    for k, part in enumerate(parts):
        part[...] = total[(k + 1) * rows : (k + 2) * rows].astype(BF16)


def split(values):
    high = values.astype(BF16)
    return jnp.concatenate([high, (values - high.astype(F32)).astype(BF16)], axis=0)


def joined(pieces):
    half = pieces.shape[0] // 2
    return pieces[:half].astype(F32) + pieces[half:].astype(F32)


def masks(count, segs, index, rows):
    def segment(back):
        at = jnp.clip(index + back, 0, count - 1)
        return segs[:, lane_slice(at * rows, rows)].astype(F32)

    left, own, right = segment(-1), segment(0), segment(1)
    left_at, own_at = column_of(left), column_of(own)
    no_left, no_right = index == 0, index == count - 1
    key = lax.broadcasted_iota(jnp.int32, (rows, rows), 0)
    query = lax.broadcasted_iota(jnp.int32, (rows, rows), 1)
    return (
        (left_at == own) & jnp.logical_not(no_left),
        (left_at == right) & jnp.logical_not(no_left | no_right),
        (own_at == own) & (key <= query),
        (own_at == right) & jnp.logical_not(no_right),
    )


def score(keys, queries, scale, mask):
    s = lax.dot_general(keys, queries, NT, preferred_element_type=F32) * scale
    return jnp.where(mask, s, NEG)


def pair_of(even, to_even, to_odd):
    def copy(items):
        for source, target in items:
            target[...] = source[...]

    @pl.when(even)
    def _():
        copy(to_even)

    @pl.when(jnp.logical_not(even))
    def _():
        copy(to_odd)


def stats_kernel(count, scale, q_ref, kv_ref, got1, got2, segs, own_out, far_out, left_k, right_q):
    index = lax.axis_index("seq")
    rows, hc = left_k.shape
    pair_of(index % 2 == 0, [(got2, left_k), (got1, right_q)], [(got1, left_k), (got2, right_q)])
    pre, far, own, _ = masks(count, segs, index, rows)
    for h in range(hc // HEAD_DIM):
        at = slice(h * HEAD_DIM, (h + 1) * HEAD_DIM)
        kl, q = left_k[:, at], q_ref[0, :, at]
        s_pre = score(kl, q, scale, pre)
        s_own = score(kv_ref[0, 0, :, at], q, scale, own)
        s_far = score(kl, right_q[:, at], scale, far)
        top = jnp.max(jnp.maximum(s_pre, s_own), axis=0, keepdims=True)
        own_out[0, h : h + 1] = top
        own_out[1, h : h + 1] = jnp.sum(jnp.exp(s_pre - top) + jnp.exp(s_own - top), axis=0, keepdims=True)
        top = jnp.max(s_far, axis=0, keepdims=True)
        far_out[0, h : h + 1] = top
        far_out[1, h : h + 1] = jnp.sum(jnp.exp(s_far - top), axis=0, keepdims=True)


def merged(one, two):
    top = jnp.maximum(one[0], two[0])
    return top, 1.0 / (one[1] * jnp.exp(one[0] - top) + two[1] * jnp.exp(two[0] - top))


def own_rows(index, own_stats, from_left, heads):
    no_left = index == 0
    far = (jnp.where(no_left, NEG, from_left[0, heads]), jnp.where(no_left, 0.0, from_left[1, heads]))
    return merged((own_stats[0, heads], own_stats[1, heads]), far)


def right_rows(index, count, far_stats, from_right, heads):
    no_right = index == count - 1
    own = (jnp.where(no_right, 0.0, from_right[0, heads]), jnp.where(no_right, 1.0, from_right[1, heads]))
    return merged(own, (far_stats[0, heads], far_stats[1, heads]))


def delta_kernel(count, first, terms, scale, mine, *refs):
    parts = refs[:terms]
    q_ref, kv_ref, left_k, got1, got2, segs, own_stats, from_left, g_out, d_out, left_v = refs[terms:]
    rows, span = mine.shape
    index = lax.axis_index("seq")
    lanes = slice(first, first + span)
    pair_of(index % 2 == 0, [(got2.at[:, lanes], left_v)], [(got1.at[:, lanes], left_v)])
    total = mine[...]
    for part in parts:
        total = total + part[...].astype(F32)
    g_out[:rows] = total.astype(BF16)
    pre, _, own, _ = masks(count, segs, index, rows)
    heads = span // HEAD_DIM
    top, inv = own_rows(index, own_stats, from_left, slice(first // HEAD_DIM, first // HEAD_DIM + heads))
    for h in range(heads):
        at = slice(h * HEAD_DIM, (h + 1) * HEAD_DIM)
        wide = slice(first + at.start, first + at.stop)
        row = slice(h, h + 1)
        q, g = q_ref[0, :, wide], g_out[:rows, at]
        s_pre = score(left_k[:, wide], q, scale, pre)
        s_own = score(kv_ref[0, 0, :, wide], q, scale, own)
        d_pre = lax.dot_general(left_v[:, at], g, NT, preferred_element_type=F32)
        d_own = lax.dot_general(kv_ref[1, 0, :, wide], g, NT, preferred_element_type=F32)
        terms_ = jnp.exp(s_pre - top[row]) * d_pre + jnp.exp(s_own - top[row]) * d_own
        d_out[row] = jnp.sum(terms_, axis=0, keepdims=True) * inv[row]
    g_out[rows:] = jnp.zeros((2 * heads, span), BF16)
    g_out[rows:, :LANES] = split(d_out[...])


def grads_kernel(count, first, scale, q_ref, kv_ref, left_k, left_v, right_q, g_ref, right_g, segs,
                 own_stats, far_stats, from_left, from_right, delta_own,
                 dq_out, dkv_out, p_out, to1, to2, far_delta):
    index = lax.axis_index("seq")
    rows, span = left_v.shape
    heads = span // HEAD_DIM
    chosen = slice(first // HEAD_DIM, first // HEAD_DIM + heads)
    pre, far, own, nxt = masks(count, segs, index, rows)
    top, inv = own_rows(index, own_stats, from_left, chosen)
    r_top, r_inv = right_rows(index, count, far_stats, from_right, chosen)
    right_delta = joined(right_g[rows:, :LANES])

    def run(up_out, down_out):
        for h in range(heads):
            at = slice(h * HEAD_DIM, (h + 1) * HEAD_DIM)
            wide = slice(first + at.start, first + at.stop)
            row = slice(h, h + 1)
            q2 = jnp.concatenate([q_ref[0, :, wide], right_q[:, wide]], axis=0)
            g2 = jnp.concatenate([g_ref[:rows, at], right_g[:rows, at]], axis=0)
            k, kl = kv_ref[0, 0, :, wide], left_k[:, wide]
            s_left = lax.dot_general(kl, q2, NT, preferred_element_type=F32) * scale
            s_here = lax.dot_general(k, q2, NT, preferred_element_type=F32) * scale
            d_left = lax.dot_general(left_v[:, at], g2, NT, preferred_element_type=F32)
            d_own = lax.dot_general(kv_ref[1, 0, :, wide], g2[:rows], NT, preferred_element_type=F32)
            p_pre = jnp.exp(jnp.where(pre, s_left[:, :rows], NEG) - top[row]) * inv[row]
            p_own = jnp.exp(jnp.where(own, s_here[:, :rows], NEG) - top[row]) * inv[row]
            p_far = jnp.exp(jnp.where(far, s_left[:, rows:], NEG) - r_top[row]) * r_inv[row]
            p_nxt = jnp.exp(jnp.where(nxt, s_here[:, rows:], NEG) - r_top[row]) * r_inv[row]
            d_pre, d_far = d_left[:, :rows], d_left[:, rows:]
            extra = jnp.sum(p_far * d_far, axis=0, keepdims=True)
            far_delta[row] = extra
            ds_pre = (p_pre * (d_pre - delta_own[row]) * scale).astype(BF16)
            ds_own = (p_own * (d_own - delta_own[row]) * scale).astype(BF16)
            ds_far = (p_far * (d_far - (right_delta[row] + extra)) * scale).astype(BF16)
            ds_nxt = (p_nxt * (extra * -scale)).astype(BF16)
            p_low = p_pre.astype(BF16)
            p_here = p_own.astype(BF16)
            p_out[h, :rows] = p_low
            p_out[h, rows:] = p_here
            dkv_out[0, :, at] = jnp.dot(
                jnp.concatenate([ds_own, ds_nxt], axis=1), q2, preferred_element_type=F32)
            dkv_out[1, :, at] = jnp.dot(p_here, g2[:rows], preferred_element_type=F32)
            down_out[0, :, at] = jnp.dot(
                jnp.concatenate([ds_pre, ds_far], axis=1), q2, preferred_element_type=F32).astype(BF16)
            down_out[1, :, at] = jnp.dot(
                jnp.concatenate([p_low, p_far.astype(BF16)], axis=1), g2, preferred_element_type=F32).astype(BF16)
            dq_out[:, at] = lax.dot_general(ds_pre, kl, TN, preferred_element_type=F32) + lax.dot_general(
                ds_own, k, TN, preferred_element_type=F32)
            up_out[0, :, at] = lax.dot_general(ds_far, kl, TN, preferred_element_type=F32).astype(BF16)
        up_out[1, : 2 * heads, :LANES] = split(far_delta[...])

    @pl.when(index % 2 == 0)
    def _():
        run(to1, to2)

    @pl.when(index % 2 == 1)
    def _():
        run(to2, to1)


def finish_kernel(count, first, scale, dq_ref, dkv_ref, p_ref, q_ref, kv_ref, left_k, got1, got2, *refs):
    grad_q, grad_kv, done, sem = refs[-4:]
    index = lax.axis_index("seq")
    rows, span = dq_ref.shape
    heads = span // HEAD_DIM

    def add(from_left, from_right):
        no_left, no_right = index == 0, index == count - 1
        delta = jnp.where(no_left, 0.0, joined(from_left[1, : 2 * heads, :LANES]))
        for h in range(heads):
            at = slice(h * HEAD_DIM, (h + 1) * HEAD_DIM)
            wide = slice(first + at.start, first + at.stop)
            factor = delta[h : h + 1] * -scale
            ds_pre = (p_ref[h, :rows].astype(F32) * factor).astype(BF16)
            ds_own = (p_ref[h, rows:].astype(F32) * factor).astype(BF16)
            dq = dq_ref[:, at] + jnp.where(no_left, 0.0, from_left[0, :, at].astype(F32))
            dq = dq + lax.dot_general(ds_pre, left_k[:, wide], TN, preferred_element_type=F32)
            dq = dq + lax.dot_general(ds_own, kv_ref[0, 0, :, wide], TN, preferred_element_type=F32)
            done[0, :, at] = dq.astype(BF16)
            dk = dkv_ref[0, :, at] + jnp.where(no_right, 0.0, from_right[0, :, at].astype(F32))
            dk = dk + jnp.dot(ds_own, q_ref[0, :, wide], preferred_element_type=F32)
            done[1, :, at] = dk.astype(BF16)
            dv = dkv_ref[1, :, at] + jnp.where(no_right, 0.0, from_right[1, :, at].astype(F32))
            done[2, :, at] = dv.astype(BF16)

    @pl.when(index % 2 == 0)
    def _():
        add(got2, got1)

    @pl.when(index % 2 == 1)
    def _():
        add(got1, got2)

    lanes = slice(first, first + span)
    copies = [
        pltpu.make_async_copy(done.at[0], grad_q.at[0, :, lanes], sem.at[0]),
        pltpu.make_async_copy(done.at[1:], grad_kv.at[:, 0, :, lanes], sem.at[1]),
    ]
    for copy in copies:
        copy.start()
    for copy in copies:
        copy.wait()


def shifted(value, steps):
    count = lax.axis_size("seq")
    return lax.ppermute(value, "seq", [(i, (i + steps) % count) for i in range(count)])


def neighbour_swaps(first, second):
    count = lax.axis_size("seq")
    one = [(i, min(i ^ 1, count - 1)) for i in range(count)]
    two = [(i, ((i + 1) ^ 1) - 1) for i in range(count)]
    two = [(i, j if 0 <= j < count else i) for i, j in two]
    return lax.ppermute(first, "seq", one), lax.ppermute(second, "seq", two)


def in_hbm(value):
    return pltpu.with_memory_space_constraint(value, pltpu.HBM)


def shape(dims, dtype=BF16):
    return jax.ShapeDtypeStruct(dims, dtype)


def cost(flops, moved):
    return pl.CostEstimate(flops=int(flops), bytes_accessed=int(moved), transcendentals=0)


def chunks(hc):
    heads = hc // HEAD_DIM
    cuts = [heads * n // PARTS for n in range(PARTS + 1)]
    return [(HEAD_DIM * a, HEAD_DIM * (b - a)) for a, b in zip(cuts, cuts[1:])]


def step(query, key_value, grad_y, tags, segments, out_weight):
    _, rows, hc = query.shape
    depth = out_weight.shape[2]
    chips = lax.axis_size("dp") // 2
    count = lax.axis_size("seq")
    scale = HEAD_DIM ** (-0.5)

    other_weight = swap(out_weight, "dp", 1)
    slices = pl.pallas_call(
        grad_slices_kernel,
        in_specs=[pl.BlockSpec(memory_space=pltpu.HBM)] * 2,
        out_shape=[shape((rows, 2 * depth + LANES))] * chips,
        scratch_shapes=[
            pltpu.VMEM(tags.shape, tags.dtype), pltpu.SemaphoreType.DMA, pltpu.SemaphoreType.DMA((chips,))],
        compiler_params=params(4),
        name="grad_slices",
        cost_estimate=cost(0, 4 * grad_y.size),
    )(in_hbm(grad_y), in_hbm(tags))
    grads = [slices[0]] + [swap(slices[k], "dp", 2 * k) for k in range(1, chips)]
    first, second, own_v = pl.pallas_call(
        side_slices_kernel,
        in_specs=[pl.BlockSpec(memory_space=pltpu.HBM)] * 2,
        out_shape=[shape((rows, hc))] * 3,
        scratch_shapes=[pltpu.SemaphoreType.DMA((3,))],
        compiler_params=params(8),
        name="side_slices",
        cost_estimate=cost(0, 12 * query.size),
    )(in_hbm(query), in_hbm(key_value))
    sides = neighbour_swaps(first, second)
    values = neighbour_swaps(own_v, own_v)

    sums = []
    for first, span in chunks(hc):
        mine, *parts = pl.pallas_call(
            functools.partial(project_kernel, chips, first),
            out_shape=[shape((rows, span), F32)] + [shape((rows, span))] * (chips - 1),
            scratch_shapes=[pltpu.VMEM((2, 2, chips * rows, depth), BF16)],
            compiler_params=params(12),
            cost_estimate=cost(8 * chips * rows * depth * span, 8 * span * depth),
        )(*grads, out_weight, other_weight)
        sums.append([mine] + [swap(part, "dp", 2 * k) for k, part in enumerate(parts, 1)])

    small = shape((2, HEADS, rows), F32)
    own, far, left_k, right_q = pl.pallas_call(
        functools.partial(stats_kernel, count, scale),
        out_shape=[small] * 2 + [shape((rows, hc))] * 2,
        compiler_params=params(8),
        name="stats",
        cost_estimate=cost(2 * 3 * rows * rows * hc, 20 * rows * hc),
    )(query, key_value, *sides, segments)
    from_right, from_left = shifted(own, -1), shifted(far, 1)

    pieces = []
    for c, (first, span) in enumerate(chunks(hc)):
        heads = span // HEAD_DIM
        gout, delta, left_v = pl.pallas_call(
            functools.partial(delta_kernel, count, first, chips - 1, scale),
            out_shape=[shape((rows + 2 * heads, span)), shape((heads, rows), F32), shape((rows, span))],
            compiler_params=params(8),
            cost_estimate=cost(4 * 2 * rows * rows * span, 20 * rows * span),
        )(*sums[c], query, key_value, left_k, *values, segments, own, from_left)
        pieces.append((gout, delta, left_v, shifted(gout, -1)))

    parts = []
    for c, (first, span) in enumerate(chunks(hc)):
        heads, half = span // HEAD_DIM, shape((2, rows, span))
        gout, delta, left_v, right_g = pieces[c]
        *kept, to1, to2 = pl.pallas_call(
            functools.partial(grads_kernel, count, first, scale),
            out_shape=[
                shape((rows, span), F32), shape((2, rows, span), F32), shape((heads, 2 * rows, rows)), half, half],
            scratch_shapes=[pltpu.VMEM((heads, rows), F32)],
            compiler_params=params(12),
            cost_estimate=cost(10 * 3 * rows * rows * span, 40 * rows * span),
        )(query, key_value, left_k, left_v, right_q, gout, right_g, segments, own, far, from_left, from_right, delta)
        parts.append((*kept, query, key_value, left_k, *neighbour_swaps(to1, to2)))

    results = ()
    anywhere = pl.BlockSpec(memory_space=pl.ANY)
    for c, (first, span) in enumerate(chunks(hc)):
        results = pl.pallas_call(
            functools.partial(finish_kernel, count, first, scale),
            in_specs=[pl.BlockSpec(memory_space=pltpu.VMEM)] * len(parts[c]) + [anywhere] * len(results),
            out_specs=[anywhere] * 2,
            out_shape=[shape(query.shape), shape(key_value.shape)],
            scratch_shapes=[pltpu.VMEM((3, rows, span), BF16), pltpu.SemaphoreType.DMA((2,))],
            input_output_aliases={len(parts[c]) + n: n for n in range(len(results))},
            compiler_params=params(12),
            cost_estimate=cost(0, 20 * rows * span),
        )(*parts[c], *results)
    return tuple(results)


def solution(mesh):
    return jax.shard_map(
        step,
        mesh=mesh,
        in_specs=(
            P("dp", "seq", None),
            P(None, "dp", "seq", None),
            P("dp", "seq", None),
            P("dp", "seq"),
            P("dp", None),
            P(None, None, "dp"),
        ),
        out_specs=(P("dp", "seq", None), P(None, "dp", "seq", None)),
        check_vma=False,
    )
```

```python
import functools
import jax
import jax.numpy as jnp
from jax import lax
from jax.experimental import pallas as pl
from jax.experimental.pallas import tpu as pltpu
from jax.sharding import PartitionSpec as P


HEADS = 16
HEAD_DIM = 128
PARTS = 2

NEG = -1e30
LANES = 128
TAG_ROWS = 16
BF16 = jnp.bfloat16
F32 = jnp.float32
NT = (((1,), (1,)), ((), ()))
TN = (((0,), (0,)), ((), ()))


def params(mib):
    return pltpu.CompilerParams(vmem_limit_bytes=mib << 20)


def lane_slice(start, size):
    return pl.ds(pl.multiple_of(start, LANES), size)


def swap(value, axis, bits):
    return lax.ppermute(value, axis, [(i, i ^ bits) for i in range(lax.axis_size(axis))])


def column_of(row):
    n = row.shape[1]
    same = lax.broadcasted_iota(jnp.int32, (n, n), 0) == lax.broadcasted_iota(jnp.int32, (n, n), 1)
    return jnp.sum(jnp.where(same, row.astype(F32), 0.0), axis=1, keepdims=True)


def grad_slices_kernel(grad_ref, tags_ref, *refs):
    outs, (tags, tag_sem, sem) = refs[:-3], refs[-3:]
    chip = lax.axis_index("dp") // 2
    rows = grad_ref.shape[1]
    blocks = (outs[0].shape[0] - TAG_ROWS) // rows
    tag_copy = pltpu.make_async_copy(tags_ref, tags, tag_sem)
    copies = [
        pltpu.make_async_copy(
            grad_ref.at[0, :, lane_slice(((chip ^ k) * blocks + n) * LANES, LANES)],
            out.at[n * rows : (n + 1) * rows],
            sem.at[k, n],
        )
        for k, out in enumerate(outs)
        for n in range(blocks)
    ]
    for copy in [tag_copy] + copies:
        copy.start()
    tag_copy.wait()
    tag = jnp.broadcast_to(tags[...].astype(F32), (TAG_ROWS, LANES)).astype(BF16)
    for out in outs:
        out[blocks * rows :] = tag
    for copy in copies:
        copy.wait()


def side_slices_kernel(cuts, q_ref, kv_ref, first, second, *refs):
    v_outs, sem = refs[:-1], refs[-1]
    v_copies = [
        pltpu.make_async_copy(kv_ref.at[1, 0, :, at : at + width], out, sem.at[2 + n])
        for n, ((at, width), out) in enumerate(zip(cuts, v_outs))
    ]

    def sides(up, down):
        copies = [
            pltpu.make_async_copy(kv_ref.at[0, 0], up, sem.at[1]),
            pltpu.make_async_copy(q_ref.at[0], down, sem.at[0]),
            *v_copies,
        ]
        for copy in copies:
            copy.start()
        for copy in copies:
            copy.wait()

    even = lax.axis_index("seq") % 2 == 0

    @pl.when(even)
    def _():
        sides(first, second)

    @pl.when(jnp.logical_not(even))
    def _():
        sides(second, first)


def project_kernel(chips, first, *refs):
    grads, (own_w, other_w), (mine, *parts, lhs) = refs[:chips], refs[chips : chips + 2], refs[chips + 2 :]
    depth = own_w.shape[2]
    blocks = depth // LANES
    rows = mine.shape[0]
    core = lax.axis_index("dp") % 2
    for k, grad in enumerate(grads):
        text = column_of(grad[2 * blocks * rows : 2 * blocks * rows + 1]) == 1.0
        for side in range(2):
            for n in range(blocks):
                at = pl.ds(pl.multiple_of(((core ^ side) * blocks + n) * rows, rows), rows)
                g = grad[at]
                where = (slice(k * rows, (k + 1) * rows), slice(n * LANES, (n + 1) * LANES))
                lhs[(side, 0, *where)] = jnp.where(text, jnp.zeros_like(g), g)
                lhs[(side, 1, *where)] = jnp.where(text, g, jnp.zeros_like(g))

    total = None
    for side, w in enumerate((own_w, other_w)):
        for kind in range(2):
            rhs = w[kind, first : first + mine.shape[1]]
            term = lax.dot_general(lhs[side, kind], rhs, NT, preferred_element_type=F32)
            total = term if total is None else total + term
    mine[...] = total[:rows]
    for k, part in enumerate(parts):
        part[...] = total[(k + 1) * rows : (k + 2) * rows].astype(BF16)


def split(values):
    high = values.astype(BF16)
    return jnp.concatenate([high, (values - high.astype(F32)).astype(BF16)], axis=0)


def joined(pieces):
    half = pieces.shape[0] // 2
    return pieces[:half].astype(F32) + pieces[half:].astype(F32)


def masks(count, segs, index, rows):
    def segment(back):
        at = jnp.clip(index + back, 0, count - 1)
        return segs[:, lane_slice(at * rows, rows)].astype(F32)

    left, own, right = segment(-1), segment(0), segment(1)
    left_at, own_at = column_of(left), column_of(own)
    no_left, no_right = index == 0, index == count - 1
    key = lax.broadcasted_iota(jnp.int32, (rows, rows), 0)
    query = lax.broadcasted_iota(jnp.int32, (rows, rows), 1)
    return (
        (left_at == own) & jnp.logical_not(no_left),
        (left_at == right) & jnp.logical_not(no_left | no_right),
        (own_at == own) & (key <= query),
        (own_at == right) & jnp.logical_not(no_right),
    )


def score(keys, queries, scale, mask):
    s = lax.dot_general(keys, queries, NT, preferred_element_type=F32) * scale
    return jnp.where(mask, s, NEG)


def pair_of(even, to_even, to_odd):
    def copy(items):
        for source, target in items:
            target[...] = source[...]

    @pl.when(even)
    def _():
        copy(to_even)

    @pl.when(jnp.logical_not(even))
    def _():
        copy(to_odd)


def stats_kernel(count, scale, q_ref, kv_ref, got1, got2, segs, own_out, far_out, left_k, right_q):
    index = lax.axis_index("seq")
    rows, hc = left_k.shape
    pair_of(index % 2 == 0, [(got2, left_k), (got1, right_q)], [(got1, left_k), (got2, right_q)])
    pre, far, own, _ = masks(count, segs, index, rows)
    for h in range(hc // HEAD_DIM):
        at = slice(h * HEAD_DIM, (h + 1) * HEAD_DIM)
        kl, q = left_k[:, at], q_ref[0, :, at]
        s_pre = score(kl, q, scale, pre)
        s_own = score(kv_ref[0, 0, :, at], q, scale, own)
        s_far = score(kl, right_q[:, at], scale, far)
        top = jnp.max(jnp.maximum(s_pre, s_own), axis=0, keepdims=True)
        own_out[0, h : h + 1] = top
        own_out[1, h : h + 1] = jnp.sum(jnp.exp(s_pre - top) + jnp.exp(s_own - top), axis=0, keepdims=True)
        top = jnp.max(s_far, axis=0, keepdims=True)
        far_out[0, h : h + 1] = top
        far_out[1, h : h + 1] = jnp.sum(jnp.exp(s_far - top), axis=0, keepdims=True)


def merged(one, two):
    top = jnp.maximum(one[0], two[0])
    first = one[1] * jnp.exp(one[0] - top)
    inverse = 1.0 / (first + two[1] * jnp.exp(two[0] - top))
    return top, inverse, first * inverse


def own_rows(index, own_stats, from_left, heads):
    no_left = index == 0
    far = (jnp.where(no_left, NEG, from_left[0, heads]), jnp.where(no_left, 0.0, from_left[1, heads]))
    return merged((own_stats[0, heads], own_stats[1, heads]), far)


def right_rows(index, count, far_stats, from_right, heads):
    no_right = index == count - 1
    own = (jnp.where(no_right, 0.0, from_right[0, heads]), jnp.where(no_right, 1.0, from_right[1, heads]))
    return merged(own, (far_stats[0, heads], far_stats[1, heads]))


def delta_kernel(count, first, terms, scale, mine, *refs):
    parts = refs[:terms]
    q_ref, kv_ref, left_k, left_v, segs, own_stats, g_out, d_out = refs[terms:]
    rows, span = mine.shape
    heads = span // HEAD_DIM
    index = lax.axis_index("seq")
    pre, _, own, _ = masks(count, segs, index, rows)
    for h in range(heads):
        at = slice(h * HEAD_DIM, (h + 1) * HEAD_DIM)
        wide = slice(first + at.start, first + at.stop)
        row = slice(h, h + 1)
        stat = first // HEAD_DIM + h
        total = mine[:, at]
        for part in parts:
            total = total + part[:, at].astype(F32)
        g_out[h * rows : (h + 1) * rows] = total.astype(BF16)
        q, g = q_ref[0, :, wide], g_out[h * rows : (h + 1) * rows]
        s_pre = score(left_k[:, wide], q, scale, pre)
        s_own = score(kv_ref[0, 0, :, wide], q, scale, own)
        d_pre = lax.dot_general(left_v[:, at], g, NT, preferred_element_type=F32)
        d_own = lax.dot_general(kv_ref[1, 0, :, wide], g, NT, preferred_element_type=F32)
        top = own_stats[0, stat : stat + 1]
        weighed = jnp.exp(s_pre - top) * d_pre + jnp.exp(s_own - top) * d_own
        d_out[row] = jnp.sum(weighed, axis=0, keepdims=True) / own_stats[1, stat : stat + 1]
    g_out[heads * rows :] = split(d_out[...])


def grads_kernel(count, first, scale, q_ref, kv_ref, left_k, left_v, right_q, g_ref, right_g, segs,
                 own_stats, far_stats, from_left, from_right, delta_own,
                 dq_out, dkv_out, p_out, to1, to2, far_delta):
    index = lax.axis_index("seq")
    rows, span = left_v.shape
    heads = span // HEAD_DIM
    chosen = slice(first // HEAD_DIM, first // HEAD_DIM + heads)
    pre, far, own, nxt = masks(count, segs, index, rows)
    top, inv, share = own_rows(index, own_stats, from_left, chosen)
    r_top, r_inv, r_share = right_rows(index, count, far_stats, from_right, chosen)
    own_delta = delta_own[...] * share
    right_delta = joined(right_g[heads * rows :]) * r_share

    def run(up_out, down_out):
        for h in range(heads):
            at = slice(h * HEAD_DIM, (h + 1) * HEAD_DIM)
            wide = slice(first + at.start, first + at.stop)
            row = slice(h, h + 1)
            q2 = jnp.concatenate([q_ref[0, :, wide], right_q[:, wide]], axis=0)
            block = slice(h * rows, (h + 1) * rows)
            g2 = jnp.concatenate([g_ref[block], right_g[block]], axis=0)
            k, kl = kv_ref[0, 0, :, wide], left_k[:, wide]
            s_left = lax.dot_general(kl, q2, NT, preferred_element_type=F32) * scale
            s_here = lax.dot_general(k, q2, NT, preferred_element_type=F32) * scale
            d_left = lax.dot_general(left_v[:, at], g2, NT, preferred_element_type=F32)
            d_own = lax.dot_general(kv_ref[1, 0, :, wide], g2[:rows], NT, preferred_element_type=F32)
            p_pre = jnp.exp(jnp.where(pre, s_left[:, :rows], NEG) - top[row]) * inv[row]
            p_own = jnp.exp(jnp.where(own, s_here[:, :rows], NEG) - top[row]) * inv[row]
            p_far = jnp.exp(jnp.where(far, s_left[:, rows:], NEG) - r_top[row]) * r_inv[row]
            p_nxt = jnp.exp(jnp.where(nxt, s_here[:, rows:], NEG) - r_top[row]) * r_inv[row]
            d_pre, d_far = d_left[:, :rows], d_left[:, rows:]
            extra = jnp.sum(p_far * d_far, axis=0, keepdims=True)
            far_delta[row] = extra
            ds_pre = (p_pre * (d_pre - own_delta[row]) * scale).astype(BF16)
            ds_own = (p_own * (d_own - own_delta[row]) * scale).astype(BF16)
            ds_far = (p_far * (d_far - (right_delta[row] + extra)) * scale).astype(BF16)
            ds_nxt = (p_nxt * (extra * -scale)).astype(BF16)
            p_low = p_pre.astype(BF16)
            p_here = p_own.astype(BF16)
            p_out[h, :rows] = p_low
            p_out[h, rows:] = p_here
            dkv_out[0, :, at] = jnp.dot(
                jnp.concatenate([ds_own, ds_nxt], axis=1), q2, preferred_element_type=F32)
            dkv_out[1, :, at] = jnp.dot(p_here, g2[:rows], preferred_element_type=F32)
            down_out[0, :, at] = jnp.dot(
                jnp.concatenate([ds_pre, ds_far], axis=1), q2, preferred_element_type=F32).astype(BF16)
            down_out[1, :, at] = jnp.dot(
                jnp.concatenate([p_low, p_far.astype(BF16)], axis=1), g2, preferred_element_type=F32).astype(BF16)
            dq_out[:, at] = lax.dot_general(ds_pre, kl, TN, preferred_element_type=F32) + lax.dot_general(
                ds_own, k, TN, preferred_element_type=F32)
            up_out[0, :, at] = lax.dot_general(ds_far, kl, TN, preferred_element_type=F32).astype(BF16)
        up_out[1, : 2 * heads, :LANES] = split(far_delta[...])

    @pl.when(index % 2 == 0)
    def _():
        run(to1, to2)

    @pl.when(index % 2 == 1)
    def _():
        run(to2, to1)


def finish_kernel(count, first, scale, dq_ref, dkv_ref, p_ref, q_ref, kv_ref, left_k, got1, got2, *refs):
    grad_q, grad_kv, done, sem = refs[-4:]
    index = lax.axis_index("seq")
    rows, span = dq_ref.shape
    heads = span // HEAD_DIM

    def add(from_left, from_right):
        no_left, no_right = index == 0, index == count - 1
        delta = jnp.where(no_left, 0.0, joined(from_left[1, : 2 * heads, :LANES]))
        for h in range(heads):
            at = slice(h * HEAD_DIM, (h + 1) * HEAD_DIM)
            wide = slice(first + at.start, first + at.stop)
            factor = delta[h : h + 1] * -scale
            ds_pre = (p_ref[h, :rows].astype(F32) * factor).astype(BF16)
            ds_own = (p_ref[h, rows:].astype(F32) * factor).astype(BF16)
            dq = dq_ref[:, at] + jnp.where(no_left, 0.0, from_left[0, :, at].astype(F32))
            dq = dq + lax.dot_general(ds_pre, left_k[:, wide], TN, preferred_element_type=F32)
            dq = dq + lax.dot_general(ds_own, kv_ref[0, 0, :, wide], TN, preferred_element_type=F32)
            done[0, :, at] = dq.astype(BF16)
            dk = dkv_ref[0, :, at] + jnp.where(no_right, 0.0, from_right[0, :, at].astype(F32))
            dk = dk + jnp.dot(ds_own, q_ref[0, :, wide], preferred_element_type=F32)
            done[1, :, at] = dk.astype(BF16)
            dv = dkv_ref[1, :, at] + jnp.where(no_right, 0.0, from_right[1, :, at].astype(F32))
            done[2, :, at] = dv.astype(BF16)

    @pl.when(index % 2 == 0)
    def _():
        add(got2, got1)

    @pl.when(index % 2 == 1)
    def _():
        add(got1, got2)

    lanes = slice(first, first + span)
    copies = [
        pltpu.make_async_copy(done.at[0], grad_q.at[0, :, lanes], sem.at[0]),
        pltpu.make_async_copy(done.at[1:], grad_kv.at[:, 0, :, lanes], sem.at[1]),
    ]
    for copy in copies:
        copy.start()
    for copy in copies:
        copy.wait()


def shifted(value, steps):
    count = lax.axis_size("seq")
    return lax.ppermute(value, "seq", [(i, (i + steps) % count) for i in range(count)])


def passed_up(value):
    return lax.ppermute(value, "seq", [(i, i + 1) for i in range(lax.axis_size("seq") - 1)])


def neighbour_swaps(first, second):
    count = lax.axis_size("seq")
    one = [(i, min(i ^ 1, count - 1)) for i in range(count)]
    two = [(i, ((i + 1) ^ 1) - 1) for i in range(count)]
    two = [(i, j if 0 <= j < count else i) for i, j in two]
    return lax.ppermute(first, "seq", one), lax.ppermute(second, "seq", two)


def in_hbm(value):
    return pltpu.with_memory_space_constraint(value, pltpu.HBM)


def shape(dims, dtype=BF16):
    return jax.ShapeDtypeStruct(dims, dtype)


def cost(flops, moved):
    return pl.CostEstimate(flops=int(flops), bytes_accessed=int(moved), transcendentals=0)


def chunks(hc):
    heads = hc // HEAD_DIM
    cuts = [heads * n // PARTS for n in range(PARTS + 1)]
    return [(HEAD_DIM * a, HEAD_DIM * (b - a)) for a, b in zip(cuts, cuts[1:])]


def step(query, key_value, grad_y, tags, segments, out_weight):
    _, rows, hc = query.shape
    depth = out_weight.shape[2]
    chips = lax.axis_size("dp") // 2
    count = lax.axis_size("seq")
    scale = HEAD_DIM ** (-0.5)
    blocks = 2 * depth // LANES

    other_weight = swap(out_weight, "dp", 1)
    slices = pl.pallas_call(
        grad_slices_kernel,
        in_specs=[pl.BlockSpec(memory_space=pltpu.HBM)] * 2,
        out_shape=[shape((blocks * rows + TAG_ROWS, LANES))] * chips,
        scratch_shapes=[
            pltpu.VMEM(tags.shape, tags.dtype), pltpu.SemaphoreType.DMA, pltpu.SemaphoreType.DMA((chips, blocks))],
        compiler_params=params(4),
        name="grad_slices",
        cost_estimate=cost(0, 4 * grad_y.size),
    )(in_hbm(grad_y), in_hbm(tags))
    grads = [slices[0]] + [swap(slices[k], "dp", 2 * k) for k in range(1, chips)]
    first, second, *own_vs = pl.pallas_call(
        functools.partial(side_slices_kernel, chunks(hc)),
        in_specs=[pl.BlockSpec(memory_space=pltpu.HBM)] * 2,
        out_shape=[shape((rows, hc))] * 2 + [shape((rows, width)) for _, width in chunks(hc)],
        scratch_shapes=[pltpu.SemaphoreType.DMA((2 + PARTS,))],
        compiler_params=params(8),
        name="side_slices",
        cost_estimate=cost(0, 12 * query.size),
    )(in_hbm(query), in_hbm(key_value))
    sides = neighbour_swaps(first, second)
    values = []
    for own_v in own_vs:
        values.append(passed_up(own_v))

    sums = []
    for first, span in chunks(hc):
        mine, *parts = pl.pallas_call(
            functools.partial(project_kernel, chips, first),
            out_shape=[shape((rows, span), F32)] + [shape((rows, span))] * (chips - 1),
            scratch_shapes=[pltpu.VMEM((2, 2, chips * rows, depth), BF16)],
            compiler_params=params(12),
            cost_estimate=cost(8 * chips * rows * depth * span, 8 * span * depth),
        )(*grads, out_weight, other_weight)
        sums.append([mine] + [swap(part, "dp", 2 * k) for k, part in enumerate(parts, 1)])

    small = shape((2, HEADS, rows), F32)
    own, far, left_k, right_q = pl.pallas_call(
        functools.partial(stats_kernel, count, scale),
        out_shape=[small] * 2 + [shape((rows, hc))] * 2,
        compiler_params=params(8),
        name="stats",
        cost_estimate=cost(2 * 3 * rows * rows * hc, 20 * rows * hc),
    )(query, key_value, *sides, segments)
    from_right, from_left = shifted(own, -1), shifted(far, 1)

    pieces = []
    for c, (first, span) in enumerate(chunks(hc)):
        heads = span // HEAD_DIM
        gout, delta = pl.pallas_call(
            functools.partial(delta_kernel, count, first, chips - 1, scale),
            out_shape=[shape((heads * rows + 2 * heads, HEAD_DIM)), shape((heads, rows), F32)],
            compiler_params=params(8),
            cost_estimate=cost(4 * 2 * rows * rows * span, 20 * rows * span),
        )(*sums[c], query, key_value, left_k, values[c], segments, own)
        pieces.append((gout, delta, shifted(gout, -1)))

    parts = []
    for c, (first, span) in enumerate(chunks(hc)):
        heads, half = span // HEAD_DIM, shape((2, rows, span))
        gout, delta, right_g = pieces[c]
        *kept, to1, to2 = pl.pallas_call(
            functools.partial(grads_kernel, count, first, scale),
            out_shape=[
                shape((rows, span), F32), shape((2, rows, span), F32), shape((heads, 2 * rows, rows)), half, half],
            scratch_shapes=[pltpu.VMEM((heads, rows), F32)],
            compiler_params=params(12),
            cost_estimate=cost(10 * 3 * rows * rows * span, 40 * rows * span),
        )(query, key_value, left_k, values[c], right_q, gout, right_g, segments, own, far, from_left, from_right, delta)
        parts.append((*kept, query, key_value, left_k, *neighbour_swaps(to1, to2)))

    results = ()
    anywhere = pl.BlockSpec(memory_space=pl.ANY)
    for c, (first, span) in enumerate(chunks(hc)):
        results = pl.pallas_call(
            functools.partial(finish_kernel, count, first, scale),
            in_specs=[pl.BlockSpec(memory_space=pltpu.VMEM)] * len(parts[c]) + [anywhere] * len(results),
            out_specs=[anywhere] * 2,
            out_shape=[shape(query.shape), shape(key_value.shape)],
            scratch_shapes=[pltpu.VMEM((3, rows, span), BF16), pltpu.SemaphoreType.DMA((2,))],
            input_output_aliases={len(parts[c]) + n: n for n in range(len(results))},
            compiler_params=params(12),
            cost_estimate=cost(0, 20 * rows * span),
        )(*parts[c], *results)
    return tuple(results)


def solution(mesh):
    return jax.shard_map(
        step,
        mesh=mesh,
        in_specs=(
            P("dp", "seq", None),
            P(None, "dp", "seq", None),
            P("dp", "seq", None),
            P("dp", "seq"),
            P("dp", None),
            P(None, None, "dp"),
        ),
        out_specs=(P("dp", "seq", None), P(None, "dp", "seq", None)),
        check_vma=False,
    )
```

```python
import functools
import jax
import jax.numpy as jnp
from jax import lax
from jax.experimental import pallas as pl
from jax.experimental.pallas import tpu as pltpu
from jax.sharding import PartitionSpec as P


HEADS = 16
HEAD_DIM = 128
PARTS = 2

NEG = -1e30
LANES = 128
TAG_ROWS = 16
BF16 = jnp.bfloat16
F32 = jnp.float32
NT = (((1,), (1,)), ((), ()))
TN = (((0,), (0,)), ((), ()))


def params(mib):
    return pltpu.CompilerParams(vmem_limit_bytes=mib << 20)


def lane_slice(start, size):
    return pl.ds(pl.multiple_of(start, LANES), size)


def swap(value, axis, bits):
    return lax.ppermute(value, axis, [(i, i ^ bits) for i in range(lax.axis_size(axis))])


def column_of(row):
    n = row.shape[1]
    same = lax.broadcasted_iota(jnp.int32, (n, n), 0) == lax.broadcasted_iota(jnp.int32, (n, n), 1)
    return jnp.sum(jnp.where(same, row.astype(F32), 0.0), axis=1, keepdims=True)


def grad_slices_kernel(grad_ref, tags_ref, *refs):
    outs, (tags, tag_sem, sem) = refs[:-3], refs[-3:]
    chip = lax.axis_index("dp") // 2
    rows = grad_ref.shape[1]
    blocks = (outs[0].shape[0] - TAG_ROWS) // rows
    tag_copy = pltpu.make_async_copy(tags_ref, tags, tag_sem)
    copies = [
        pltpu.make_async_copy(
            grad_ref.at[0, :, lane_slice(((chip ^ k) * blocks + n) * LANES, LANES)],
            out.at[n * rows : (n + 1) * rows],
            sem.at[k, n],
        )
        for k, out in enumerate(outs)
        for n in range(blocks)
    ]
    for copy in [tag_copy] + copies:
        copy.start()
    tag_copy.wait()
    tag = jnp.broadcast_to(tags[...].astype(F32), (TAG_ROWS, LANES)).astype(BF16)
    for out in outs:
        out[blocks * rows :] = tag
    for copy in copies:
        copy.wait()


def side_slices_kernel(cuts, q_ref, kv_ref, first, second, *refs):
    v_outs, sem = refs[:-1], refs[-1]
    v_copies = [
        pltpu.make_async_copy(kv_ref.at[1, 0, :, at : at + width], out, sem.at[2 + n])
        for n, ((at, width), out) in enumerate(zip(cuts, v_outs))
    ]

    def sides(up, down):
        copies = [
            pltpu.make_async_copy(kv_ref.at[0, 0], up, sem.at[1]),
            pltpu.make_async_copy(q_ref.at[0], down, sem.at[0]),
            *v_copies,
        ]
        for copy in copies:
            copy.start()
        for copy in copies:
            copy.wait()

    even = lax.axis_index("seq") % 2 == 0

    @pl.when(even)
    def _():
        sides(first, second)

    @pl.when(jnp.logical_not(even))
    def _():
        sides(second, first)


def project_kernel(chips, first, *refs):
    grads, (own_w, other_w), (mine, *parts, lhs) = refs[:chips], refs[chips : chips + 2], refs[chips + 2 :]
    depth = own_w.shape[2]
    blocks = depth // LANES
    rows = mine.shape[0]
    core = lax.axis_index("dp") % 2
    for k, grad in enumerate(grads):
        text = column_of(grad[2 * blocks * rows : 2 * blocks * rows + 1]) == 1.0
        for side in range(2):
            for n in range(blocks):
                at = pl.ds(pl.multiple_of(((core ^ side) * blocks + n) * rows, rows), rows)
                g = grad[at]
                where = (slice(k * rows, (k + 1) * rows), slice(n * LANES, (n + 1) * LANES))
                lhs[(side, 0, *where)] = jnp.where(text, jnp.zeros_like(g), g)
                lhs[(side, 1, *where)] = jnp.where(text, g, jnp.zeros_like(g))

    total = None
    for side, w in enumerate((own_w, other_w)):
        for kind in range(2):
            rhs = w[kind, first : first + mine.shape[1]]
            term = lax.dot_general(lhs[side, kind], rhs, NT, preferred_element_type=F32)
            total = term if total is None else total + term
    mine[...] = total[:rows]
    for k, part in enumerate(parts):
        part[...] = total[(k + 1) * rows : (k + 2) * rows].astype(BF16)


def split(values):
    high = values.astype(BF16)
    return jnp.concatenate([high, (values - high.astype(F32)).astype(BF16)], axis=0)


def joined(pieces):
    half = pieces.shape[0] // 2
    return pieces[:half].astype(F32) + pieces[half:].astype(F32)


def masks(count, segs, index, rows):
    def segment(back):
        at = jnp.clip(index + back, 0, count - 1)
        return segs[:, lane_slice(at * rows, rows)].astype(F32)

    left, own, right = segment(-1), segment(0), segment(1)
    left_at, own_at = column_of(left), column_of(own)
    no_left, no_right = index == 0, index == count - 1
    key = lax.broadcasted_iota(jnp.int32, (rows, rows), 0)
    query = lax.broadcasted_iota(jnp.int32, (rows, rows), 1)
    return (
        (left_at == own) & jnp.logical_not(no_left),
        (left_at == right) & jnp.logical_not(no_left | no_right),
        (own_at == own) & (key <= query),
        (own_at == right) & jnp.logical_not(no_right),
    )


def score(keys, queries, scale, mask):
    s = lax.dot_general(keys, queries, NT, preferred_element_type=F32) * scale
    return jnp.where(mask, s, NEG)


def pair_of(even, to_even, to_odd):
    def copy(items):
        for source, target in items:
            target[...] = source[...]

    @pl.when(even)
    def _():
        copy(to_even)

    @pl.when(jnp.logical_not(even))
    def _():
        copy(to_odd)


def stats_kernel(count, scale, q_ref, kv_ref, got1, got2, segs, own_out, far_out, left_k, right_q):
    index = lax.axis_index("seq")
    rows, hc = left_k.shape
    pair_of(index % 2 == 0, [(got2, left_k), (got1, right_q)], [(got1, left_k), (got2, right_q)])
    pre, far, own, _ = masks(count, segs, index, rows)
    for h in range(hc // HEAD_DIM):
        at = slice(h * HEAD_DIM, (h + 1) * HEAD_DIM)
        kl, q = left_k[:, at], q_ref[0, :, at]
        s_pre = score(kl, q, scale, pre)
        s_own = score(kv_ref[0, 0, :, at], q, scale, own)
        s_far = score(kl, right_q[:, at], scale, far)
        top = jnp.max(jnp.maximum(s_pre, s_own), axis=0, keepdims=True)
        own_out[0, h : h + 1] = top
        own_out[1, h : h + 1] = jnp.sum(jnp.exp(s_pre - top) + jnp.exp(s_own - top), axis=0, keepdims=True)
        top = jnp.max(s_far, axis=0, keepdims=True)
        far_out[0, h : h + 1] = top
        far_out[1, h : h + 1] = jnp.sum(jnp.exp(s_far - top), axis=0, keepdims=True)


def merged(one, two):
    top = jnp.maximum(one[0], two[0])
    first = one[1] * jnp.exp(one[0] - top)
    inverse = 1.0 / (first + two[1] * jnp.exp(two[0] - top))
    return top, inverse, first * inverse


def own_rows(index, own_stats, from_left, heads):
    no_left = index == 0
    far = (jnp.where(no_left, NEG, from_left[0, heads]), jnp.where(no_left, 0.0, from_left[1, heads]))
    return merged((own_stats[0, heads], own_stats[1, heads]), far)


def right_rows(index, count, far_stats, from_right, heads):
    no_right = index == count - 1
    own = (jnp.where(no_right, 0.0, from_right[0, heads]), jnp.where(no_right, 1.0, from_right[1, heads]))
    return merged(own, (far_stats[0, heads], far_stats[1, heads]))


def delta_kernel(count, first, terms, scale, mine, *refs):
    parts = refs[:terms]
    q_ref, kv_ref, left_k, left_v, segs, own_stats, g_out, d_out = refs[terms:]
    rows, span = mine.shape
    heads = span // HEAD_DIM
    index = lax.axis_index("seq")
    pre, _, own, _ = masks(count, segs, index, rows)
    for h in range(heads):
        at = slice(h * HEAD_DIM, (h + 1) * HEAD_DIM)
        wide = slice(first + at.start, first + at.stop)
        row = slice(h, h + 1)
        stat = first // HEAD_DIM + h
        total = mine[:, at]
        for part in parts:
            total = total + part[:, at].astype(F32)
        g_out[h * rows : (h + 1) * rows] = total.astype(BF16)
        q, g = q_ref[0, :, wide], g_out[h * rows : (h + 1) * rows]
        s_pre = score(left_k[:, wide], q, scale, pre)
        s_own = score(kv_ref[0, 0, :, wide], q, scale, own)
        d_pre = lax.dot_general(left_v[:, at], g, NT, preferred_element_type=F32)
        d_own = lax.dot_general(kv_ref[1, 0, :, wide], g, NT, preferred_element_type=F32)
        top = own_stats[0, stat : stat + 1]
        weighed = jnp.exp(s_pre - top) * d_pre + jnp.exp(s_own - top) * d_own
        d_out[row] = jnp.sum(weighed, axis=0, keepdims=True) / own_stats[1, stat : stat + 1]
    g_out[heads * rows :] = split(d_out[...])


def grads_kernel(count, first, scale, q_ref, kv_ref, left_k, left_v, right_q, g_ref, right_g, segs,
                 own_stats, far_stats, from_left, from_right, delta_own,
                 dq_out, dkv_out, p_out, to1, to2, far_delta):
    index = lax.axis_index("seq")
    rows, span = left_v.shape
    heads = span // HEAD_DIM
    chosen = slice(first // HEAD_DIM, first // HEAD_DIM + heads)
    pre, far, own, nxt = masks(count, segs, index, rows)
    top, inv, share = own_rows(index, own_stats, from_left, chosen)
    r_top, r_inv, r_share = right_rows(index, count, far_stats, from_right, chosen)
    own_delta = delta_own[...] * share
    right_delta = joined(right_g[heads * rows :]) * r_share

    def run(up_out, down_out):
        for h in range(heads):
            at = slice(h * HEAD_DIM, (h + 1) * HEAD_DIM)
            wide = slice(first + at.start, first + at.stop)
            row = slice(h, h + 1)
            q2 = jnp.concatenate([q_ref[0, :, wide], right_q[:, wide]], axis=0)
            block = slice(h * rows, (h + 1) * rows)
            g2 = jnp.concatenate([g_ref[block], right_g[block]], axis=0)
            k, kl = kv_ref[0, 0, :, wide], left_k[:, wide]
            s_left = lax.dot_general(kl, q2, NT, preferred_element_type=F32) * scale
            s_here = lax.dot_general(k, q2, NT, preferred_element_type=F32) * scale
            d_left = lax.dot_general(left_v[:, at], g2, NT, preferred_element_type=F32)
            d_own = lax.dot_general(kv_ref[1, 0, :, wide], g2[:rows], NT, preferred_element_type=F32)
            p_pre = jnp.exp(jnp.where(pre, s_left[:, :rows], NEG) - top[row]) * inv[row]
            p_own = jnp.exp(jnp.where(own, s_here[:, :rows], NEG) - top[row]) * inv[row]
            p_far = jnp.exp(jnp.where(far, s_left[:, rows:], NEG) - r_top[row]) * r_inv[row]
            p_nxt = jnp.exp(jnp.where(nxt, s_here[:, rows:], NEG) - r_top[row]) * r_inv[row]
            d_pre, d_far = d_left[:, :rows], d_left[:, rows:]
            extra = jnp.sum(p_far * d_far, axis=0, keepdims=True)
            far_delta[row] = extra
            ds_pre = (p_pre * (d_pre - own_delta[row]) * scale).astype(BF16)
            ds_own = (p_own * (d_own - own_delta[row]) * scale).astype(BF16)
            ds_far = (p_far * (d_far - (right_delta[row] + extra)) * scale).astype(BF16)
            ds_nxt = (p_nxt * (extra * -scale)).astype(BF16)
            p_low = p_pre.astype(BF16)
            p_here = p_own.astype(BF16)
            p_out[h, :rows] = p_low
            p_out[h, rows:] = p_here
            dkv_out[0, :, at] = jnp.dot(
                jnp.concatenate([ds_own, ds_nxt], axis=1), q2, preferred_element_type=F32)
            dkv_out[1, :, at] = jnp.dot(p_here, g2[:rows], preferred_element_type=F32)
            down_out[0, :, at] = jnp.dot(
                jnp.concatenate([ds_pre, ds_far], axis=1), q2, preferred_element_type=F32).astype(BF16)
            down_out[1, :, at] = jnp.dot(
                jnp.concatenate([p_low, p_far.astype(BF16)], axis=1), g2, preferred_element_type=F32).astype(BF16)
            dq_out[:, at] = lax.dot_general(ds_pre, kl, TN, preferred_element_type=F32) + lax.dot_general(
                ds_own, k, TN, preferred_element_type=F32)
            up_out[0, :, at] = lax.dot_general(ds_far, kl, TN, preferred_element_type=F32).astype(BF16)
        up_out[1, : 2 * heads, :LANES] = split(far_delta[...])

    @pl.when(index % 2 == 0)
    def _():
        run(to1, to2)

    @pl.when(index % 2 == 1)
    def _():
        run(to2, to1)


def finish_kernel(count, first, scale, dq_ref, dkv_ref, p_ref, q_ref, kv_ref, left_k, got1, got2, *refs):
    grad_q, grad_kv, done, sem = refs[-4:]
    index = lax.axis_index("seq")
    rows, span = dq_ref.shape
    heads = span // HEAD_DIM

    lanes = slice(first, first + span)
    copies = [
        pltpu.make_async_copy(done.at[0], grad_q.at[0, :, lanes], sem.at[0]),
        pltpu.make_async_copy(done.at[1], grad_kv.at[0, 0, :, lanes], sem.at[1]),
        pltpu.make_async_copy(done.at[2], grad_kv.at[1, 0, :, lanes], sem.at[2]),
    ]

    def add(from_left, from_right):
        no_left, no_right = index == 0, index == count - 1
        done[2] = (dkv_ref[1] + jnp.where(no_right, 0.0, from_right[1].astype(F32))).astype(BF16)
        copies[2].start()
        delta = jnp.where(no_left, 0.0, joined(from_left[1, : 2 * heads, :LANES]))
        for h in range(heads):
            at = slice(h * HEAD_DIM, (h + 1) * HEAD_DIM)
            wide = slice(first + at.start, first + at.stop)
            factor = delta[h : h + 1] * -scale
            ds_pre = (p_ref[h, :rows].astype(F32) * factor).astype(BF16)
            ds_own = (p_ref[h, rows:].astype(F32) * factor).astype(BF16)
            dq = dq_ref[:, at] + jnp.where(no_left, 0.0, from_left[0, :, at].astype(F32))
            dq = dq + lax.dot_general(ds_pre, left_k[:, wide], TN, preferred_element_type=F32)
            dq = dq + lax.dot_general(ds_own, kv_ref[0, 0, :, wide], TN, preferred_element_type=F32)
            done[0, :, at] = dq.astype(BF16)
            dk = dkv_ref[0, :, at] + jnp.where(no_right, 0.0, from_right[0, :, at].astype(F32))
            dk = dk + jnp.dot(ds_own, q_ref[0, :, wide], preferred_element_type=F32)
            done[1, :, at] = dk.astype(BF16)

    @pl.when(index % 2 == 0)
    def _():
        add(got2, got1)

    @pl.when(index % 2 == 1)
    def _():
        add(got1, got2)

    for copy in copies[:2]:
        copy.start()
    for copy in copies:
        copy.wait()


def passed(value, steps):
    count = lax.axis_size("seq")
    first, last = max(0, -steps), min(count, count - steps)
    return lax.ppermute(value, "seq", [(i, i + steps) for i in range(first, last)])


def neighbour_swaps(first, second):
    count = lax.axis_size("seq")
    one = [(i, min(i ^ 1, count - 1)) for i in range(count)]
    two = [(i, ((i + 1) ^ 1) - 1) for i in range(count)]
    two = [(i, j if 0 <= j < count else i) for i, j in two]
    return lax.ppermute(first, "seq", one), lax.ppermute(second, "seq", two)


def in_hbm(value):
    return pltpu.with_memory_space_constraint(value, pltpu.HBM)


def shape(dims, dtype=BF16):
    return jax.ShapeDtypeStruct(dims, dtype)


def cost(flops, moved):
    return pl.CostEstimate(flops=int(flops), bytes_accessed=int(moved), transcendentals=0)


def chunks(hc):
    heads = hc // HEAD_DIM
    cuts = [heads * n // PARTS for n in range(PARTS + 1)]
    return [(HEAD_DIM * a, HEAD_DIM * (b - a)) for a, b in zip(cuts, cuts[1:])]


def step(query, key_value, grad_y, tags, segments, out_weight):
    _, rows, hc = query.shape
    depth = out_weight.shape[2]
    chips = lax.axis_size("dp") // 2
    count = lax.axis_size("seq")
    scale = HEAD_DIM ** (-0.5)
    blocks = 2 * depth // LANES

    other_weight = swap(out_weight, "dp", 1)
    slices = pl.pallas_call(
        grad_slices_kernel,
        in_specs=[pl.BlockSpec(memory_space=pltpu.HBM)] * 2,
        out_shape=[shape((blocks * rows + TAG_ROWS, LANES))] * chips,
        scratch_shapes=[
            pltpu.VMEM(tags.shape, tags.dtype), pltpu.SemaphoreType.DMA, pltpu.SemaphoreType.DMA((chips, blocks))],
        compiler_params=params(4),
        name="grad_slices",
        cost_estimate=cost(0, 4 * grad_y.size),
    )(in_hbm(grad_y), in_hbm(tags))
    grads = [slices[0]] + [swap(slices[k], "dp", 2 * k) for k in range(1, chips)]
    first, second, *own_vs = pl.pallas_call(
        functools.partial(side_slices_kernel, chunks(hc)),
        in_specs=[pl.BlockSpec(memory_space=pltpu.HBM)] * 2,
        out_shape=[shape((rows, hc))] * 2 + [shape((rows, width)) for _, width in chunks(hc)],
        scratch_shapes=[pltpu.SemaphoreType.DMA((2 + PARTS,))],
        compiler_params=params(8),
        name="side_slices",
        cost_estimate=cost(0, 12 * query.size),
    )(in_hbm(query), in_hbm(key_value))
    sides = neighbour_swaps(first, second)
    values = []
    for own_v in own_vs:
        values.append(passed(own_v, 1))

    sums = []
    for first, span in chunks(hc):
        mine, *parts = pl.pallas_call(
            functools.partial(project_kernel, chips, first),
            out_shape=[shape((rows, span), F32)] + [shape((rows, span))] * (chips - 1),
            scratch_shapes=[pltpu.VMEM((2, 2, chips * rows, depth), BF16)],
            compiler_params=params(12),
            cost_estimate=cost(8 * chips * rows * depth * span, 8 * span * depth),
        )(*grads, out_weight, other_weight)
        sums.append([mine] + [swap(part, "dp", 2 * k) for k, part in enumerate(parts, 1)])

    small = shape((2, HEADS, rows), F32)
    own, far, left_k, right_q = pl.pallas_call(
        functools.partial(stats_kernel, count, scale),
        out_shape=[small] * 2 + [shape((rows, hc))] * 2,
        compiler_params=params(8),
        name="stats",
        cost_estimate=cost(2 * 3 * rows * rows * hc, 20 * rows * hc),
    )(query, key_value, *sides, segments)
    from_right, from_left = passed(own, -1), passed(far, 1)

    pieces = []
    for c, (first, span) in enumerate(chunks(hc)):
        heads = span // HEAD_DIM
        gout, delta = pl.pallas_call(
            functools.partial(delta_kernel, count, first, chips - 1, scale),
            out_shape=[shape((heads * rows + 2 * heads, HEAD_DIM)), shape((heads, rows), F32)],
            compiler_params=params(8),
            cost_estimate=cost(4 * 2 * rows * rows * span, 20 * rows * span),
        )(*sums[c], query, key_value, left_k, values[c], segments, own)
        pieces.append((gout, delta, passed(gout, -1)))

    parts = []
    for c, (first, span) in enumerate(chunks(hc)):
        heads, half = span // HEAD_DIM, shape((2, rows, span))
        gout, delta, right_g = pieces[c]
        *kept, to1, to2 = pl.pallas_call(
            functools.partial(grads_kernel, count, first, scale),
            out_shape=[
                shape((rows, span), F32), shape((2, rows, span), F32), shape((heads, 2 * rows, rows)), half, half],
            scratch_shapes=[pltpu.VMEM((heads, rows), F32)],
            compiler_params=params(12),
            cost_estimate=cost(10 * 3 * rows * rows * span, 40 * rows * span),
        )(query, key_value, left_k, values[c], right_q, gout, right_g, segments, own, far, from_left, from_right, delta)
        parts.append((*kept, query, key_value, left_k, *neighbour_swaps(to1, to2)))

    results = ()
    anywhere = pl.BlockSpec(memory_space=pl.ANY)
    for c, (first, span) in enumerate(chunks(hc)):
        results = pl.pallas_call(
            functools.partial(finish_kernel, count, first, scale),
            in_specs=[pl.BlockSpec(memory_space=pltpu.VMEM)] * len(parts[c]) + [anywhere] * len(results),
            out_specs=[anywhere] * 2,
            out_shape=[shape(query.shape), shape(key_value.shape)],
            scratch_shapes=[pltpu.VMEM((3, rows, span), BF16), pltpu.SemaphoreType.DMA((3,))],
            input_output_aliases={len(parts[c]) + n: n for n in range(len(results))},
            compiler_params=params(12),
            cost_estimate=cost(0, 20 * rows * span),
        )(*parts[c], *results)
    return tuple(results)


def solution(mesh):
    return jax.shard_map(
        step,
        mesh=mesh,
        in_specs=(
            P("dp", "seq", None),
            P(None, "dp", "seq", None),
            P("dp", "seq", None),
            P("dp", "seq"),
            P("dp", None),
            P(None, None, "dp"),
        ),
        out_specs=(P("dp", "seq", None), P(None, "dp", "seq", None)),
        check_vma=False,
    )
```

```python
import functools
import jax
import jax.numpy as jnp
from jax import lax
from jax.experimental import pallas as pl
from jax.experimental.pallas import tpu as pltpu
from jax.sharding import PartitionSpec as P


HEADS = 16
HEAD_DIM = 128
PARTS = 2

NEG = -1e30
LANES = 128
TAG_ROWS = 16
BF16 = jnp.bfloat16
F32 = jnp.float32
NT = (((1,), (1,)), ((), ()))
TN = (((0,), (0,)), ((), ()))


def params(mib):
    return pltpu.CompilerParams(vmem_limit_bytes=mib << 20)


def lane_slice(start, size):
    return pl.ds(pl.multiple_of(start, LANES), size)


def swap(value, axis, bits):
    return lax.ppermute(value, axis, [(i, i ^ bits) for i in range(lax.axis_size(axis))])


def column_of(row):
    n = row.shape[1]
    same = lax.broadcasted_iota(jnp.int32, (n, n), 0) == lax.broadcasted_iota(jnp.int32, (n, n), 1)
    return jnp.sum(jnp.where(same, row.astype(F32), 0.0), axis=1, keepdims=True)


def grad_slices_kernel(grad_ref, tags_ref, *refs):
    outs, (tags, tag_sem, sem) = refs[:-3], refs[-3:]
    chip = lax.axis_index("dp") // 2
    rows = grad_ref.shape[1]
    blocks = (outs[0].shape[0] - TAG_ROWS) // rows
    tag_copy = pltpu.make_async_copy(tags_ref, tags, tag_sem)
    copies = [
        pltpu.make_async_copy(
            grad_ref.at[0, :, lane_slice(((chip ^ k) * blocks + n) * LANES, LANES)],
            out.at[n * rows : (n + 1) * rows],
            sem.at[k, n],
        )
        for k, out in enumerate(outs)
        for n in range(blocks)
    ]
    for copy in [tag_copy] + copies:
        copy.start()
    tag_copy.wait()
    tag = jnp.broadcast_to(tags[...].astype(F32), (TAG_ROWS, LANES)).astype(BF16)
    for out in outs:
        out[blocks * rows :] = tag
    for copy in copies:
        copy.wait()


def side_slices_kernel(cuts, q_ref, kv_ref, first, second, *refs):
    v_outs, sem = refs[:-1], refs[-1]
    v_copies = [
        pltpu.make_async_copy(kv_ref.at[1, 0, :, at : at + width], out, sem.at[2 + n])
        for n, ((at, width), out) in enumerate(zip(cuts, v_outs))
    ]

    def sides(up, down):
        copies = [
            pltpu.make_async_copy(kv_ref.at[0, 0], up, sem.at[1]),
            pltpu.make_async_copy(q_ref.at[0], down, sem.at[0]),
            *v_copies,
        ]
        for copy in copies:
            copy.start()
        for copy in copies:
            copy.wait()

    even = lax.axis_index("seq") % 2 == 0

    @pl.when(even)
    def _():
        sides(first, second)

    @pl.when(jnp.logical_not(even))
    def _():
        sides(second, first)


def project_kernel(chips, first, *refs):
    grads, (own_w, other_w), (mine, *parts, lhs) = refs[:chips], refs[chips : chips + 2], refs[chips + 2 :]
    depth = own_w.shape[2]
    blocks = depth // LANES
    rows = mine.shape[0]
    core = lax.axis_index("dp") % 2
    for k, grad in enumerate(grads):
        text = column_of(grad[2 * blocks * rows : 2 * blocks * rows + 1]) == 1.0
        for side in range(2):
            for n in range(blocks):
                at = pl.ds(pl.multiple_of(((core ^ side) * blocks + n) * rows, rows), rows)
                g = grad[at]
                where = (slice(k * rows, (k + 1) * rows), slice(n * LANES, (n + 1) * LANES))
                lhs[(side, 0, *where)] = jnp.where(text, jnp.zeros_like(g), g)
                lhs[(side, 1, *where)] = jnp.where(text, g, jnp.zeros_like(g))

    total = None
    for side, w in enumerate((own_w, other_w)):
        for kind in range(2):
            rhs = w[kind, first : first + mine.shape[1]]
            term = lax.dot_general(lhs[side, kind], rhs, NT, preferred_element_type=F32)
            total = term if total is None else total + term
    mine[...] = total[:rows]
    for k, part in enumerate(parts):
        part[...] = total[(k + 1) * rows : (k + 2) * rows].astype(BF16)


def split(values):
    high = values.astype(BF16)
    return jnp.concatenate([high, (values - high.astype(F32)).astype(BF16)], axis=0)


def joined(pieces):
    half = pieces.shape[0] // 2
    return pieces[:half].astype(F32) + pieces[half:].astype(F32)


def masks(count, segs, index, rows):
    def segment(back):
        at = jnp.clip(index + back, 0, count - 1)
        return segs[:, lane_slice(at * rows, rows)].astype(F32)

    left, own, right = segment(-1), segment(0), segment(1)
    left_at, own_at = column_of(left), column_of(own)
    no_left, no_right = index == 0, index == count - 1
    key = lax.broadcasted_iota(jnp.int32, (rows, rows), 0)
    query = lax.broadcasted_iota(jnp.int32, (rows, rows), 1)
    return (
        (left_at == own) & jnp.logical_not(no_left),
        (left_at == right) & jnp.logical_not(no_left | no_right),
        (own_at == own) & (key <= query),
        (own_at == right) & jnp.logical_not(no_right),
    )


def score(keys, queries, scale, mask):
    s = lax.dot_general(keys, queries, NT, preferred_element_type=F32) * scale
    return jnp.where(mask, s, NEG)


def pair_of(even, to_even, to_odd):
    def copy(items):
        for source, target in items:
            target[...] = source[...]

    @pl.when(even)
    def _():
        copy(to_even)

    @pl.when(jnp.logical_not(even))
    def _():
        copy(to_odd)


def stats_kernel(count, scale, q_ref, kv_ref, got1, got2, segs, own_out, far_out, left_k, right_q):
    index = lax.axis_index("seq")
    rows, hc = left_k.shape
    pair_of(index % 2 == 0, [(got2, left_k), (got1, right_q)], [(got1, left_k), (got2, right_q)])
    pre, far, own, _ = masks(count, segs, index, rows)
    for h in range(hc // HEAD_DIM):
        at = slice(h * HEAD_DIM, (h + 1) * HEAD_DIM)
        kl, q = left_k[:, at], q_ref[0, :, at]
        s_pre = score(kl, q, scale, pre)
        s_own = score(kv_ref[0, 0, :, at], q, scale, own)
        s_far = score(kl, right_q[:, at], scale, far)
        top = jnp.max(jnp.maximum(s_pre, s_own), axis=0, keepdims=True)
        own_out[0, h : h + 1] = top
        own_out[1, h : h + 1] = jnp.sum(jnp.exp(s_pre - top) + jnp.exp(s_own - top), axis=0, keepdims=True)
        top = jnp.max(s_far, axis=0, keepdims=True)
        far_out[0, h : h + 1] = top
        far_out[1, h : h + 1] = jnp.sum(jnp.exp(s_far - top), axis=0, keepdims=True)


def merged(one, two):
    top = jnp.maximum(one[0], two[0])
    first = one[1] * jnp.exp(one[0] - top)
    inverse = 1.0 / (first + two[1] * jnp.exp(two[0] - top))
    return top, inverse, first * inverse


def own_rows(index, own_stats, from_left, heads):
    no_left = index == 0
    far = (jnp.where(no_left, NEG, from_left[0, heads]), jnp.where(no_left, 0.0, from_left[1, heads]))
    return merged((own_stats[0, heads], own_stats[1, heads]), far)


def right_rows(index, count, far_stats, from_right, heads):
    no_right = index == count - 1
    own = (jnp.where(no_right, 0.0, from_right[0, heads]), jnp.where(no_right, 1.0, from_right[1, heads]))
    return merged(own, (far_stats[0, heads], far_stats[1, heads]))


def delta_kernel(count, first, terms, scale, mine, *refs):
    parts = refs[:terms]
    q_ref, kv_ref, left_k, left_v, segs, own_stats, g_out, d_out = refs[terms:]
    rows, span = mine.shape
    heads = span // HEAD_DIM
    index = lax.axis_index("seq")
    pre, _, own, _ = masks(count, segs, index, rows)
    for h in range(heads):
        at = slice(h * HEAD_DIM, (h + 1) * HEAD_DIM)
        wide = slice(first + at.start, first + at.stop)
        row = slice(h, h + 1)
        stat = first // HEAD_DIM + h
        total = mine[:, at]
        for part in parts:
            total = total + part[:, at].astype(F32)
        g_out[h * rows : (h + 1) * rows] = total.astype(BF16)
        q, g = q_ref[0, :, wide], g_out[h * rows : (h + 1) * rows]
        s_pre = score(left_k[:, wide], q, scale, pre)
        s_own = score(kv_ref[0, 0, :, wide], q, scale, own)
        d_pre = lax.dot_general(left_v[:, at], g, NT, preferred_element_type=F32)
        d_own = lax.dot_general(kv_ref[1, 0, :, wide], g, NT, preferred_element_type=F32)
        top = own_stats[0, stat : stat + 1]
        weighed = jnp.exp(s_pre - top) * d_pre + jnp.exp(s_own - top) * d_own
        d_out[row] = jnp.sum(weighed, axis=0, keepdims=True) / own_stats[1, stat : stat + 1]
    g_out[heads * rows :] = split(d_out[...])


def left_kernel(count, first, scale, q_ref, left_k, left_v, right_q, g_ref, right_g, segs,
                own_stats, far_stats, from_left, from_right, delta_own,
                p_out, ds_out, far_delta, to1, to2):
    index = lax.axis_index("seq")
    rows, span = left_v.shape
    heads = span // HEAD_DIM
    chosen = slice(first // HEAD_DIM, first // HEAD_DIM + heads)
    pre, far, _, _ = masks(count, segs, index, rows)
    top, inv, share = own_rows(index, own_stats, from_left, chosen)
    r_top, r_inv, r_share = right_rows(index, count, far_stats, from_right, chosen)
    own_delta = delta_own[...] * share
    right_delta = joined(right_g[heads * rows :]) * r_share

    def run(up_out, down_out):
        for h in range(heads):
            at = slice(h * HEAD_DIM, (h + 1) * HEAD_DIM)
            wide = slice(first + at.start, first + at.stop)
            block = slice(h * rows, (h + 1) * rows)
            row = slice(h, h + 1)
            q2 = jnp.concatenate([q_ref[0, :, wide], right_q[:, wide]], axis=0)
            g2 = jnp.concatenate([g_ref[block], right_g[block]], axis=0)
            kl = left_k[:, wide]
            s_left = lax.dot_general(kl, q2, NT, preferred_element_type=F32) * scale
            d_left = lax.dot_general(left_v[:, at], g2, NT, preferred_element_type=F32)
            p_pre = jnp.exp(jnp.where(pre, s_left[:, :rows], NEG) - top[row]) * inv[row]
            p_far = jnp.exp(jnp.where(far, s_left[:, rows:], NEG) - r_top[row]) * r_inv[row]
            d_pre, d_far = d_left[:, :rows], d_left[:, rows:]
            extra = jnp.sum(p_far * d_far, axis=0, keepdims=True)
            far_delta[row] = extra
            ds_pre = (p_pre * (d_pre - own_delta[row]) * scale).astype(BF16)
            ds_far = (p_far * (d_far - (right_delta[row] + extra)) * scale).astype(BF16)
            p_low = p_pre.astype(BF16)
            p_out[h] = p_low
            ds_out[h] = ds_pre
            down_out[0, :, at] = jnp.dot(
                jnp.concatenate([ds_pre, ds_far], axis=1), q2, preferred_element_type=F32).astype(BF16)
            down_out[1, :, at] = jnp.dot(
                jnp.concatenate([p_low, p_far.astype(BF16)], axis=1), g2, preferred_element_type=F32).astype(BF16)
            up_out[0, :, at] = lax.dot_general(ds_far, kl, TN, preferred_element_type=F32).astype(BF16)
        up_out[1, : 2 * heads, :LANES] = split(far_delta[...])

    @pl.when(index % 2 == 0)
    def _():
        run(to1, to2)

    @pl.when(index % 2 == 1)
    def _():
        run(to2, to1)


def own_kernel(count, first, scale, q_ref, kv_ref, left_k, right_q, g_ref, segs,
               own_stats, far_stats, from_left, from_right, delta_own, ds_left, far_delta,
               dq_out, dkv_out, p_out):
    index = lax.axis_index("seq")
    rows, span = dq_out.shape
    heads = span // HEAD_DIM
    chosen = slice(first // HEAD_DIM, first // HEAD_DIM + heads)
    _, _, own, nxt = masks(count, segs, index, rows)
    top, inv, share = own_rows(index, own_stats, from_left, chosen)
    r_top, r_inv, _ = right_rows(index, count, far_stats, from_right, chosen)
    own_delta = delta_own[...] * share
    for h in range(heads):
        at = slice(h * HEAD_DIM, (h + 1) * HEAD_DIM)
        wide = slice(first + at.start, first + at.stop)
        row = slice(h, h + 1)
        q2 = jnp.concatenate([q_ref[0, :, wide], right_q[:, wide]], axis=0)
        g, k = g_ref[h * rows : (h + 1) * rows], kv_ref[0, 0, :, wide]
        s_here = lax.dot_general(k, q2, NT, preferred_element_type=F32) * scale
        d_own = lax.dot_general(kv_ref[1, 0, :, wide], g, NT, preferred_element_type=F32)
        p_own = jnp.exp(jnp.where(own, s_here[:, :rows], NEG) - top[row]) * inv[row]
        p_nxt = jnp.exp(jnp.where(nxt, s_here[:, rows:], NEG) - r_top[row]) * r_inv[row]
        ds_own = (p_own * (d_own - own_delta[row]) * scale).astype(BF16)
        ds_nxt = (p_nxt * (far_delta[row] * -scale)).astype(BF16)
        p_low = p_own.astype(BF16)
        p_out[h] = p_low
        dkv_out[0, :, at] = jnp.dot(jnp.concatenate([ds_own, ds_nxt], axis=1), q2, preferred_element_type=F32)
        dkv_out[1, :, at] = jnp.dot(p_low, g, preferred_element_type=F32)
        dq_out[:, at] = lax.dot_general(ds_left[h], left_k[:, wide], TN, preferred_element_type=F32) + lax.dot_general(
            ds_own, k, TN, preferred_element_type=F32)


def finish_kernel(count, first, scale, dq_ref, dkv_ref, p_own, p_left, q_ref, kv_ref, left_k, got1, got2, *refs):
    grad_q, grad_kv, done, sem = refs[-4:]
    index = lax.axis_index("seq")
    _, span = dq_ref.shape
    heads = span // HEAD_DIM

    lanes = slice(first, first + span)
    copies = [
        pltpu.make_async_copy(done.at[0], grad_q.at[0, :, lanes], sem.at[0]),
        pltpu.make_async_copy(done.at[1], grad_kv.at[0, 0, :, lanes], sem.at[1]),
        pltpu.make_async_copy(done.at[2], grad_kv.at[1, 0, :, lanes], sem.at[2]),
    ]

    def add(from_left, from_right):
        no_left, no_right = index == 0, index == count - 1
        done[2] = (dkv_ref[1] + jnp.where(no_right, 0.0, from_right[1].astype(F32))).astype(BF16)
        copies[2].start()
        delta = jnp.where(no_left, 0.0, joined(from_left[1, : 2 * heads, :LANES]))
        for h in range(heads):
            at = slice(h * HEAD_DIM, (h + 1) * HEAD_DIM)
            wide = slice(first + at.start, first + at.stop)
            factor = delta[h : h + 1] * -scale
            ds_pre = (p_left[h].astype(F32) * factor).astype(BF16)
            ds_own = (p_own[h].astype(F32) * factor).astype(BF16)
            dq = dq_ref[:, at] + jnp.where(no_left, 0.0, from_left[0, :, at].astype(F32))
            dq = dq + lax.dot_general(ds_pre, left_k[:, wide], TN, preferred_element_type=F32)
            dq = dq + lax.dot_general(ds_own, kv_ref[0, 0, :, wide], TN, preferred_element_type=F32)
            done[0, :, at] = dq.astype(BF16)
            dk = dkv_ref[0, :, at] + jnp.where(no_right, 0.0, from_right[0, :, at].astype(F32))
            dk = dk + jnp.dot(ds_own, q_ref[0, :, wide], preferred_element_type=F32)
            done[1, :, at] = dk.astype(BF16)

    @pl.when(index % 2 == 0)
    def _():
        add(got2, got1)

    @pl.when(index % 2 == 1)
    def _():
        add(got1, got2)

    for copy in copies[:2]:
        copy.start()
    for copy in copies:
        copy.wait()


def passed(value, steps):
    count = lax.axis_size("seq")
    first, last = max(0, -steps), min(count, count - steps)
    return lax.ppermute(value, "seq", [(i, i + steps) for i in range(first, last)])


def neighbour_swaps(first, second):
    count = lax.axis_size("seq")
    one = [(i, min(i ^ 1, count - 1)) for i in range(count)]
    two = [(i, ((i + 1) ^ 1) - 1) for i in range(count)]
    two = [(i, j if 0 <= j < count else i) for i, j in two]
    return lax.ppermute(first, "seq", one), lax.ppermute(second, "seq", two)


def in_hbm(value):
    return pltpu.with_memory_space_constraint(value, pltpu.HBM)


def shape(dims, dtype=BF16):
    return jax.ShapeDtypeStruct(dims, dtype)


def cost(flops, moved):
    return pl.CostEstimate(flops=int(flops), bytes_accessed=int(moved), transcendentals=0)


def chunks(hc):
    heads = hc // HEAD_DIM
    cuts = [heads * n // PARTS for n in range(PARTS + 1)]
    return [(HEAD_DIM * a, HEAD_DIM * (b - a)) for a, b in zip(cuts, cuts[1:])]


def step(query, key_value, grad_y, tags, segments, out_weight):
    _, rows, hc = query.shape
    depth = out_weight.shape[2]
    chips = lax.axis_size("dp") // 2
    count = lax.axis_size("seq")
    scale = HEAD_DIM ** (-0.5)
    blocks = 2 * depth // LANES

    other_weight = swap(out_weight, "dp", 1)
    slices = pl.pallas_call(
        grad_slices_kernel,
        in_specs=[pl.BlockSpec(memory_space=pltpu.HBM)] * 2,
        out_shape=[shape((blocks * rows + TAG_ROWS, LANES))] * chips,
        scratch_shapes=[
            pltpu.VMEM(tags.shape, tags.dtype), pltpu.SemaphoreType.DMA, pltpu.SemaphoreType.DMA((chips, blocks))],
        compiler_params=params(4),
        name="grad_slices",
        cost_estimate=cost(0, 4 * grad_y.size),
    )(in_hbm(grad_y), in_hbm(tags))
    grads = [slices[0]] + [swap(slices[k], "dp", 2 * k) for k in range(1, chips)]
    first, second, *own_vs = pl.pallas_call(
        functools.partial(side_slices_kernel, chunks(hc)),
        in_specs=[pl.BlockSpec(memory_space=pltpu.HBM)] * 2,
        out_shape=[shape((rows, hc))] * 2 + [shape((rows, width)) for _, width in chunks(hc)],
        scratch_shapes=[pltpu.SemaphoreType.DMA((2 + PARTS,))],
        compiler_params=params(8),
        name="side_slices",
        cost_estimate=cost(0, 12 * query.size),
    )(in_hbm(query), in_hbm(key_value))
    sides = neighbour_swaps(first, second)
    values = []
    for own_v in own_vs:
        values.append(passed(own_v, 1))

    sums = []
    for first, span in chunks(hc):
        mine, *parts = pl.pallas_call(
            functools.partial(project_kernel, chips, first),
            out_shape=[shape((rows, span), F32)] + [shape((rows, span))] * (chips - 1),
            scratch_shapes=[pltpu.VMEM((2, 2, chips * rows, depth), BF16)],
            compiler_params=params(12),
            cost_estimate=cost(8 * chips * rows * depth * span, 8 * span * depth),
        )(*grads, out_weight, other_weight)
        sums.append([mine] + [swap(part, "dp", 2 * k) for k, part in enumerate(parts, 1)])

    small = shape((2, HEADS, rows), F32)
    own, far, left_k, right_q = pl.pallas_call(
        functools.partial(stats_kernel, count, scale),
        out_shape=[small] * 2 + [shape((rows, hc))] * 2,
        compiler_params=params(8),
        name="stats",
        cost_estimate=cost(2 * 3 * rows * rows * hc, 20 * rows * hc),
    )(query, key_value, *sides, segments)
    from_right, from_left = passed(own, -1), passed(far, 1)

    pieces = []
    for c, (first, span) in enumerate(chunks(hc)):
        heads = span // HEAD_DIM
        gout, delta = pl.pallas_call(
            functools.partial(delta_kernel, count, first, chips - 1, scale),
            out_shape=[shape((heads * rows + 2 * heads, HEAD_DIM)), shape((heads, rows), F32)],
            compiler_params=params(8),
            cost_estimate=cost(4 * 2 * rows * rows * span, 20 * rows * span),
        )(*sums[c], query, key_value, left_k, values[c], segments, own)
        pieces.append((gout, delta, passed(gout, -1)))

    parts = []
    for c, (first, span) in enumerate(chunks(hc)):
        heads, half = span // HEAD_DIM, shape((2, rows, span))
        gout, delta, right_g = pieces[c]
        square, table = shape((heads, rows, rows)), (own, far, from_left, from_right, delta)
        p_left, ds_left, far_delta, to1, to2 = pl.pallas_call(
            functools.partial(left_kernel, count, first, scale),
            out_shape=[square, square, shape((heads, rows), F32), half, half],
            compiler_params=params(12),
            cost_estimate=cost(10 * 2 * rows * rows * span, 30 * rows * span),
        )(query, left_k, values[c], right_q, gout, right_g, segments, *table)
        got = neighbour_swaps(to1, to2)
        kept = pl.pallas_call(
            functools.partial(own_kernel, count, first, scale),
            out_shape=[shape((rows, span), F32), shape((2, rows, span), F32), square],
            compiler_params=params(12),
            cost_estimate=cost(10 * 2 * rows * rows * span, 30 * rows * span),
        )(query, key_value, left_k, right_q, gout, segments, *table, ds_left, far_delta)
        parts.append((*kept, p_left, query, key_value, left_k, *got))

    results = ()
    anywhere = pl.BlockSpec(memory_space=pl.ANY)
    for c, (first, span) in enumerate(chunks(hc)):
        results = pl.pallas_call(
            functools.partial(finish_kernel, count, first, scale),
            in_specs=[pl.BlockSpec(memory_space=pltpu.VMEM)] * len(parts[c]) + [anywhere] * len(results),
            out_specs=[anywhere] * 2,
            out_shape=[shape(query.shape), shape(key_value.shape)],
            scratch_shapes=[pltpu.VMEM((3, rows, span), BF16), pltpu.SemaphoreType.DMA((3,))],
            input_output_aliases={len(parts[c]) + n: n for n in range(len(results))},
            compiler_params=params(12),
            cost_estimate=cost(0, 20 * rows * span),
        )(*parts[c], *results)
    return tuple(results)


def solution(mesh):
    return jax.shard_map(
        step,
        mesh=mesh,
        in_specs=(
            P("dp", "seq", None),
            P(None, "dp", "seq", None),
            P("dp", "seq", None),
            P("dp", "seq"),
            P("dp", None),
            P(None, None, "dp"),
        ),
        out_specs=(P("dp", "seq", None), P(None, "dp", "seq", None)),
        check_vma=False,
    )
```

```python
import functools
import jax
import jax.numpy as jnp
from jax import lax
from jax.experimental import pallas as pl
from jax.experimental.pallas import tpu as pltpu
from jax.sharding import PartitionSpec as P


HEADS = 16
HEAD_DIM = 128
PARTS = 2

NEG = -1e30
LANES = 128
TAG_ROWS = 16
BF16 = jnp.bfloat16
F32 = jnp.float32
NT = (((1,), (1,)), ((), ()))
TN = (((0,), (0,)), ((), ()))


def params(mib):
    return pltpu.CompilerParams(vmem_limit_bytes=mib << 20)


def lane_slice(start, size):
    return pl.ds(pl.multiple_of(start, LANES), size)


def swap(value, axis, bits):
    return lax.ppermute(value, axis, [(i, i ^ bits) for i in range(lax.axis_size(axis))])


def column_of(row):
    n = row.shape[1]
    same = lax.broadcasted_iota(jnp.int32, (n, n), 0) == lax.broadcasted_iota(jnp.int32, (n, n), 1)
    return jnp.sum(jnp.where(same, row.astype(F32), 0.0), axis=1, keepdims=True)


def grad_slices_kernel(grad_ref, tags_ref, *refs):
    outs, (tags, tag_sem, sem) = refs[:-3], refs[-3:]
    chip = lax.axis_index("dp") // 2
    rows = grad_ref.shape[1]
    blocks = (outs[0].shape[0] - TAG_ROWS) // rows
    tag_copy = pltpu.make_async_copy(tags_ref, tags, tag_sem)
    copies = [
        pltpu.make_async_copy(
            grad_ref.at[0, :, lane_slice(((chip ^ k) * blocks + n) * LANES, LANES)],
            out.at[n * rows : (n + 1) * rows],
            sem.at[k, n],
        )
        for k, out in enumerate(outs)
        for n in range(blocks)
    ]
    for copy in [tag_copy] + copies:
        copy.start()
    tag_copy.wait()
    tag = jnp.broadcast_to(tags[...].astype(F32), (TAG_ROWS, LANES)).astype(BF16)
    for out in outs:
        out[blocks * rows :] = tag
    for copy in copies:
        copy.wait()


def side_slices_kernel(cuts, q_ref, kv_ref, first, second, *refs):
    v_outs, sem = refs[:-1], refs[-1]
    v_copies = [
        pltpu.make_async_copy(kv_ref.at[1, 0, :, at : at + width], out, sem.at[2 + n])
        for n, ((at, width), out) in enumerate(zip(cuts, v_outs))
    ]

    def sides(up, down):
        copies = [
            pltpu.make_async_copy(kv_ref.at[0, 0], up, sem.at[1]),
            pltpu.make_async_copy(q_ref.at[0], down, sem.at[0]),
            *v_copies,
        ]
        for copy in copies:
            copy.start()
        for copy in copies:
            copy.wait()

    even = lax.axis_index("seq") % 2 == 0

    @pl.when(even)
    def _():
        sides(first, second)

    @pl.when(jnp.logical_not(even))
    def _():
        sides(second, first)


def project_kernel(chips, first, *refs):
    grads, (own_w, other_w), (mine, *parts, lhs) = refs[:chips], refs[chips : chips + 2], refs[chips + 2 :]
    depth = own_w.shape[2]
    blocks = depth // LANES
    rows = mine.shape[0]
    core = lax.axis_index("dp") % 2
    for k, grad in enumerate(grads):
        text = column_of(grad[2 * blocks * rows : 2 * blocks * rows + 1]) == 1.0
        for side in range(2):
            for n in range(blocks):
                at = pl.ds(pl.multiple_of(((core ^ side) * blocks + n) * rows, rows), rows)
                g = grad[at]
                where = (slice(k * rows, (k + 1) * rows), slice(n * LANES, (n + 1) * LANES))
                lhs[(side, 0, *where)] = jnp.where(text, jnp.zeros_like(g), g)
                lhs[(side, 1, *where)] = jnp.where(text, g, jnp.zeros_like(g))

    total = None
    for side, w in enumerate((own_w, other_w)):
        for kind in range(2):
            rhs = w[kind, first : first + mine.shape[1]]
            term = lax.dot_general(lhs[side, kind], rhs, NT, preferred_element_type=F32)
            total = term if total is None else total + term
    mine[...] = total[:rows]
    for k, part in enumerate(parts):
        part[...] = total[(k + 1) * rows : (k + 2) * rows].astype(BF16)


def split(values):
    high = values.astype(BF16)
    return jnp.concatenate([high, (values - high.astype(F32)).astype(BF16)], axis=0)


def joined(pieces):
    half = pieces.shape[0] // 2
    return pieces[:half].astype(F32) + pieces[half:].astype(F32)


def masks(count, segs, index, rows):
    def segment(back):
        at = jnp.clip(index + back, 0, count - 1)
        return segs[:, lane_slice(at * rows, rows)].astype(F32)

    left, own, right = segment(-1), segment(0), segment(1)
    left_at, own_at = column_of(left), column_of(own)
    no_left, no_right = index == 0, index == count - 1
    key = lax.broadcasted_iota(jnp.int32, (rows, rows), 0)
    query = lax.broadcasted_iota(jnp.int32, (rows, rows), 1)
    return (
        (left_at == own) & jnp.logical_not(no_left),
        (left_at == right) & jnp.logical_not(no_left | no_right),
        (own_at == own) & (key <= query),
        (own_at == right) & jnp.logical_not(no_right),
    )


def score(keys, queries, scale, mask):
    s = lax.dot_general(keys, queries, NT, preferred_element_type=F32) * scale
    return jnp.where(mask, s, NEG)


def pair_of(even, to_even, to_odd):
    def copy(items):
        for source, target in items:
            target[...] = source[...]

    @pl.when(even)
    def _():
        copy(to_even)

    @pl.when(jnp.logical_not(even))
    def _():
        copy(to_odd)


def stats_kernel(count, scale, q_ref, kv_ref, got1, got2, segs, own_out, far_out, left_k, right_q):
    index = lax.axis_index("seq")
    rows, hc = left_k.shape
    pair_of(index % 2 == 0, [(got2, left_k), (got1, right_q)], [(got1, left_k), (got2, right_q)])
    pre, far, own, _ = masks(count, segs, index, rows)
    for h in range(hc // HEAD_DIM):
        at = slice(h * HEAD_DIM, (h + 1) * HEAD_DIM)
        kl, q = left_k[:, at], q_ref[0, :, at]
        s_pre = score(kl, q, scale, pre)
        s_own = score(kv_ref[0, 0, :, at], q, scale, own)
        s_far = score(kl, right_q[:, at], scale, far)
        top = jnp.max(jnp.maximum(s_pre, s_own), axis=0, keepdims=True)
        own_out[0, h : h + 1] = top
        own_out[1, h : h + 1] = jnp.sum(jnp.exp(s_pre - top) + jnp.exp(s_own - top), axis=0, keepdims=True)
        top = jnp.max(s_far, axis=0, keepdims=True)
        far_out[0, h : h + 1] = top
        far_out[1, h : h + 1] = jnp.sum(jnp.exp(s_far - top), axis=0, keepdims=True)


def merged(one, two):
    top = jnp.maximum(one[0], two[0])
    first = one[1] * jnp.exp(one[0] - top)
    inverse = 1.0 / (first + two[1] * jnp.exp(two[0] - top))
    return top, inverse, first * inverse


def own_rows(index, own_stats, from_left, heads):
    no_left = index == 0
    far = (jnp.where(no_left, NEG, from_left[0, heads]), jnp.where(no_left, 0.0, from_left[1, heads]))
    return merged((own_stats[0, heads], own_stats[1, heads]), far)


def right_rows(index, count, far_stats, from_right, heads):
    no_right = index == count - 1
    own = (jnp.where(no_right, 0.0, from_right[0, heads]), jnp.where(no_right, 1.0, from_right[1, heads]))
    return merged(own, (far_stats[0, heads], far_stats[1, heads]))


def delta_kernel(count, first, terms, scale, mine, *refs):
    parts = refs[:terms]
    q_ref, kv_ref, left_k, left_v, segs, own_stats, g_out, d_out = refs[terms:]
    rows, span = mine.shape
    heads = span // HEAD_DIM
    index = lax.axis_index("seq")
    pre, _, own, _ = masks(count, segs, index, rows)
    for h in range(heads):
        at = slice(h * HEAD_DIM, (h + 1) * HEAD_DIM)
        wide = slice(first + at.start, first + at.stop)
        row = slice(h, h + 1)
        stat = first // HEAD_DIM + h
        total = mine[:, at]
        for part in parts:
            total = total + part[:, at].astype(F32)
        g_out[h * rows : (h + 1) * rows] = total.astype(BF16)
        q, g = q_ref[0, :, wide], g_out[h * rows : (h + 1) * rows]
        s_pre = score(left_k[:, wide], q, scale, pre)
        s_own = score(kv_ref[0, 0, :, wide], q, scale, own)
        d_pre = lax.dot_general(left_v[:, at], g, NT, preferred_element_type=F32)
        d_own = lax.dot_general(kv_ref[1, 0, :, wide], g, NT, preferred_element_type=F32)
        top = own_stats[0, stat : stat + 1]
        weighed = jnp.exp(s_pre - top) * d_pre + jnp.exp(s_own - top) * d_own
        d_out[row] = jnp.sum(weighed, axis=0, keepdims=True) / own_stats[1, stat : stat + 1]
    g_out[heads * rows :] = split(d_out[...])


def grads_kernel(count, first, scale, q_ref, kv_ref, left_k, left_v, right_q, g_ref, right_g, segs,
                 own_stats, far_stats, from_left, from_right, delta_own,
                 dq_out, dkv_out, p_out, to1, to2, far_delta):
    index = lax.axis_index("seq")
    rows, span = left_v.shape
    heads = span // HEAD_DIM
    chosen = slice(first // HEAD_DIM, first // HEAD_DIM + heads)
    pre, far, own, nxt = masks(count, segs, index, rows)
    top, inv, share = own_rows(index, own_stats, from_left, chosen)
    r_top, r_inv, r_share = right_rows(index, count, far_stats, from_right, chosen)
    own_delta = delta_own[...] * share
    right_delta = joined(right_g[heads * rows :]) * r_share

    def run(up_out, down_out):
        for h in range(heads):
            at = slice(h * HEAD_DIM, (h + 1) * HEAD_DIM)
            wide = slice(first + at.start, first + at.stop)
            row = slice(h, h + 1)
            q2 = jnp.concatenate([q_ref[0, :, wide], right_q[:, wide]], axis=0)
            block = slice(h * rows, (h + 1) * rows)
            g2 = jnp.concatenate([g_ref[block], right_g[block]], axis=0)
            k, kl = kv_ref[0, 0, :, wide], left_k[:, wide]
            s_left = lax.dot_general(kl, q2, NT, preferred_element_type=F32) * scale
            s_here = lax.dot_general(k, q2, NT, preferred_element_type=F32) * scale
            d_left = lax.dot_general(left_v[:, at], g2, NT, preferred_element_type=F32)
            d_own = lax.dot_general(kv_ref[1, 0, :, wide], g2[:rows], NT, preferred_element_type=F32)
            p_pre = jnp.exp(jnp.where(pre, s_left[:, :rows], NEG) - top[row]) * inv[row]
            p_own = jnp.exp(jnp.where(own, s_here[:, :rows], NEG) - top[row]) * inv[row]
            p_far = jnp.exp(jnp.where(far, s_left[:, rows:], NEG) - r_top[row]) * r_inv[row]
            p_nxt = jnp.exp(jnp.where(nxt, s_here[:, rows:], NEG) - r_top[row]) * r_inv[row]
            d_pre, d_far = d_left[:, :rows], d_left[:, rows:]
            extra = jnp.sum(p_far * d_far, axis=0, keepdims=True)
            far_delta[row] = extra
            ds_pre = (p_pre * (d_pre - own_delta[row]) * scale).astype(BF16)
            ds_own = (p_own * (d_own - own_delta[row]) * scale).astype(BF16)
            ds_far = (p_far * (d_far - (right_delta[row] + extra)) * scale).astype(BF16)
            ds_nxt = (p_nxt * (extra * -scale)).astype(BF16)
            p_low = p_pre.astype(BF16)
            p_here = p_own.astype(BF16)
            p_out[h, :rows] = p_low
            p_out[h, rows:] = p_here
            dkv_out[0, :, at] = jnp.dot(
                jnp.concatenate([ds_own, ds_nxt], axis=1), q2, preferred_element_type=F32)
            dkv_out[1, :, at] = jnp.dot(p_here, g2[:rows], preferred_element_type=F32)
            down_out[0, :, at] = jnp.dot(
                jnp.concatenate([ds_pre, ds_far], axis=1), q2, preferred_element_type=F32).astype(BF16)
            down_out[1, :, at] = jnp.dot(
                jnp.concatenate([p_low, p_far.astype(BF16)], axis=1), g2, preferred_element_type=F32).astype(BF16)
            dq_out[:, at] = lax.dot_general(ds_pre, kl, TN, preferred_element_type=F32) + lax.dot_general(
                ds_own, k, TN, preferred_element_type=F32)
            up_out[0, :, at] = lax.dot_general(ds_far, kl, TN, preferred_element_type=F32).astype(BF16)
        up_out[1, : 2 * heads, :LANES] = split(far_delta[...])

    @pl.when(index % 2 == 0)
    def _():
        run(to1, to2)

    @pl.when(index % 2 == 1)
    def _():
        run(to2, to1)


def finish_kernel(count, first, scale, dq_ref, dkv_ref, p_ref, q_ref, kv_ref, left_k, got1, got2, *refs):
    grad_q, grad_kv, done, sem = refs[-4:]
    index = lax.axis_index("seq")
    rows, span = dq_ref.shape
    heads = span // HEAD_DIM

    def add(from_left, from_right):
        no_left, no_right = index == 0, index == count - 1
        delta = jnp.where(no_left, 0.0, joined(from_left[1, : 2 * heads, :LANES]))
        for h in range(heads):
            at = slice(h * HEAD_DIM, (h + 1) * HEAD_DIM)
            wide = slice(first + at.start, first + at.stop)
            factor = delta[h : h + 1] * -scale
            ds_pre = (p_ref[h, :rows].astype(F32) * factor).astype(BF16)
            ds_own = (p_ref[h, rows:].astype(F32) * factor).astype(BF16)
            dq = dq_ref[:, at] + jnp.where(no_left, 0.0, from_left[0, :, at].astype(F32))
            dq = dq + lax.dot_general(ds_pre, left_k[:, wide], TN, preferred_element_type=F32)
            dq = dq + lax.dot_general(ds_own, kv_ref[0, 0, :, wide], TN, preferred_element_type=F32)
            done[0, :, at] = dq.astype(BF16)
            dk = dkv_ref[0, :, at] + jnp.where(no_right, 0.0, from_right[0, :, at].astype(F32))
            dk = dk + jnp.dot(ds_own, q_ref[0, :, wide], preferred_element_type=F32)
            done[1, :, at] = dk.astype(BF16)
            dv = dkv_ref[1, :, at] + jnp.where(no_right, 0.0, from_right[1, :, at].astype(F32))
            done[2, :, at] = dv.astype(BF16)

    @pl.when(index % 2 == 0)
    def _():
        add(got2, got1)

    @pl.when(index % 2 == 1)
    def _():
        add(got1, got2)

    lanes = slice(first, first + span)
    copies = [
        pltpu.make_async_copy(done.at[0], grad_q.at[0, :, lanes], sem.at[0]),
        pltpu.make_async_copy(done.at[1:], grad_kv.at[:, 0, :, lanes], sem.at[1]),
    ]
    for copy in copies:
        copy.start()
    for copy in copies:
        copy.wait()


def shifted(value, steps):
    count = lax.axis_size("seq")
    return lax.ppermute(value, "seq", [(i, (i + steps) % count) for i in range(count)])


def passed(value, steps):
    count = lax.axis_size("seq")
    first, last = max(0, -steps), min(count, count - steps)
    return lax.ppermute(value, "seq", [(i, i + steps) for i in range(first, last)])


def neighbour_swaps(first, second):
    count = lax.axis_size("seq")
    one = [(i, min(i ^ 1, count - 1)) for i in range(count)]
    two = [(i, ((i + 1) ^ 1) - 1) for i in range(count)]
    two = [(i, j if 0 <= j < count else i) for i, j in two]
    return lax.ppermute(first, "seq", one), lax.ppermute(second, "seq", two)


def in_hbm(value):
    return pltpu.with_memory_space_constraint(value, pltpu.HBM)


def shape(dims, dtype=BF16):
    return jax.ShapeDtypeStruct(dims, dtype)


def cost(flops, moved):
    return pl.CostEstimate(flops=int(flops), bytes_accessed=int(moved), transcendentals=0)


def chunks(hc):
    heads = hc // HEAD_DIM
    cuts = [heads * n // PARTS for n in range(PARTS + 1)]
    return [(HEAD_DIM * a, HEAD_DIM * (b - a)) for a, b in zip(cuts, cuts[1:])]


def step(query, key_value, grad_y, tags, segments, out_weight):
    _, rows, hc = query.shape
    depth = out_weight.shape[2]
    chips = lax.axis_size("dp") // 2
    count = lax.axis_size("seq")
    scale = HEAD_DIM ** (-0.5)
    blocks = 2 * depth // LANES

    other_weight = swap(out_weight, "dp", 1)
    slices = pl.pallas_call(
        grad_slices_kernel,
        in_specs=[pl.BlockSpec(memory_space=pltpu.HBM)] * 2,
        out_shape=[shape((blocks * rows + TAG_ROWS, LANES))] * chips,
        scratch_shapes=[
            pltpu.VMEM(tags.shape, tags.dtype), pltpu.SemaphoreType.DMA, pltpu.SemaphoreType.DMA((chips, blocks))],
        compiler_params=params(4),
        name="grad_slices",
        cost_estimate=cost(0, 4 * grad_y.size),
    )(in_hbm(grad_y), in_hbm(tags))
    grads = [slices[0]] + [swap(slices[k], "dp", 2 * k) for k in range(1, chips)]
    first, second, *own_vs = pl.pallas_call(
        functools.partial(side_slices_kernel, chunks(hc)),
        in_specs=[pl.BlockSpec(memory_space=pltpu.HBM)] * 2,
        out_shape=[shape((rows, hc))] * 2 + [shape((rows, width)) for _, width in chunks(hc)],
        scratch_shapes=[pltpu.SemaphoreType.DMA((2 + PARTS,))],
        compiler_params=params(8),
        name="side_slices",
        cost_estimate=cost(0, 12 * query.size),
    )(in_hbm(query), in_hbm(key_value))
    sides = neighbour_swaps(first, second)
    values = []
    for own_v in own_vs:
        values.append(passed(own_v, 1))

    sums = []
    for first, span in chunks(hc):
        mine, *parts = pl.pallas_call(
            functools.partial(project_kernel, chips, first),
            out_shape=[shape((rows, span), F32)] + [shape((rows, span))] * (chips - 1),
            scratch_shapes=[pltpu.VMEM((2, 2, chips * rows, depth), BF16)],
            compiler_params=params(12),
            cost_estimate=cost(8 * chips * rows * depth * span, 8 * span * depth),
        )(*grads, out_weight, other_weight)
        sums.append([mine] + [swap(part, "dp", 2 * k) for k, part in enumerate(parts, 1)])

    small = shape((2, HEADS, rows), F32)
    own, far, left_k, right_q = pl.pallas_call(
        functools.partial(stats_kernel, count, scale),
        out_shape=[small] * 2 + [shape((rows, hc))] * 2,
        compiler_params=params(8),
        name="stats",
        cost_estimate=cost(2 * 3 * rows * rows * hc, 20 * rows * hc),
    )(query, key_value, *sides, segments)
    from_right, from_left = shifted(own, -1), shifted(far, 1)

    pieces = []
    for c, (first, span) in enumerate(chunks(hc)):
        heads = span // HEAD_DIM
        gout, delta = pl.pallas_call(
            functools.partial(delta_kernel, count, first, chips - 1, scale),
            out_shape=[shape((heads * rows + 2 * heads, HEAD_DIM)), shape((heads, rows), F32)],
            compiler_params=params(8),
            cost_estimate=cost(4 * 2 * rows * rows * span, 20 * rows * span),
        )(*sums[c], query, key_value, left_k, values[c], segments, own)
        pieces.append((gout, delta, passed(gout, -1)))

    parts = []
    for c, (first, span) in enumerate(chunks(hc)):
        heads, half = span // HEAD_DIM, shape((2, rows, span))
        gout, delta, right_g = pieces[c]
        *kept, to1, to2 = pl.pallas_call(
            functools.partial(grads_kernel, count, first, scale),
            out_shape=[
                shape((rows, span), F32), shape((2, rows, span), F32), shape((heads, 2 * rows, rows)), half, half],
            scratch_shapes=[pltpu.VMEM((heads, rows), F32)],
            compiler_params=params(12),
            cost_estimate=cost(10 * 3 * rows * rows * span, 40 * rows * span),
        )(query, key_value, left_k, values[c], right_q, gout, right_g, segments, own, far, from_left, from_right, delta)
        parts.append((*kept, query, key_value, left_k, *neighbour_swaps(to1, to2)))

    results = ()
    anywhere = pl.BlockSpec(memory_space=pl.ANY)
    for c, (first, span) in enumerate(chunks(hc)):
        results = pl.pallas_call(
            functools.partial(finish_kernel, count, first, scale),
            in_specs=[pl.BlockSpec(memory_space=pltpu.VMEM)] * len(parts[c]) + [anywhere] * len(results),
            out_specs=[anywhere] * 2,
            out_shape=[shape(query.shape), shape(key_value.shape)],
            scratch_shapes=[pltpu.VMEM((3, rows, span), BF16), pltpu.SemaphoreType.DMA((2,))],
            input_output_aliases={len(parts[c]) + n: n for n in range(len(results))},
            compiler_params=params(12),
            cost_estimate=cost(0, 20 * rows * span),
        )(*parts[c], *results)
    return tuple(results)


def solution(mesh):
    return jax.shard_map(
        step,
        mesh=mesh,
        in_specs=(
            P("dp", "seq", None),
            P(None, "dp", "seq", None),
            P("dp", "seq", None),
            P("dp", "seq"),
            P("dp", None),
            P(None, None, "dp"),
        ),
        out_specs=(P("dp", "seq", None), P(None, "dp", "seq", None)),
        check_vma=False,
    )
```
